128 devices in a mesh: seq: 32 (over z, y, core), tp: 4 (over x).
Axes of the slice: x: 4, y: 4, z: 4, core: 2. Of those that a mesh axis runs over, the one named last changes fastest.
Arguments:
- tokens: bfloat16 [32768, 2048], P('seq', 'tp'), may hold values from -8 to 8
- col_order: int32 [32768], P('seq'), may hold values from 0 to 32767, as said below
- in_gain: float32 [2, 2048], replicated, may hold values from 0.5 to 1.5
- w_in: bfloat16 [2, 2048, 2, 2048], P(None, None, None, 'tp'), may hold values from -0.125 to 0.125
- w_bc: bfloat16 [2, 2048, 256], replicated, may hold values from -0.0625 to 0.0625
- w_dt: bfloat16 [2, 2048, 32], P(None, None, 'tp'), may hold values from -2 to 2
- conv_x: float32 [2, 4, 2048], P(None, None, 'tp'), may hold values from -3 to 3
- conv_bc: float32 [2, 4, 256], replicated, may hold values from -3 to 3
- dt_bias: float32 [2, 32], P(None, 'tp'), may hold values from -1 to 0.5
- a_log: float32 [2, 32], P(None, 'tp'), may hold values from -16 to -2, as said below
- d_skip: float32 [2, 32], P(None, 'tp'), may hold values from 0.5 to 2
- out_gain: float32 [2, 2048], P(None, 'tp'), may hold values from 0.5 to 1.5
- w_out: bfloat16 [2, 2048, 2048], P(None, 'tp'), may hold values from -0.125 to 0.125
Outputs:
- mixed_out: bfloat16 [32768, 2048], P('seq', 'tp')
The draws below stay inside these ranges and needn't reach their ends.
Inputs may be any that keep to these rules, and one draw needn't show every extreme that they name: `col_order`: A permutation of the 32768 positions of a frame of 64 rows and 512 columns stored row by row: the column order visits the columns one after another in a drawn order, each from top to bottom or from bottom to top as drawn. So every aligned block of 1024 positions takes exactly 32 row-order positions from each aligned block of 1024 row-order positions. Each head's decay rate exp(a_log) is either between about one in fifty and one in seventeen a step or between 0.3 / 32768 and 2 / 32768 a step.
All inputs are finite; a program needn't handle non-finite values.
Results may differ from the reference program's by a relative error of at most 0.024.
Values may be sent and summed in bfloat16 or wider, within the bound.
No kernel may reach another device: no remote copies, remote signals or barrier semaphores. Data moves between devices by JAX's collectives and lax.ppermute only.
A program may use at most 128 MiB of HBM per device.

```python
import math
import jax
import jax.numpy as jnp
from jax import lax

D = 2048
HEADS = 32
HEAD_DIM = 64
STATE = 128
CONV = 4
STRETCH = 128
WIDTH_CELLS = 512
INNER = 2048
FRAME_ROWS = 64
TOKENS = 32768
N_TP = 4


def shared_direction(key):
    raw = jax.random.normal(jax.random.fold_in(key, 31), (D,), dtype=jnp.float32)
    return raw / jnp.sqrt(jnp.sum(raw * raw))


def draw_tokens(key, part):
    direction = shared_direction(key)
    noise_key, level_key = jax.random.split(jax.random.fold_in(key, 17), 2)
    noise = jnp.clip(jax.random.normal(noise_key, (TOKENS, D), dtype=jnp.float32), -6.0, 6.0)
    levels = jax.random.uniform(level_key, (FRAME_ROWS,), minval=-3.0, maxval=3.0)
    along = jnp.repeat(levels, WIDTH_CELLS, total_repeat_length=TOKENS)
    return (noise + along[:, None] * direction[None, :]).astype(jnp.bfloat16)


def draw_w_dt(key, part):
    direction = shared_direction(key)
    base_key, amp_key = jax.random.split(jax.random.fold_in(key, 19), 2)
    base = jnp.clip(jax.random.normal(base_key, (2, D, HEADS), dtype=jnp.float32), -4.0, 4.0) / math.sqrt(D)
    amplitude = jax.random.uniform(amp_key, (2, HEADS), minval=0.5, maxval=1.5)
    return (base + direction[None, :, None] * amplitude[:, None, :]).astype(jnp.bfloat16)


def draw_a_log(key, part):
    base = jax.random.fold_in(key, 7)
    pick_key, fast_key, slow_key = jax.random.split(base, 3)
    share = 0.5
    fast = jax.random.uniform(pick_key, (2, HEADS)) < share
    fast_rate = jnp.exp(jax.random.uniform(fast_key, (2, HEADS), minval=math.log(1.0 / 50.0), maxval=math.log(1.0 / 17.0)))
    slow_rate = jnp.exp(jax.random.uniform(slow_key, (2, HEADS), minval=math.log(0.3), maxval=math.log(2.0))) / TOKENS
    return jnp.log(jnp.where(fast, fast_rate, slow_rate)).astype(jnp.float32)


def draw_col_order(key, part):
    base = jax.random.fold_in(key, 13)
    perm_key, turn_key = jax.random.split(base, 2)
    columns = jax.random.permutation(perm_key, WIDTH_CELLS).astype(jnp.int32)
    downward = jax.random.randint(turn_key, (WIDTH_CELLS,), 0, 2).astype(jnp.int32)
    position = jnp.arange(TOKENS, dtype=jnp.int32)
    visit = position // FRAME_ROWS
    along = position % FRAME_ROWS
    row_index = jnp.where(downward[visit] == 1, along, FRAME_ROWS - 1 - along)
    return (row_index * WIDTH_CELLS + columns[visit]).astype(jnp.int32)


def steps_of(own_key, shape, shards, least, high):
    factor_of, own = 1.0, jax.random.fold_in(own_key, 6)
    for dim, blocks in shards:
        draws = jnp.exp(jax.random.uniform(jax.random.fold_in(own, dim), (blocks,), jnp.float32, least / len(shards), high / len(shards)))
        factor_of = factor_of * jnp.repeat(draws, shape[dim] // blocks).reshape([-1 if axis == dim else 1 for axis in range(len(shape))])
    return factor_of


def normal_values(key, dims, scale, bound, cuts=(), kind=jnp.bfloat16):
    gain = steps_of(key, dims, cuts, -0.22, 0.18) if cuts else 1.0
    drawn = jax.random.normal(key, dims, jnp.float32) * scale * gain
    return jnp.minimum(jnp.maximum(drawn, -bound), bound).astype(kind)


def setup_inputs(seed: int = 0) -> dict:
    keys = jax.random.split(jax.random.key(seed), 14)
    return {
        "tokens": draw_tokens(jax.random.fold_in(keys[13], 71), 0),
        "col_order": draw_col_order(jax.random.fold_in(keys[13], 71), 0),
        "in_gain": jnp.clip(1.0 + 0.1 * jax.random.normal(keys[2], (2, D), jnp.float32), 0.5, 1.5),
        "w_in": normal_values(keys[3], (2, D, 2, INNER), D ** -0.5, 0.125, ((3, 4),)),
        "w_bc": normal_values(keys[4], (2, D, 2 * STATE), (4 * D) ** -0.5, 0.0625),
        "w_dt": draw_w_dt(jax.random.fold_in(keys[13], 71), 0),
        "conv_x": normal_values(keys[6], (2, CONV, INNER), 0.5, 3.0, ((2, 4),), jnp.float32),
        "conv_bc": normal_values(keys[7], (2, CONV, 2 * STATE), 0.5, 3.0, (), jnp.float32),
        "dt_bias": jnp.clip(-1.0 + 1.5 * jax.random.uniform(keys[8], (2, HEADS), jnp.float32) ** steps_of(keys[8], (2, HEADS), ((1, 4),), -0.2, 0.2), -1.0, 0.5),
        "a_log": draw_a_log(jax.random.fold_in(keys[13], 71), 0),
        "d_skip": jnp.clip(0.5 + 1.5 * jax.random.uniform(keys[10], (2, HEADS), jnp.float32) ** steps_of(keys[10], (2, HEADS), ((1, 4),), -0.2, 0.2), 0.5, 2.0),
        "out_gain": jnp.clip(1.0 + 0.1 * jax.random.normal(keys[11], (2, INNER), jnp.float32), 0.5, 1.5),
        "w_out": normal_values(keys[12], (2, INNER, D), INNER ** -0.5, 0.125, ((1, 4),)),
    }


highest = lax.Precision.HIGHEST
epsilon = 1e-05

def causal_mix(signal, taps):
    length = signal.shape[0]
    padded = jnp.concatenate([jnp.zeros((CONV - 1, signal.shape[1]), jnp.float32), signal.astype(jnp.float32)], axis=0)
    mixed = jnp.zeros((length, signal.shape[1]), jnp.float32)
    for offset in range(CONV):
        mixed = mixed + taps[offset] * padded[offset:offset + length]
    return mixed

def block_step(state, pieces):
    decay_log, b_rows, c_rows, feed = pieces
    cumul = jnp.cumsum(decay_log, axis=0)
    cumul_t = cumul.T
    lower = jnp.arange(STRETCH)[:, None] >= jnp.arange(STRETCH)[None, :]
    spread = jnp.where(lower[None], cumul_t[:, :, None] - cumul_t[:, None, :], -jnp.inf)
    weights = jnp.exp(spread)
    intersection = jnp.dot(c_rows, b_rows.T, precision=highest)
    inside = jnp.einsum('hqk,khp->qhp', intersection[None] * weights, feed, precision=highest)
    carried = jnp.einsum('qn,hpn->qhp', c_rows, state, precision=highest) * jnp.exp(cumul)[:, :, None]
    to_end = jnp.exp(cumul_t[:, -1:] - cumul_t)
    fresh = jnp.einsum('hk,kn,khp->hpn', to_end, b_rows, feed, precision=highest)
    new_state = jnp.exp(cumul[-1])[:, None, None] * state + fresh
    return (new_state, inside + carried)

def mix_layer(stream, which, in_gain, w_in, w_bc, w_dt, conv_x, conv_bc, dt_bias, a_log, d_skip, out_gain, w_out):
    widen = stream.astype(jnp.float32)
    scale = lax.rsqrt(lax.optimization_barrier(jnp.mean(widen * widen, axis=-1, keepdims=True)) + epsilon)
    normed = (widen * scale * in_gain[which]).astype(jnp.bfloat16)
    projected = jnp.dot(normed, w_in[which].reshape(D, 2 * INNER), preferred_element_type=jnp.float32)
    pre_x = projected[:, :INNER].astype(jnp.bfloat16)
    gate_z = projected[:, INNER:].astype(jnp.bfloat16)
    pre_bc = jnp.dot(normed, w_bc[which], preferred_element_type=jnp.float32).astype(jnp.bfloat16)
    dt_raw = jnp.dot(normed, w_dt[which], preferred_element_type=jnp.float32)
    conv_out = jax.nn.silu(causal_mix(pre_x, conv_x[which]))
    bc_out = jax.nn.silu(causal_mix(pre_bc, conv_bc[which]))
    step_size = jax.nn.softplus(dt_raw + dt_bias[which])
    decay_log = -step_size * jnp.exp(a_log[which])
    heads_in = conv_out.reshape(TOKENS, HEADS, HEAD_DIM)
    feed = heads_in * step_size[:, :, None]
    blocks = TOKENS // STRETCH
    pieces = (decay_log.reshape(blocks, STRETCH, HEADS), bc_out[:, :STATE].reshape(blocks, STRETCH, STATE), bc_out[:, STATE:].reshape(blocks, STRETCH, STATE), feed.reshape(blocks, STRETCH, HEADS, HEAD_DIM))
    start_state = jnp.zeros((HEADS, HEAD_DIM, STATE), jnp.float32)
    final_state, outputs = lax.scan(block_step, start_state, pieces)
    ssd = outputs.reshape(TOKENS, HEADS, HEAD_DIM) + d_skip[which][None, :, None] * heads_in
    gated = ssd * jax.nn.silu(gate_z.astype(jnp.float32).reshape(TOKENS, HEADS, HEAD_DIM))
    norm_scale = lax.rsqrt(lax.optimization_barrier(jnp.mean(gated * gated, axis=-1, keepdims=True)) + epsilon)
    mixed_heads = (gated * norm_scale * out_gain[which].reshape(HEADS, HEAD_DIM)).reshape(TOKENS, INNER).astype(jnp.bfloat16)
    group = INNER // N_TP
    total = jnp.zeros((TOKENS, D), jnp.float32)
    for member in range(N_TP):
        partial_sum = jnp.dot(mixed_heads[:, member * group:(member + 1) * group], w_out[which][member * group:(member + 1) * group], preferred_element_type=jnp.float32)
        rounded = lax.optimization_barrier(partial_sum.astype(jnp.bfloat16))
        total = total + rounded.astype(jnp.float32)
    return (widen + total).astype(jnp.bfloat16)

def reference(tokens, col_order, in_gain, w_in, w_bc, w_dt, conv_x, conv_bc, dt_bias, a_log, d_skip, out_gain, w_out):
    params = (in_gain, w_in, w_bc, w_dt, conv_x, conv_bc, dt_bias, a_log, d_skip, out_gain, w_out)
    row_result = mix_layer(tokens, 0, *params)
    column_rows = row_result[col_order.astype(jnp.int32)]
    return mix_layer(column_rows, 1, *params)
```

```python
import functools

import jax
import jax.numpy as jnp
from jax import lax
from jax.experimental import pallas as pl
from jax.experimental.pallas import tpu as pltpu
from jax.sharding import Mesh
from jax.sharding import PartitionSpec as P

HEAD_DIM = 64
STATE = 128
STRETCH = 128
HEADS = 8
LANES = 512
HALO = 16
BLOCK = 256
MSG = 144
SEQ = ("seq_0", "seq_1", "seq_2")
TP = 4
epsilon = 1e-05
f32 = jnp.float32
bf16 = jnp.bfloat16
NT = (((1,), (1,)), ((), ()))
TN = (((0,), (0,)), ((), ()))
VMEM_BYTES = 56 * 2**20


def dot(a, b, dims=None):
    dims = dims or (((1,), (0,)), ((), ()))
    return lax.dot_general(a, b, dims, preferred_element_type=f32)


def silu(x):
    return x / (1.0 + jnp.exp(-x))


def softplus(x):
    return jnp.maximum(x, 0.0) + jnp.log1p(jnp.exp(-jnp.abs(x)))


def spread_heads(values, fan):
    high = values.astype(bf16)
    low = (values - high.astype(f32)).astype(bf16)
    return dot(jnp.concatenate([high, low], axis=0), fan, TN)


def head_fan():
    row = lax.broadcasted_iota(jnp.int32, (2 * HEADS, LANES), 0)
    lane = lax.broadcasted_iota(jnp.int32, (2 * HEADS, LANES), 1)
    return (row % HEADS == lane // HEAD_DIM).astype(bf16)


def entry_kernel(first, last, rows, *refs):
    (order, own, left, right, opposite) = refs[:5]
    refs = refs[5:]
    if first:
        halos, refs = refs[:4], refs[4:]
    else:
        tail_in, state_in, total_in, refs = *refs[:3], refs[3:]
    (gain, w_any, wbc_any, wdt, taps, dt_bias, a_log), refs = refs[:7], refs[7:]
    (z_out, xc_out, b_out, c_out, cum_out, step_out, ent_out, pri_out), refs = refs[:8], refs[8:]
    if last:
        (msg_out,), refs = refs[:1], refs[1:]
    else:
        (tail_out, state_out, total_out), refs = refs[:3], refs[3:]
    wv, wbcv, nbuf, xbuf, sems = refs

    copies = []
    for p in range(4):
        source = pl.ds(pl.multiple_of(order[p] * 512, 512), 512)
        target = pl.ds(p * 512, 512)
        copies.append(pltpu.make_async_copy(w_any.at[source, :], wv.at[target, :], sems.at[0, p]))
        copies.append(
            pltpu.make_async_copy(wbc_any.at[source, :], wbcv.at[target, :], sems.at[1, p])
        )
    for c in copies:
        c.start()

    fan = head_fan()
    k_pos = lax.broadcasted_iota(jnp.int32, (STRETCH, STRETCH), 0)
    q_pos = lax.broadcasted_iota(jnp.int32, (STRETCH, STRETCH), 1)
    upto = (k_pos <= q_pos).astype(f32)
    lane = lax.broadcasted_iota(jnp.int32, (HEADS, STRETCH), 1)
    rate = jnp.exp(a_log[...])
    if first:
        state = jnp.zeros((STATE, LANES), f32)
        total = jnp.zeros((HEADS, 1), f32)
    else:
        state = state_in[...]
        total = total_in[:, 0:1]
        xbuf[0:HALO, :] = tail_in[...]
    waited = False
    for i in range(rows // BLOCK):
        span = pl.ds(i * BLOCK, BLOCK)
        pieces = [r[span, :] for r in (own, left, right, opposite)]
        widen = [x.astype(f32) for x in pieces]
        square = sum(jnp.sum(x * x, axis=1, keepdims=True) for x in widen)
        scale = lax.rsqrt(square * (1.0 / 2048) + epsilon)
        for p in range(4):
            nbuf[HALO : HALO + BLOCK, p * 512 : (p + 1) * 512] = (
                widen[p] * scale * gain[order[p]]
            ).astype(bf16)
        if first and i == 0:
            widen = [r[...].astype(f32) for r in halos]
            square = sum(jnp.sum(x * x, axis=1, keepdims=True) for x in widen)
            scale = lax.rsqrt(square * (1.0 / 2048) + epsilon)
            for p in range(4):
                nbuf[0:HALO, p * 512 : (p + 1) * 512] = (
                    widen[p] * scale * gain[order[p]]
                ).astype(bf16)
        if not waited:
            for c in copies:
                c.wait()
            waited = True
        low = 0 if first and i == 0 else HALO
        if low and i > 0:
            xbuf[0:HALO, :] = xbuf[BLOCK : BLOCK + HALO, :]
        normed = nbuf[low : HALO + BLOCK, :]
        xbuf[low : HALO + BLOCK, 0:LANES] = dot(normed, wv[:, 0:LANES]).astype(bf16).astype(f32)
        z_out[span, :] = dot(nbuf[HALO:, :], wv[:, LANES:]).astype(bf16)
        xbuf[low : HALO + BLOCK, LANES:] = dot(normed, wbcv[...]).astype(bf16).astype(f32)
        dt = sum(
            dot(wdt[order[p]], nbuf[HALO:, p * 512 : (p + 1) * 512], NT) for p in range(4)
        )
        mixed = jnp.zeros((BLOCK, LANES + 2 * STATE), f32)
        for k in range(4):
            mixed = mixed + taps[k : k + 1, :] * xbuf[pl.ds(HALO - 3 + k, BLOCK), :]
        mixed = silu(mixed)
        xc = mixed[:, 0:LANES]
        b = mixed[:, LANES : LANES + STATE].astype(bf16)
        xc_out[span, :] = xc.astype(bf16)
        b_out[span, :] = b
        c_out[span, :] = mixed[:, LANES + STATE :].astype(bf16)
        step = softplus(dt + dt_bias[...])
        decay = -step * rate
        step_out[:, i * BLOCK : (i + 1) * BLOCK] = step
        cums, marks = [], jnp.zeros((HEADS, STRETCH), f32)
        for j in range(2):
            part = decay[:, j * STRETCH : (j + 1) * STRETCH]
            cum = lax.dot_general(
                part,
                upto,
                (((1,), (0,)), ((), ())),
                preferred_element_type=f32,
                precision=lax.Precision.HIGHEST,
            )
            cum_out[:, i * BLOCK + j * STRETCH : i * BLOCK + (j + 1) * STRETCH] = cum
            end = cum[:, STRETCH - 1 : STRETCH]
            marks = jnp.where(lane == j, end, jnp.where(lane == 2 + j, total, marks))
            total = total + end
            cums.append((cum, end))
        marks = jnp.where(lane == 4, total, marks)
        marks = spread_heads(jnp.exp(marks), fan)
        for j in range(2):
            cum, end = cums[j]
            here = slice(j * STRETCH, (j + 1) * STRETCH)
            weight = spread_heads(step[:, here] * jnp.exp(end - cum), fan)
            fresh = dot(b[here, :], (xc[here, :] * weight).astype(bf16), TN)
            ent_out[2 * i + j] = state
            pri_out[2 * i + j] = marks[2 + j : 3 + j, :]
            state = state * marks[j : j + 1, :] + fresh
    if last:
        msg_out[0:STATE, :] = state.astype(bf16)
        decayed = marks[4:5, :]
        high = decayed.astype(bf16).astype(f32)
        row = lax.broadcasted_iota(jnp.int32, (MSG - STATE, LANES), 0)
        msg_out[STATE:MSG, :] = jnp.where(
            row == 0, high, jnp.where(row == 1, decayed - high, 0.0)
        ).astype(bf16)
    else:
        tail_out[...] = xbuf[BLOCK : BLOCK + HALO, :]
        state_out[...] = state
        total_out[...] = jnp.broadcast_to(total, (HEADS, STRETCH))


def vmem():
    return pl.BlockSpec(memory_space=pltpu.VMEM)


def smem():
    return pl.BlockSpec(memory_space=pltpu.SMEM)


def anywhere():
    return pl.BlockSpec(memory_space=pl.ANY)


def entry(order, pieces, halos, carry, gain, w, wbc, wdt, taps, dt_bias, a_log, last):
    rows = pieces[0].shape[0]
    first = carry is None
    shape = jax.ShapeDtypeStruct
    outs = [
        shape((rows, LANES), bf16),
        shape((rows, LANES), bf16),
        shape((rows, STATE), bf16),
        shape((rows, STATE), bf16),
        shape((HEADS, rows), f32),
        shape((HEADS, rows), f32),
        shape((rows // STRETCH, STATE, LANES), f32),
        shape((rows // STRETCH, 1, LANES), f32),
    ]
    if last:
        outs += [shape((MSG, LANES), bf16)]
    else:
        outs += [
            shape((HALO, LANES + 2 * STATE), f32),
            shape((STATE, LANES), f32),
            shape((HEADS, STRETCH), f32),
        ]
    extra = list(halos) if first else list(carry)
    operands = [order, *pieces, *extra, gain, w, wbc, wdt, taps, dt_bias, a_log]
    specs = [smem()] + [vmem()] * (4 + len(extra) + 1) + [anywhere()] * 2 + [vmem()] * 4
    return pl.pallas_call(
        functools.partial(entry_kernel, first, last, rows),
        out_shape=outs,
        in_specs=specs,
        out_specs=[vmem()] * len(outs),
        scratch_shapes=[
            pltpu.VMEM((2048, 2 * LANES), bf16),
            pltpu.VMEM((2048, 2 * STATE), bf16),
            pltpu.VMEM((HALO + BLOCK, 2048), bf16),
            pltpu.VMEM((HALO + BLOCK, LANES + 2 * STATE), f32),
            pltpu.SemaphoreType.DMA((2, 4)),
        ],
        compiler_params=pltpu.CompilerParams(vmem_limit_bytes=VMEM_BYTES),
        name="entry",
    )(*operands)


def inside_kernel(rows, xc, b, c, cum, step, skip, y_out):
    q_pos = lax.broadcasted_iota(jnp.int32, (STRETCH, STRETCH), 0)
    k_pos = lax.broadcasted_iota(jnp.int32, (STRETCH, STRETCH), 1)
    causal = k_pos <= q_pos
    low_half = k_pos < HEAD_DIM
    for j in range(rows // STRETCH):
        here = slice(j * STRETCH, (j + 1) * STRETCH)
        match = jnp.where(causal, dot(c[here, :], b[here, :], NT), 0.0)
        cum_rows = cum[:, here]
        step_rows = step[:, here]
        cum_cols = jnp.transpose(cum_rows)
        for pair in range(HEADS // 2):
            weights = []
            for h in (2 * pair, 2 * pair + 1):
                gap = jnp.minimum(cum_cols[:, h : h + 1] - cum_rows[h : h + 1, :], 0.0)
                weights.append((match * (jnp.exp(gap) * step_rows[h : h + 1, :])).astype(bf16))
            lanes = slice(pair * STRETCH, (pair + 1) * STRETCH)
            x = xc[here, lanes].astype(f32)
            stacked = jnp.concatenate(
                [jnp.where(low_half, x, 0.0), jnp.where(low_half, 0.0, x)], axis=0
            ).astype(bf16)
            y_out[here, lanes] = (
                dot(jnp.concatenate(weights, axis=1), stacked) + skip[:, lanes] * x
            )


def inside(xc, b, c, cum, step, skip):
    rows = xc.shape[0]
    return pl.pallas_call(
        functools.partial(inside_kernel, rows),
        out_shape=jax.ShapeDtypeStruct((rows, LANES), f32),
        in_specs=[vmem()] * 6,
        out_specs=vmem(),
        compiler_params=pltpu.CompilerParams(vmem_limit_bytes=VMEM_BYTES),
        name="inside",
    )(xc, b, c, cum, step, skip)


def exit_kernel(rows, order, arriving, y, z, c, cum, ent, pri, gain, w_any, *refs):
    outs, (wv, sems) = refs[:4], refs[4:]
    copies = []
    for p in range(4):
        source = pl.ds(pl.multiple_of(order[p] * 512, 512), 512)
        copies.append(pltpu.make_async_copy(w_any.at[:, source], wv.at[p], sems.at[p]))
    for k in copies:
        k.start()
    fan = head_fan()
    row = lax.broadcasted_iota(jnp.int32, (BLOCK, BLOCK), 0) // HEAD_DIM
    lane = lax.broadcasted_iota(jnp.int32, (BLOCK, BLOCK), 1) // HEAD_DIM
    same_head = (row == lane).astype(bf16)
    came = arriving[...]
    waited = False
    for i in range(rows // BLOCK):
        mixed = []
        for j in (2 * i, 2 * i + 1):
            here = slice(j * STRETCH, (j + 1) * STRETCH)
            entering = (ent[j] + pri[j] * came).astype(bf16)
            carried = dot(c[here, :], entering) * spread_heads(jnp.exp(cum[:, here]), fan)
            gated = (y[here, :] + carried) * silu(z[here, :].astype(f32))
            square = (gated * gated).astype(bf16)
            sums = jnp.concatenate(
                [dot(square[:, 0:BLOCK], same_head), dot(square[:, BLOCK:], same_head)], axis=1
            )
            scale = lax.rsqrt(sums * (1.0 / HEAD_DIM) + epsilon)
            mixed.append((gated * scale * gain[...]).astype(bf16))
        mixed = jnp.concatenate(mixed, axis=0)
        if not waited:
            for k in copies:
                k.wait()
            waited = True
        for p in range(4):
            outs[p][i * BLOCK : (i + 1) * BLOCK, :] = dot(mixed, wv[p]).astype(bf16)


def leave(order, arriving, y, z, c, cum, ent, pri, gain, w):
    rows = y.shape[0]
    return pl.pallas_call(
        functools.partial(exit_kernel, rows),
        out_shape=[jax.ShapeDtypeStruct((rows, LANES), bf16)] * 4,
        in_specs=[smem()] + [vmem()] * 8 + [anywhere()],
        out_specs=[vmem()] * 4,
        scratch_shapes=[pltpu.VMEM((4, LANES, LANES), bf16), pltpu.SemaphoreType.DMA((4,))],
        compiler_params=pltpu.CompilerParams(vmem_limit_bytes=VMEM_BYTES),
        name="leave",
    )(order, arriving, y, z, c, cum, ent, pri, gain, w)


def turned(by):
    return [(i, (i + by) % TP) for i in range(TP)]


def around(x, by):
    return lax.ppermute(x, "tp", turned(by))


def halo_from(shard, by):
    count = lax.axis_size(SEQ)
    pairs = [
        (s * TP + t, (s + 1) * TP + (t + by) % TP) for s in range(count - 1) for t in range(TP)
    ]
    return lax.ppermute(shard[-HALO:], SEQ + ("tp",), pairs)


def arriving_state(msg):
    core, y = lax.axis_index("seq_2"), lax.axis_index("seq_1")

    def opened(m):
        m = m.astype(f32)
        return m[:STATE], m[STATE : STATE + 1] + m[STATE + 1 : STATE + 2]

    def closed(state, decay):
        high = decay.astype(bf16).astype(f32)
        blank = jnp.zeros((MSG - STATE - 2, LANES), f32)
        return jnp.concatenate([state, high, decay - high, blank], axis=0).astype(bf16)

    def after(a, b):
        return b[0] + b[1] * a[0], a[1] * b[1]

    def chosen(pred, a, b):
        return jnp.where(pred, a[0], b[0]), jnp.where(pred, a[1], b[1])

    nothing = (jnp.zeros((STATE, LANES), f32), jnp.ones((1, LANES), f32))
    mine = opened(msg)
    other = opened(lax.ppermute(msg, "seq_2", [(0, 1), (1, 0)]))
    is_one = core == 1
    both = after(chosen(is_one, other, mine), chosen(is_one, mine, other))
    before_core = chosen(is_one, other, nothing)
    both_msg = closed(*both)
    ring = [both_msg] + [lax.ppermute(both_msg, "seq_1", turned(k)) for k in (1, 2, 3)]
    ring = [opened(m) for m in ring]
    row, before_y = nothing, nothing
    for at in range(4):
        here = ring[0]
        for k in range(1, 4):
            here = chosen((y - at) % 4 == k, ring[k], here)
        before_y = chosen(at < y, after(before_y, here), before_y)
        row = after(row, here)
    row_msg = closed(*row)
    before = nothing
    for k in (3, 2, 1):
        pairs = [(i, i + k) for i in range(4 - k)]
        before = after(before, opened(lax.ppermute(row_msg, "seq_0", pairs)))
    return after(after(before, before_y), before_core)[0]


def layer(shard, order, out_order, params):
    gain, w, wbc, wdt, taps, dt_bias, a_log, skip, out_gain, w_out = params
    halos = [halo_from(shard, by) for by in (0, 1, -1, 2)]
    half = shard.shape[0] // 2
    own = [shard[:half], shard[half:]]
    left = [around(own[0], 1), None]
    right = [around(own[0], -1), None]
    opposite = [around(left[0], 1), None]
    left[1], right[1] = around(own[1], 1), around(own[1], -1)
    opposite[1] = around(right[1], -1)
    carry = None
    kept = []
    for i in range(2):
        out = entry(
            order,
            (own[i], left[i], right[i], opposite[i]),
            halos,
            carry,
            gain,
            w,
            wbc,
            wdt,
            taps,
            dt_bias,
            a_log,
            i == 1,
        )
        kept.append(out[:8])
        carry = out[8:]
    arriving = arriving_state(carry[0])
    sums = []
    for i in range(2):
        z, xc, b, c, cum, step, ent, pri = kept[i]
        y = inside(xc, b, c, cum, step, skip)
        mine, plus, minus, opp = leave(out_order, arriving, y, z, c, cum, ent, pri, out_gain, w_out)
        quarter = half // 2
        from_left = around(opp[:quarter], 1)
        from_right = around(opp[quarter:], -1)
        up = jnp.concatenate(
            [(plus[:quarter].astype(f32) + from_left.astype(f32)).astype(bf16), plus[quarter:]], 0
        )
        down = jnp.concatenate(
            [minus[:quarter], (minus[quarter:].astype(f32) + from_right.astype(f32)).astype(bf16)],
            0,
        )
        up, down = around(up, 1), around(down, -1)
        sums.append(own[i].astype(f32) + mine.astype(f32) + up.astype(f32) + down.astype(f32))
    return jnp.concatenate(sums, axis=0).astype(bf16)


def permuted(x, source):
    pick = (source[:, None] == jnp.arange(x.shape[0])[None, :]).astype(bf16)
    return jnp.dot(pick, x, preferred_element_type=f32).astype(bf16)


def body(
    tokens,
    col_order,
    in_gain,
    w_in,
    w_bc,
    w_dt,
    conv_x,
    conv_bc,
    dt_bias,
    a_log,
    d_skip,
    out_gain,
    w_out,
):
    x = lax.axis_index("tp")
    order = jnp.stack([x, (x + 3) % TP, (x + 1) % TP, (x + 2) % TP]).astype(jnp.int32)
    out_order = jnp.stack([x, (x + 1) % TP, (x + 3) % TP, (x + 2) % TP]).astype(jnp.int32)

    def params(which):
        return (
            in_gain[which].reshape(TP, 1, 512),
            w_in[which].reshape(2048, 2 * LANES),
            w_bc[which],
            w_dt[which].T.reshape(HEADS, TP, 512).transpose(1, 0, 2),
            jnp.concatenate([conv_x[which], conv_bc[which]], axis=1),
            dt_bias[which].reshape(HEADS, 1),
            a_log[which].reshape(HEADS, 1),
            jnp.repeat(d_skip[which], HEAD_DIM).reshape(1, LANES),
            out_gain[which].reshape(1, LANES),
            w_out[which],
        )

    heads_of = col_order.reshape(16, 64)[:, 0]
    columns = lax.all_gather(heads_of % 512, SEQ, axis=0, tiled=True)
    upward = heads_of >= 512
    slot = jnp.arange(1024)
    give = (slot % 2) * 512 + columns[slot // 2]
    visit, along = slot // 64, slot % 64
    row = jnp.where(upward[visit], 63 - along, along)
    take = (row // 2) * 32 + visit * 2 + row % 2

    row_result = layer(tokens, order, out_order, params(0))
    payload = permuted(row_result, give).reshape(32, 32, 512)
    arrived = lax.all_to_all(payload, SEQ, 0, 0, tiled=True).reshape(1024, 512)
    own_rows = permuted(arrived, take)
    return layer(own_rows, order, out_order, params(1))


def solution(mesh):
    torus = Mesh(mesh.devices.reshape(4, 4, 2, mesh.shape["tp"]), ("seq_0", "seq_1", "seq_2", "tp"))
    return jax.shard_map(
        body,
        mesh=torus,
        in_specs=(
            P(SEQ, "tp"),
            P(SEQ),
            P(),
            P(None, None, None, "tp"),
            P(),
            P(None, None, "tp"),
            P(None, None, "tp"),
            P(),
            P(None, "tp"),
            P(None, "tp"),
            P(None, "tp"),
            P(None, "tp"),
            P(None, "tp", None),
        ),
        out_specs=P(SEQ, "tp"),
        check_vma=False,
    )
```

```python
import functools

import jax
import jax.numpy as jnp
from jax import lax
from jax.experimental import pallas as pl
from jax.experimental.pallas import tpu as pltpu
from jax.sharding import Mesh
from jax.sharding import PartitionSpec as P

HEAD_DIM = 64
STATE = 128
STRETCH = 128
HEADS = 8
LANES = 512
HALF = 256
HALO = 16
BLOCK = 256
MSG = 144
SEQ = ("seq_0", "seq_1", "seq_2")
TP = 4
epsilon = 1e-05
f32 = jnp.float32
bf16 = jnp.bfloat16
NT = (((1,), (1,)), ((), ()))
TN = (((0,), (0,)), ((), ()))
VMEM_BYTES = 18 * 2**20


def dot(a, b, dims=None):
    dims = dims or (((1,), (0,)), ((), ()))
    return lax.dot_general(a, b, dims, preferred_element_type=f32)


def silu(x):
    return x / (1.0 + jnp.exp(-x))


def softplus(x):
    return jnp.maximum(x, 0.0) + jnp.log1p(jnp.exp(-jnp.abs(x)))


def spread_heads(values, fan):
    high = values.astype(bf16)
    low = (values - high.astype(f32)).astype(bf16)
    return dot(jnp.concatenate([high, low], axis=0), fan, TN)


def packed(state, decay):
    high = decay.astype(bf16).astype(f32)
    row = lax.broadcasted_iota(jnp.int32, (MSG - STATE, decay.shape[1]), 0)
    rest = jnp.where(row == 0, high, jnp.where(row == 1, decay - high, 0.0))
    return jnp.concatenate([state, rest], axis=0)


def opened(msg):
    msg = msg[...].astype(f32)
    return msg[:STATE], msg[STATE : STATE + 1] + msg[STATE + 1 : STATE + 2]


def after(a, b):
    return b[0] + b[1] * a[0], a[1] * b[1]


def chosen(pred, a, b):
    return jnp.where(pred, a[0], b[0]), jnp.where(pred, a[1], b[1])


def nothing():
    return jnp.zeros((STATE, HALF), f32), jnp.ones((1, HALF), f32)


def head_fan():
    row = lax.broadcasted_iota(jnp.int32, (2 * HEADS, LANES), 0)
    lane = lax.broadcasted_iota(jnp.int32, (2 * HEADS, LANES), 1)
    return (row % HEADS == lane // HEAD_DIM).astype(bf16)


def entry_kernel(which, first, last, rows, *refs):
    (order, own, left, right, opposite) = refs[:5]
    refs = refs[5:]
    ahead = HALO if first else 0
    if not first:
        tail_in, state_in, total_in, refs = *refs[:3], refs[3:]
    (gain, w_any, wbc_any, wdt, taps, dt_bias, a_log), refs = refs[:7], refs[7:]
    (z_out, xc_out, b_out, c_out, cum_out, step_out, ent_out, pri_out), refs = refs[:8], refs[8:]
    if last:
        (keep_out, send_out), refs = refs[:2], refs[2:]
    else:
        (tail_out, state_out, total_out), refs = refs[:3], refs[3:]
    wv, wbcv, nbuf, xbuf, sems = refs

    copies = []
    for p in range(4):
        source = pl.ds(pl.multiple_of(order[p] * 512, 512), 512)
        target = pl.ds(p * 512, 512)
        copies.append(pltpu.make_async_copy(w_any.at[which, source, :], wv.at[target, :], sems.at[0, p]))
        copies.append(
            pltpu.make_async_copy(
                wbc_any.at[which, source, :], wbcv.at[target, :], sems.at[1, p]
            )
        )
    for c in copies:
        c.start()

    fan = head_fan()
    k_pos = lax.broadcasted_iota(jnp.int32, (STRETCH, STRETCH), 0)
    q_pos = lax.broadcasted_iota(jnp.int32, (STRETCH, STRETCH), 1)
    upto = (k_pos <= q_pos).astype(f32)
    lane = lax.broadcasted_iota(jnp.int32, (HEADS, STRETCH), 1)
    rate = jnp.exp(a_log[...])
    if first:
        state = jnp.zeros((STATE, LANES), f32)
        total = jnp.zeros((HEADS, 1), f32)
    else:
        state = state_in[...]
        total = total_in[:, 0:1]
        xbuf[0:HALO, :] = tail_in[...]
    waited = False
    for i in range(rows // BLOCK):
        span = pl.ds(i * BLOCK, BLOCK)
        above = pl.ds(ahead + i * BLOCK, BLOCK)
        pieces = [r[above, :] for r in (own, left, right, opposite)]
        widen = [x.astype(f32) for x in pieces]
        square = sum(jnp.sum(x * x, axis=1, keepdims=True) for x in widen)
        scale = lax.rsqrt(square * (1.0 / 2048) + epsilon)
        for p in range(4):
            nbuf[HALO : HALO + BLOCK, p * 512 : (p + 1) * 512] = (
                widen[p] * scale * gain[order[p]]
            ).astype(bf16)
        if first and i == 0:
            widen = [r[0:HALO, :].astype(f32) for r in (own, left, right, opposite)]
            square = sum(jnp.sum(x * x, axis=1, keepdims=True) for x in widen)
            scale = lax.rsqrt(square * (1.0 / 2048) + epsilon)
            for p in range(4):
                nbuf[0:HALO, p * 512 : (p + 1) * 512] = (
                    widen[p] * scale * gain[order[p]]
                ).astype(bf16)
        if not waited:
            for c in copies:
                c.wait()
            waited = True
        low = 0 if first and i == 0 else HALO
        if low and i > 0:
            xbuf[0:HALO, :] = xbuf[BLOCK : BLOCK + HALO, :]
        normed = nbuf[low : HALO + BLOCK, :]
        xbuf[low : HALO + BLOCK, 0:LANES] = dot(normed, wv[:, 0:LANES]).astype(bf16).astype(f32)
        z_out[span, :] = dot(nbuf[HALO:, :], wv[:, LANES:]).astype(bf16)
        xbuf[low : HALO + BLOCK, LANES:] = dot(normed, wbcv[...]).astype(bf16).astype(f32)
        dt = sum(
            dot(wdt[order[p]], nbuf[HALO:, p * 512 : (p + 1) * 512], NT) for p in range(4)
        )
        mixed = jnp.zeros((BLOCK, LANES + 2 * STATE), f32)
        for k in range(4):
            mixed = mixed + taps[k : k + 1, :] * xbuf[pl.ds(HALO - 3 + k, BLOCK), :]
        mixed = silu(mixed)
        xc = mixed[:, 0:LANES]
        b = mixed[:, LANES : LANES + STATE].astype(bf16)
        xc_out[span, :] = xc.astype(bf16)
        b_out[span, :] = b
        c_out[span, :] = mixed[:, LANES + STATE :].astype(bf16)
        step = softplus(dt + dt_bias[...])
        decay = -step * rate
        step_out[:, i * BLOCK : (i + 1) * BLOCK] = step
        cums, marks = [], jnp.zeros((HEADS, STRETCH), f32)
        for j in range(2):
            part = decay[:, j * STRETCH : (j + 1) * STRETCH]
            cum = lax.dot_general(
                part,
                upto,
                (((1,), (0,)), ((), ())),
                preferred_element_type=f32,
                precision=lax.Precision.HIGHEST,
            )
            cum_out[:, i * BLOCK + j * STRETCH : i * BLOCK + (j + 1) * STRETCH] = cum
            end = cum[:, STRETCH - 1 : STRETCH]
            marks = jnp.where(lane == j, end, jnp.where(lane == 2 + j, total, marks))
            total = total + end
            cums.append((cum, end))
        marks = jnp.where(lane == 4, total, marks)
        marks = spread_heads(jnp.exp(marks), fan)
        for j in range(2):
            cum, end = cums[j]
            here = slice(j * STRETCH, (j + 1) * STRETCH)
            weight = spread_heads(step[:, here] * jnp.exp(end - cum), fan)
            fresh = dot(b[here, :], (xc[here, :] * weight).astype(bf16), TN)
            ent_out[2 * i + j] = state
            pri_out[2 * i + j] = marks[2 + j : 3 + j, :]
            state = state * marks[j : j + 1, :] + fresh
    if last:
        whole = packed(state, marks[4:5, :])
        near, far = whole[:, 0:HALF], whole[:, HALF:]
        even = order[4] == 0
        keep_out[...] = jnp.where(even, near, far).astype(bf16)
        send_out[...] = jnp.where(even, far, near).astype(bf16)
    else:
        tail_out[...] = xbuf[BLOCK : BLOCK + HALO, :]
        state_out[...] = state
        total_out[...] = jnp.broadcast_to(total, (HEADS, STRETCH))


def vmem():
    return pl.BlockSpec(memory_space=pltpu.VMEM)


def smem():
    return pl.BlockSpec(memory_space=pltpu.SMEM)


def anywhere():
    return pl.BlockSpec(memory_space=pl.ANY)


def entry(which, order, pieces, carry, gain, w, wbc, wdt, taps, dt_bias, a_log, last):
    first = carry is None
    rows = pieces[0].shape[0] - (HALO if first else 0)
    shape = jax.ShapeDtypeStruct
    outs = [
        shape((rows, LANES), bf16),
        shape((rows, LANES), bf16),
        shape((rows, STATE), bf16),
        shape((rows, STATE), bf16),
        shape((HEADS, rows), f32),
        shape((HEADS, rows), f32),
        shape((rows // STRETCH, STATE, LANES), f32),
        shape((rows // STRETCH, 1, LANES), f32),
    ]
    if last:
        outs += [shape((MSG, HALF), bf16)] * 2
    else:
        outs += [
            shape((HALO, LANES + 2 * STATE), f32),
            shape((STATE, LANES), f32),
            shape((HEADS, STRETCH), f32),
        ]
    extra = [] if first else list(carry)
    operands = [order, *pieces, *extra, gain, w, wbc, wdt, taps, dt_bias, a_log]
    specs = [smem()] + [vmem()] * (4 + len(extra) + 1) + [anywhere()] * 2 + [vmem()] * 4
    return pl.pallas_call(
        functools.partial(entry_kernel, which, first, last, rows),
        out_shape=outs,
        in_specs=specs,
        out_specs=[vmem()] * len(outs),
        scratch_shapes=[
            pltpu.VMEM((2048, 2 * LANES), bf16),
            pltpu.VMEM((2048, 2 * STATE), bf16),
            pltpu.VMEM((HALO + BLOCK, 2048), bf16),
            pltpu.VMEM((HALO + BLOCK, LANES + 2 * STATE), f32),
            pltpu.SemaphoreType.DMA((2, 4)),
        ],
        compiler_params=pltpu.CompilerParams(vmem_limit_bytes=VMEM_BYTES),
        name="entry",
    )(*operands)


def inside_kernel(rows, xc, b, c, cum, step, skip, y_out):
    q_pos = lax.broadcasted_iota(jnp.int32, (STRETCH, STRETCH), 0)
    k_pos = lax.broadcasted_iota(jnp.int32, (STRETCH, STRETCH), 1)
    causal = k_pos <= q_pos
    low_half = k_pos < HEAD_DIM
    for j in range(rows // STRETCH):
        here = slice(j * STRETCH, (j + 1) * STRETCH)
        match = jnp.where(causal, dot(c[here, :], b[here, :], NT), 0.0)
        cum_rows = cum[:, here]
        step_rows = step[:, here]
        cum_cols = jnp.transpose(cum_rows)
        for pair in range(HEADS // 2):
            weights = []
            for h in (2 * pair, 2 * pair + 1):
                gap = jnp.minimum(cum_cols[:, h : h + 1] - cum_rows[h : h + 1, :], 0.0)
                weights.append((match * (jnp.exp(gap) * step_rows[h : h + 1, :])).astype(bf16))
            lanes = slice(pair * STRETCH, (pair + 1) * STRETCH)
            x = xc[here, lanes].astype(f32)
            stacked = jnp.concatenate(
                [jnp.where(low_half, x, 0.0), jnp.where(low_half, 0.0, x)], axis=0
            ).astype(bf16)
            y_out[here, lanes] = (
                dot(jnp.concatenate(weights, axis=1), stacked) + skip[:, lanes] * x
            )


def inside(xc, b, c, cum, step, skip):
    rows = xc.shape[0]
    return pl.pallas_call(
        functools.partial(inside_kernel, rows),
        out_shape=jax.ShapeDtypeStruct((rows, LANES), f32),
        in_specs=[vmem()] * 6,
        out_specs=vmem(),
        compiler_params=pltpu.CompilerParams(vmem_limit_bytes=VMEM_BYTES),
        name="inside",
    )(xc, b, c, cum, step, skip)


def exit_kernel(which, rows, order, mine, other, y, z, c, cum, ent, pri, gain, w_any, *refs):
    (own, plus_a, plus_b, minus_a, minus_b, opp_a, opp_b), (wv, sems) = refs[:7], refs[7:]
    outs = ((own, own), (plus_a, plus_b), (minus_a, minus_b), (opp_a, opp_b))
    copies = []
    for p in range(4):
        source = pl.ds(pl.multiple_of(order[p] * 512, 512), 512)
        copies.append(pltpu.make_async_copy(w_any.at[which, :, source], wv.at[p], sems.at[p]))
    for k in copies:
        k.start()
    fan = head_fan()
    row = lax.broadcasted_iota(jnp.int32, (BLOCK, BLOCK), 0) // HEAD_DIM
    lane = lax.broadcasted_iota(jnp.int32, (BLOCK, BLOCK), 1) // HEAD_DIM
    same_head = (row == lane).astype(bf16)
    here, there = mine[...].astype(f32), other[...].astype(f32)
    even = order[4] == 0
    came = jnp.concatenate([jnp.where(even, here, there), jnp.where(even, there, here)], axis=1)
    waited = False
    for i in range(rows // BLOCK):
        mixed = []
        for j in (2 * i, 2 * i + 1):
            here = slice(j * STRETCH, (j + 1) * STRETCH)
            entering = (ent[j] + pri[j] * came).astype(bf16)
            carried = dot(c[here, :], entering) * spread_heads(jnp.exp(cum[:, here]), fan)
            gated = (y[here, :] + carried) * silu(z[here, :].astype(f32))
            square = (gated * gated).astype(bf16)
            sums = jnp.concatenate(
                [dot(square[:, 0:BLOCK], same_head), dot(square[:, BLOCK:], same_head)], axis=1
            )
            scale = lax.rsqrt(sums * (1.0 / HEAD_DIM) + epsilon)
            mixed.append((gated * scale * gain[...]).astype(bf16))
        mixed = jnp.concatenate(mixed, axis=0)
        if not waited:
            for k in copies:
                k.wait()
            waited = True
        for p in range(4):
            out = outs[p][i]
            at = i * BLOCK if p == 0 else 0
            out[at : at + BLOCK, :] = dot(mixed, wv[p]).astype(bf16)


def leave(which, order, mine, other, y, z, c, cum, ent, pri, gain, w):
    rows = y.shape[0]
    shape = jax.ShapeDtypeStruct
    outs = [shape((rows, LANES), bf16)] + [shape((BLOCK, LANES), bf16)] * 6
    return pl.pallas_call(
        functools.partial(exit_kernel, which, rows),
        out_shape=outs,
        in_specs=[smem()] + [vmem()] * 9 + [anywhere()],
        out_specs=[vmem()] * len(outs),
        scratch_shapes=[pltpu.VMEM((4, LANES, LANES), bf16), pltpu.SemaphoreType.DMA((4,))],
        compiler_params=pltpu.CompilerParams(vmem_limit_bytes=VMEM_BYTES),
        name="leave",
    )(order, mine, other, y, z, c, cum, ent, pri, gain, w)


def small_call(kernel, name, outs, place, *operands):
    return pl.pallas_call(
        kernel,
        out_shape=outs,
        in_specs=[smem()] + [vmem()] * len(operands),
        out_specs=[vmem()] * len(outs),
        compiler_params=pltpu.CompilerParams(vmem_limit_bytes=VMEM_BYTES // 2),
        name=name,
    )(place, *operands)


def chip_kernel(place, keep, got, out):
    even = place[0] == 0
    mine, other = opened(keep), opened(got)
    out[...] = packed(*after(chosen(even, mine, other), chosen(even, other, mine))).astype(bf16)


def row_kernel(place, chip, one, two, three, row_out, before_out):
    y = place[1]
    ring = [opened(r) for r in (chip, one, two, three)]
    row, before = nothing(), nothing()
    for at in range(4):
        here = ring[0]
        for k in range(1, 4):
            here = chosen((y + 4 - at) % 4 == k, ring[k], here)
        before = chosen(at < y, after(before, here), before)
        row = after(row, here)
    row_out[...] = packed(*row).astype(bf16)
    before_out[...] = packed(*before)


def arrive_kernel(place, one, two, three, before, keep, got, mine_out, other_out):
    even = place[0] == 0
    came = nothing()
    for r in (three, two, one):
        came = after(came, opened(r))
    first = after(came, opened(before))
    second = after(first, chosen(even, opened(keep), opened(got)))
    mine_out[...] = jnp.where(even, first[0], second[0]).astype(bf16)
    other_out[...] = jnp.where(even, second[0], first[0]).astype(bf16)


def turned(by):
    return [(i, (i + by) % TP) for i in range(TP)]


def around(x, by):
    return lax.ppermute(x, "tp", turned(by))


def swapped(x):
    return lax.ppermute(x, "seq_2", [(0, 1), (1, 0)])


def arriving_state(place, keep, send):
    shape = jax.ShapeDtypeStruct
    got = swapped(send)
    msg = shape((MSG, HALF), bf16)
    (chip,) = small_call(chip_kernel, "chip", [msg], place, keep, got)
    ring = [lax.ppermute(chip, "seq_1", turned(k)) for k in (1, 2, 3)]
    row, before = small_call(
        row_kernel, "row", [msg, shape((MSG, HALF), f32)], place, chip, *ring
    )
    earlier = [
        lax.ppermute(row, "seq_0", [(i, i + k) for i in range(4 - k)]) for k in (1, 2, 3)
    ]
    mine, other = small_call(
        arrive_kernel,
        "arrive",
        [shape((STATE, HALF), bf16)] * 2,
        place,
        *earlier,
        before,
        keep,
        got,
    )
    return mine, swapped(other)


def behind(x, *done):
    return lax.optimization_barrier((x, *done))[0]


def layer(which, shard, order, out_order, place, params):
    gain, w, wbc, wdt, taps, dt_bias, a_log, skip, out_gain, w_out = params
    count = lax.axis_size(SEQ)
    halo = lax.ppermute(shard[-HALO:], SEQ, [(i, i + 1) for i in range(count - 1)])
    half = shard.shape[0] // 2
    halves = [shard[:half], shard[half:]]
    own = [jnp.concatenate([halo, halves[0]], axis=0), None]
    left, right = [around(own[0], 1), None], [around(own[0], -1), None]
    own[1] = behind(halves[1], left[0], right[0])
    opposite = [around(left[0], 1), None]
    right[1] = around(own[1], -1)
    left[1] = around(own[1], 1)
    opposite[1] = around(right[1], -1)
    carry = None
    kept = []
    for i in range(2):
        out = entry(
            which,
            order,
            (own[i], left[i], right[i], opposite[i]),
            carry,
            gain,
            w,
            wbc,
            wdt,
            taps,
            dt_bias,
            a_log,
            i == 1,
        )
        kept.append(out[:8])
        carry = out[8:]
    mine, other = arriving_state(place, *carry)
    results = []
    for i in range(2):
        z, xc, b, c, cum, step, ent, pri = kept[i]
        y = inside(xc, b, c, cum, step, skip)
        own_part, plus_a, plus_b, minus_a, minus_b, opp_a, opp_b = leave(
            which, out_order, mine, other, y, z, c, cum, ent, pri, out_gain, w_out
        )
        across_a, across_b = around(opp_a, 1), around(opp_b, -1)
        down_a, up_b = around(minus_a, -1), around(plus_b, 1)
        up_a = around((plus_a.astype(f32) + across_a.astype(f32)).astype(bf16), 1)
        down_b = around((minus_b.astype(f32) + across_b.astype(f32)).astype(bf16), -1)
        quarter = half // 2
        parts = []
        for rows, up, down in ((slice(0, quarter), up_a, down_a), (slice(quarter, half), up_b, down_b)):
            parts.append(
                halves[i][rows].astype(f32)
                + own_part[rows].astype(f32)
                + up.astype(f32)
                + down.astype(f32)
            )
        results.append(jnp.concatenate(parts, axis=0).astype(bf16))
    return results


def permuted(x, source):
    pick = (source[:, None] == jnp.arange(x.shape[0])[None, :]).astype(bf16)
    return jnp.dot(pick, x, preferred_element_type=f32).astype(bf16)


def body(
    tokens,
    col_order,
    in_gain,
    w_in,
    w_bc,
    w_dt,
    conv_x,
    conv_bc,
    dt_bias,
    a_log,
    d_skip,
    out_gain,
    w_out,
):
    x = lax.axis_index("tp")
    core, y = lax.axis_index("seq_2"), lax.axis_index("seq_1")
    order = jnp.stack([x, (x + 3) % TP, (x + 1) % TP, (x + 2) % TP, core]).astype(jnp.int32)
    out_order = jnp.stack([x, (x + 1) % TP, (x + 3) % TP, (x + 2) % TP, core]).astype(jnp.int32)
    place = jnp.stack([core, y]).astype(jnp.int32)
    w = w_in.reshape(2, 2048, 2 * LANES)

    def params(which):
        return (
            in_gain[which].reshape(TP, 1, 512),
            w,
            w_bc,
            w_dt[which].T.reshape(HEADS, TP, 512).transpose(1, 0, 2),
            jnp.concatenate([conv_x[which], conv_bc[which]], axis=1),
            dt_bias[which].reshape(HEADS, 1),
            a_log[which].reshape(HEADS, 1),
            jnp.repeat(d_skip[which], HEAD_DIM).reshape(1, LANES),
            out_gain[which].reshape(1, LANES),
            w_out,
        )

    starts = col_order.reshape(16, 64)[:, 0]
    columns = lax.all_to_all(
        jnp.broadcast_to((starts % 512)[None], (32, 16)), SEQ, 0, 0, tiled=True
    ).reshape(512)
    visit = jnp.arange(16)[:, None]
    along = jnp.arange(64)[None, :]
    row = jnp.where((starts >= 512)[:, None], 63 - along, along)
    take = ((row % 2) * 512 + (row // 2) * 16 + visit).reshape(1024)
    order, columns, take = lax.optimization_barrier((order, columns, take))

    arrived = []
    for half in layer(0, tokens, order, out_order, place, params(0)):
        payload = permuted(half, columns).reshape(32, 16, 512)
        arrived.append(lax.all_to_all(payload, SEQ, 0, 0, tiled=True).reshape(512, 512))
    own_rows = permuted(jnp.concatenate(arrived, axis=0), take)
    return jnp.concatenate(layer(1, own_rows, order, out_order, place, params(1)), axis=0)


def solution(mesh):
    torus = Mesh(mesh.devices.reshape(4, 4, 2, mesh.shape["tp"]), ("seq_0", "seq_1", "seq_2", "tp"))
    return jax.shard_map(
        body,
        mesh=torus,
        in_specs=(
            P(SEQ, "tp"),
            P(SEQ),
            P(),
            P(None, None, None, "tp"),
            P(),
            P(None, None, "tp"),
            P(None, None, "tp"),
            P(),
            P(None, "tp"),
            P(None, "tp"),
            P(None, "tp"),
            P(None, "tp"),
            P(None, "tp", None),
        ),
        out_specs=P(SEQ, "tp"),
        check_vma=False,
    )
```

```python
import functools

import jax
import jax.numpy as jnp
from jax import lax
from jax.experimental import pallas as pl
from jax.experimental.pallas import tpu as pltpu
from jax.sharding import Mesh
from jax.sharding import PartitionSpec as P

HEAD_DIM = 64
STATE = 128
STRETCH = 128
HEADS = 8
LANES = 512
HALF = 256
HALO = 16
BLOCK = 256
MSG = 144
SEQ = ("seq_0", "seq_1", "seq_2")
TP = 4
epsilon = 1e-05
f32 = jnp.float32
bf16 = jnp.bfloat16
NT = (((1,), (1,)), ((), ()))
TN = (((0,), (0,)), ((), ()))
MIB = 2**20


def dot(a, b, dims=None):
    dims = dims or (((1,), (0,)), ((), ()))
    return lax.dot_general(a, b, dims, preferred_element_type=f32)


def silu(x):
    return x / (1.0 + jnp.exp(-x))


def softplus(x):
    return jnp.maximum(x, 0.0) + jnp.log1p(jnp.exp(-jnp.abs(x)))


def spread_heads(values, fan):
    high = values.astype(bf16)
    low = (values - high.astype(f32)).astype(bf16)
    return dot(jnp.concatenate([high, low], axis=0), fan, TN)


def packed(state, decay):
    high = decay.astype(bf16).astype(f32)
    row = lax.broadcasted_iota(jnp.int32, (MSG - STATE, decay.shape[1]), 0)
    rest = jnp.where(row == 0, high, jnp.where(row == 1, decay - high, 0.0))
    return jnp.concatenate([state, rest], axis=0)


def opened(msg):
    msg = msg[...].astype(f32)
    return msg[:STATE], msg[STATE : STATE + 1] + msg[STATE + 1 : STATE + 2]


def after(a, b):
    return b[0] + b[1] * a[0], a[1] * b[1]


def chosen(pred, a, b):
    return jnp.where(pred, a[0], b[0]), jnp.where(pred, a[1], b[1])


def nothing():
    return jnp.zeros((STATE, HALF), f32), jnp.ones((1, HALF), f32)


def head_fan():
    row = lax.broadcasted_iota(jnp.int32, (2 * HEADS, LANES), 0)
    lane = lax.broadcasted_iota(jnp.int32, (2 * HEADS, LANES), 1)
    return (row % HEADS == lane // HEAD_DIM).astype(bf16)


def entry_kernel(which, first, last, rows, *refs):
    (order, own, left, right, opposite) = refs[:5]
    refs = refs[5:]
    ahead = HALO if first else 0
    if not first:
        tail_in, state_in, total_in, refs = *refs[:3], refs[3:]
    (gain, w_any, wbc_any, wdt, taps, dt_bias, a_log), refs = refs[:7], refs[7:]
    (z_out, xc_out, b_out, c_out, cum_out, step_out, ent_out, pri_out), refs = refs[:8], refs[8:]
    if last:
        (keep_out, send_out), refs = refs[:2], refs[2:]
    else:
        (tail_out, state_out, total_out), refs = refs[:3], refs[3:]
    wv, wbcv, nbuf, xbuf, sems = refs

    copies = []
    for p in range(4):
        source = pl.ds(pl.multiple_of(order[p] * 512, 512), 512)
        target = pl.ds(p * 512, 512)
        copies.append(pltpu.make_async_copy(w_any.at[which, source, :], wv.at[target, :], sems.at[0, p]))
        copies.append(
            pltpu.make_async_copy(
                wbc_any.at[which, source, :], wbcv.at[target, :], sems.at[1, p]
            )
        )
    for c in copies:
        c.start()

    fan = head_fan()
    k_pos = lax.broadcasted_iota(jnp.int32, (STRETCH, STRETCH), 0)
    q_pos = lax.broadcasted_iota(jnp.int32, (STRETCH, STRETCH), 1)
    upto = (k_pos <= q_pos).astype(f32)
    lane = lax.broadcasted_iota(jnp.int32, (HEADS, STRETCH), 1)
    rate = jnp.exp(a_log[...])
    if first:
        state = jnp.zeros((STATE, LANES), f32)
        total = jnp.zeros((HEADS, 1), f32)
    else:
        state = state_in[...]
        total = total_in[:, 0:1]
        xbuf[0:HALO, :] = tail_in[...]
    waited = False
    for i in range(rows // BLOCK):
        span = pl.ds(i * BLOCK, BLOCK)
        above = pl.ds(ahead + i * BLOCK, BLOCK)
        pieces = [r[above, :] for r in (own, left, right, opposite)]
        widen = [x.astype(f32) for x in pieces]
        square = sum(jnp.sum(x * x, axis=1, keepdims=True) for x in widen)
        scale = lax.rsqrt(square * (1.0 / 2048) + epsilon)
        for p in range(4):
            nbuf[HALO : HALO + BLOCK, p * 512 : (p + 1) * 512] = (
                widen[p] * scale * gain[order[p]]
            ).astype(bf16)
        if first and i == 0:
            widen = [r[0:HALO, :].astype(f32) for r in (own, left, right, opposite)]
            square = sum(jnp.sum(x * x, axis=1, keepdims=True) for x in widen)
            scale = lax.rsqrt(square * (1.0 / 2048) + epsilon)
            for p in range(4):
                nbuf[0:HALO, p * 512 : (p + 1) * 512] = (
                    widen[p] * scale * gain[order[p]]
                ).astype(bf16)
        if not waited:
            for c in copies:
                c.wait()
            waited = True
        low = 0 if first and i == 0 else HALO
        if low and i > 0:
            xbuf[0:HALO, :] = xbuf[BLOCK : BLOCK + HALO, :]
        normed = nbuf[low : HALO + BLOCK, :]
        xbuf[low : HALO + BLOCK, 0:LANES] = dot(normed, wv[:, 0:LANES]).astype(bf16).astype(f32)
        z_out[span, :] = dot(nbuf[HALO:, :], wv[:, LANES:]).astype(bf16)
        xbuf[low : HALO + BLOCK, LANES:] = dot(normed, wbcv[...]).astype(bf16).astype(f32)
        dt = sum(
            dot(wdt[order[p]], nbuf[HALO:, p * 512 : (p + 1) * 512], NT) for p in range(4)
        )
        mixed = jnp.zeros((BLOCK, LANES + 2 * STATE), f32)
        for k in range(4):
            mixed = mixed + taps[k : k + 1, :] * xbuf[pl.ds(HALO - 3 + k, BLOCK), :]
        mixed = silu(mixed)
        xc = mixed[:, 0:LANES]
        b = mixed[:, LANES : LANES + STATE].astype(bf16)
        xc_out[span, :] = xc.astype(bf16)
        b_out[span, :] = b
        c_out[span, :] = mixed[:, LANES + STATE :].astype(bf16)
        step = softplus(dt + dt_bias[...])
        decay = -step * rate
        step_out[:, i * BLOCK : (i + 1) * BLOCK] = step
        cums, marks = [], jnp.zeros((HEADS, STRETCH), f32)
        for j in range(2):
            part = decay[:, j * STRETCH : (j + 1) * STRETCH]
            cum = lax.dot_general(
                part,
                upto,
                (((1,), (0,)), ((), ())),
                preferred_element_type=f32,
                precision=lax.Precision.HIGHEST,
            )
            cum_out[:, i * BLOCK + j * STRETCH : i * BLOCK + (j + 1) * STRETCH] = cum
            end = cum[:, STRETCH - 1 : STRETCH]
            marks = jnp.where(lane == j, end, jnp.where(lane == 2 + j, total, marks))
            total = total + end
            cums.append((cum, end))
        marks = jnp.where(lane == 4, total, marks)
        marks = spread_heads(jnp.exp(marks), fan)
        for j in range(2):
            cum, end = cums[j]
            here = slice(j * STRETCH, (j + 1) * STRETCH)
            weight = spread_heads(step[:, here] * jnp.exp(end - cum), fan)
            fresh = dot(b[here, :], (xc[here, :] * weight).astype(bf16), TN)
            ent_out[2 * i + j] = state
            pri_out[2 * i + j] = marks[2 + j : 3 + j, :]
            state = state * marks[j : j + 1, :] + fresh
    if last:
        whole = packed(state, marks[4:5, :])
        near, far = whole[:, 0:HALF], whole[:, HALF:]
        even = order[4] == 0
        keep_out[...] = jnp.where(even, near, far).astype(bf16)
        send_out[...] = jnp.where(even, far, near).astype(bf16)
    else:
        tail_out[...] = xbuf[BLOCK : BLOCK + HALO, :]
        state_out[...] = state
        total_out[...] = jnp.broadcast_to(total, (HEADS, STRETCH))


def vmem():
    return pl.BlockSpec(memory_space=pltpu.VMEM)


def smem():
    return pl.BlockSpec(memory_space=pltpu.SMEM)


def in_hbm():
    return pl.BlockSpec(memory_space=pltpu.HBM)


def kept_in_hbm(x):
    return pltpu.with_memory_space_constraint(x, pltpu.HBM)


def entry(which, order, pieces, carry, gain, w, wbc, wdt, taps, dt_bias, a_log, last):
    first = carry is None
    rows = pieces[0].shape[0] - (HALO if first else 0)
    shape = jax.ShapeDtypeStruct
    outs = [
        pltpu.VMEM((rows, LANES), bf16),
        pltpu.VMEM((rows, LANES), bf16),
        pltpu.VMEM((rows, STATE), bf16),
        pltpu.VMEM((rows, STATE), bf16),
        pltpu.VMEM((HEADS, rows), f32),
        pltpu.VMEM((HEADS, rows), f32),
        pltpu.VMEM((rows // STRETCH, STATE, LANES), f32),
        pltpu.VMEM((rows // STRETCH, 1, LANES), f32),
    ]
    if last:
        outs += [shape((MSG, HALF), bf16)] * 2
    else:
        outs += [
            pltpu.VMEM((HALO, LANES + 2 * STATE), f32),
            pltpu.VMEM((STATE, LANES), f32),
            pltpu.VMEM((HEADS, STRETCH), f32),
        ]
    extra = [] if first else list(carry)
    w, wbc = kept_in_hbm(w), kept_in_hbm(wbc)
    operands = [order, *pieces, *extra, gain, w, wbc, wdt, taps, dt_bias, a_log]
    specs = [smem()] + [vmem()] * (4 + len(extra) + 1) + [in_hbm()] * 2 + [vmem()] * 4
    return pl.pallas_call(
        functools.partial(entry_kernel, which, first, last, rows),
        out_shape=outs,
        in_specs=specs,
        out_specs=[vmem()] * len(outs),
        scratch_shapes=[
            pltpu.VMEM((2048, 2 * LANES), bf16),
            pltpu.VMEM((2048, 2 * STATE), bf16),
            pltpu.VMEM((HALO + BLOCK, 2048), bf16),
            pltpu.VMEM((HALO + BLOCK, LANES + 2 * STATE), f32),
            pltpu.SemaphoreType.DMA((2, 4)),
        ],
        compiler_params=pltpu.CompilerParams(vmem_limit_bytes=12 * MIB),
        name="entry",
    )(*operands)


def inside_kernel(rows, xc, b, c, cum, step, skip, y_out):
    q_pos = lax.broadcasted_iota(jnp.int32, (STRETCH, STRETCH), 0)
    k_pos = lax.broadcasted_iota(jnp.int32, (STRETCH, STRETCH), 1)
    causal = k_pos <= q_pos
    low_half = k_pos < HEAD_DIM
    for j in range(rows // STRETCH):
        here = slice(j * STRETCH, (j + 1) * STRETCH)
        match = jnp.where(causal, dot(c[here, :], b[here, :], NT), 0.0)
        cum_rows = cum[:, here]
        step_rows = step[:, here]
        cum_cols = jnp.transpose(cum_rows)
        for pair in range(HEADS // 2):
            weights = []
            for h in (2 * pair, 2 * pair + 1):
                gap = jnp.minimum(cum_cols[:, h : h + 1] - cum_rows[h : h + 1, :], 0.0)
                weights.append((match * (jnp.exp(gap) * step_rows[h : h + 1, :])).astype(bf16))
            lanes = slice(pair * STRETCH, (pair + 1) * STRETCH)
            x = xc[here, lanes].astype(f32)
            stacked = jnp.concatenate(
                [jnp.where(low_half, x, 0.0), jnp.where(low_half, 0.0, x)], axis=0
            ).astype(bf16)
            y_out[here, lanes] = (
                dot(jnp.concatenate(weights, axis=1), stacked) + skip[:, lanes] * x
            )


def inside(xc, b, c, cum, step, skip):
    rows = xc.shape[0]
    return pl.pallas_call(
        functools.partial(inside_kernel, rows),
        out_shape=pltpu.VMEM((rows, LANES), f32),
        in_specs=[vmem()] * 6,
        out_specs=vmem(),
        compiler_params=pltpu.CompilerParams(vmem_limit_bytes=4 * MIB),
        name="inside",
    )(xc, b, c, cum, step, skip)


def exit_kernel(which, rows, order, mine, other, y, z, c, cum, ent, pri, gain, w_any, *refs):
    (own, plus_a, plus_b, minus_a, minus_b, opp_a, opp_b), (wv, sems) = refs[:7], refs[7:]
    outs = ((own, own), (plus_a, plus_b), (minus_a, minus_b), (opp_a, opp_b))
    copies = []
    for p in range(4):
        source = pl.ds(pl.multiple_of(order[(0, 2, 1, 3)[p]] * 512, 512), 512)
        copies.append(pltpu.make_async_copy(w_any.at[which, :, source], wv.at[p], sems.at[p]))
    for k in copies:
        k.start()
    fan = head_fan()
    row = lax.broadcasted_iota(jnp.int32, (BLOCK, BLOCK), 0) // HEAD_DIM
    lane = lax.broadcasted_iota(jnp.int32, (BLOCK, BLOCK), 1) // HEAD_DIM
    same_head = (row == lane).astype(bf16)
    here, there = mine[...].astype(f32), other[...].astype(f32)
    even = order[4] == 0
    came = jnp.concatenate([jnp.where(even, here, there), jnp.where(even, there, here)], axis=1)
    waited = False
    for i in range(rows // BLOCK):
        mixed = []
        for j in (2 * i, 2 * i + 1):
            here = slice(j * STRETCH, (j + 1) * STRETCH)
            entering = (ent[j] + pri[j] * came).astype(bf16)
            carried = dot(c[here, :], entering) * spread_heads(jnp.exp(cum[:, here]), fan)
            gated = (y[here, :] + carried) * silu(z[here, :].astype(f32))
            square = (gated * gated).astype(bf16)
            sums = jnp.concatenate(
                [dot(square[:, 0:BLOCK], same_head), dot(square[:, BLOCK:], same_head)], axis=1
            )
            scale = lax.rsqrt(sums * (1.0 / HEAD_DIM) + epsilon)
            mixed.append((gated * scale * gain[...]).astype(bf16))
        mixed = jnp.concatenate(mixed, axis=0)
        if not waited:
            for k in copies:
                k.wait()
            waited = True
        for p in range(4):
            out = outs[p][i]
            at = i * BLOCK if p == 0 else 0
            out[at : at + BLOCK, :] = dot(mixed, wv[p]).astype(bf16)


def leave(which, order, mine, other, y, z, c, cum, ent, pri, gain, w):
    w = kept_in_hbm(w)
    rows = y.shape[0]
    shape = jax.ShapeDtypeStruct
    outs = [shape((rows, LANES), bf16)] + [shape((BLOCK, LANES), bf16)] * 6
    return pl.pallas_call(
        functools.partial(exit_kernel, which, rows),
        out_shape=outs,
        in_specs=[smem()] + [vmem()] * 9 + [in_hbm()],
        out_specs=[vmem()] * len(outs),
        scratch_shapes=[pltpu.VMEM((4, LANES, LANES), bf16), pltpu.SemaphoreType.DMA((4,))],
        compiler_params=pltpu.CompilerParams(vmem_limit_bytes=8 * MIB),
        name="leave",
    )(order, mine, other, y, z, c, cum, ent, pri, gain, w)


def small_call(kernel, name, outs, place, *operands):
    return pl.pallas_call(
        kernel,
        out_shape=outs,
        in_specs=[smem()] + [vmem()] * len(operands),
        out_specs=[vmem()] * len(outs),
        compiler_params=pltpu.CompilerParams(vmem_limit_bytes=2 * MIB),
        name=name,
    )(place, *operands)


def chip_kernel(place, keep, got, out):
    even = place[4] == 0
    mine, other = opened(keep), opened(got)
    out[...] = packed(*after(chosen(even, mine, other), chosen(even, other, mine))).astype(bf16)


def row_kernel(place, chip, one, two, three, row_out, before_out):
    y = place[5]
    ring = [opened(r) for r in (chip, one, two, three)]
    row, before = nothing(), nothing()
    for at in range(4):
        here = ring[0]
        for k in range(1, 4):
            here = chosen((y + 4 - at) % 4 == k, ring[k], here)
        before = chosen(at < y, after(before, here), before)
        row = after(row, here)
    row_out[...] = packed(*row).astype(bf16)
    before_out[...] = packed(*before)


def arrive_kernel(place, one, two, three, before, keep, got, mine_out, other_out):
    even = place[4] == 0
    came = nothing()
    for r in (three, two, one):
        came = after(came, opened(r))
    first = after(came, opened(before))
    second = after(first, chosen(even, opened(keep), opened(got)))
    mine_out[...] = jnp.where(even, first[0], second[0]).astype(bf16)
    other_out[...] = jnp.where(even, second[0], first[0]).astype(bf16)


def turned(by):
    return [(i, (i + by) % TP) for i in range(TP)]


def around(x, by):
    return lax.ppermute(x, "tp", turned(by))


def swapped(x):
    return lax.ppermute(x, "seq_2", [(0, 1), (1, 0)])


def arriving_state(place, keep, send, beside):
    shape = jax.ShapeDtypeStruct
    got = swapped(send)
    msg = shape((MSG, HALF), bf16)
    (chip,) = small_call(chip_kernel, "chip", [msg], place, keep, got)
    ring = [lax.ppermute(chip, "seq_1", turned(k)) for k in (1, 2, 3)]
    row, before = small_call(
        row_kernel, "row", [msg, shape((MSG, HALF), f32)], place, chip, *ring
    )
    earlier = [
        lax.ppermute(row, "seq_0", [(i, i + k) for i in range(4 - k)]) for k in (1, 2, 3)
    ]
    mine, other = small_call(
        arrive_kernel,
        "arrive",
        [shape((STATE, HALF), bf16)] * 2,
        behind(place, *beside),
        *earlier,
        before,
        keep,
        got,
    )
    return mine, swapped(other)


def behind(x, *done):
    return lax.optimization_barrier((x, *done))[0]


def with_halo(shard):
    count = lax.axis_size(SEQ)
    halo = lax.ppermute(shard[-HALO:], SEQ, [(i, i + 1) for i in range(count - 1)])
    return jnp.concatenate([halo, shard[: shard.shape[0] // 2]], axis=0)


def layer(which, shard, first, place, params, large, early=(), later=None):
    gain, wdt, taps, dt_bias, a_log, skip, out_gain = params
    w, wbc, w_out = large
    half = shard.shape[0] // 2
    halves = [shard[:half], shard[half:]]
    own = [first, None]
    left, right = [around(own[0], 1), None], [around(own[0], -1), None]
    own[1] = behind(halves[1], left[0], right[0], *early)
    opposite = [around(left[0], 1), None]
    right[1] = around(own[1], -1)
    left[1] = around(own[1], 1)
    opposite[1] = around(right[1], -1)
    extras = later(left[0]) if later else None
    if later:
        place, extras = lax.optimization_barrier((place, extras))
    carry = None
    kept = []
    for i in range(2):
        out = entry(
            which,
            place,
            (own[i], left[i], right[i], opposite[i]),
            carry,
            gain,
            w,
            wbc,
            wdt,
            taps,
            dt_bias,
            a_log,
            i == 1,
        )
        kept.append(out[:8])
        carry = out[8:]
    insides = [inside(*k[1:6], skip) for k in kept]
    mine, other = arriving_state(place, *carry, insides)
    results = []
    for i in range(2):
        z, xc, b, c, cum, step, ent, pri = kept[i]
        y = insides[i]
        own_part, plus_a, plus_b, minus_a, minus_b, opp_a, opp_b = leave(
            which, place, mine, other, y, z, c, cum, ent, pri, out_gain, w_out
        )
        across_a, across_b = around(opp_a, 1), around(opp_b, -1)
        down_a, up_b = around(minus_a, -1), around(plus_b, 1)
        up_a = around((plus_a.astype(f32) + across_a.astype(f32)).astype(bf16), 1)
        down_b = around((minus_b.astype(f32) + across_b.astype(f32)).astype(bf16), -1)
        quarter = half // 2
        parts = []
        for rows, up, down in ((slice(0, quarter), up_a, down_a), (slice(quarter, half), up_b, down_b)):
            parts.append(
                halves[i][rows].astype(f32)
                + own_part[rows].astype(f32)
                + up.astype(f32)
                + down.astype(f32)
            )
        results += parts
    return jnp.concatenate(results, axis=0).astype(bf16), extras


def permuted(x, source):
    pick = (source[:, None] == jnp.arange(x.shape[0])[None, :]).astype(bf16)
    return jnp.dot(pick, x, preferred_element_type=f32).astype(bf16)


def body(
    tokens,
    col_order,
    in_gain,
    w_in,
    w_bc,
    w_dt,
    conv_x,
    conv_bc,
    dt_bias,
    a_log,
    d_skip,
    out_gain,
    w_out,
):
    first = with_halo(tokens)
    arguments = (in_gain, w_in, w_dt, conv_x, conv_bc, dt_bias, a_log, d_skip, out_gain, col_order)
    in_gain, w_in, w_dt, conv_x, conv_bc, dt_bias, a_log, d_skip, out_gain, col_order = behind(
        arguments, first
    )
    x = lax.axis_index("tp")
    core, y = lax.axis_index("seq_2"), lax.axis_index("seq_1")
    place = jnp.stack([x, (x + 3) & 3, (x + 1) & 3, (x + 2) & 3, core, y]).astype(jnp.int32)
    w = w_in.reshape(2, 2048, 2 * LANES)

    def params(which):
        return (
            in_gain[which].reshape(TP, 1, 512),
            w_dt[which].T.reshape(HEADS, TP, 512).transpose(1, 0, 2),
            jnp.concatenate([conv_x[which], conv_bc[which]], axis=1),
            dt_bias[which].reshape(HEADS, 1),
            a_log[which].reshape(HEADS, 1),
            jnp.repeat(d_skip[which], HEAD_DIM).reshape(1, LANES),
            out_gain[which].reshape(1, LANES),
        )

    place, small, w = lax.optimization_barrier((place, [params(0), params(1)], w))
    large = (w, w_bc, w_out)

    starts = col_order.reshape(16, 64)[:, 0]

    def routes(gate):
        own_columns = behind(starts % 512, gate)
        columns = lax.all_to_all(
            jnp.broadcast_to(own_columns[None], (32, 16)), SEQ, 0, 0, tiled=True
        )
        give = (columns.reshape(32, 1, 16) + 512 * jnp.arange(2)[None, :, None]).reshape(1024)
        visit = jnp.arange(16)[:, None]
        along = jnp.arange(64)[None, :]
        row = jnp.where((starts >= 512)[:, None], 63 - along, along)
        return give, ((row // 2) * 32 + (row % 2) * 16 + visit).reshape(1024)

    row_result, (give, take) = layer(0, tokens, first, place, small[0], large, (w,), routes)
    payload = permuted(row_result, give).reshape(32, 32, 512)
    arrived = lax.all_to_all(payload, SEQ, 0, 0, tiled=True).reshape(1024, 512)
    own_rows = permuted(arrived, take)
    return layer(1, own_rows, with_halo(own_rows), place, small[1], large)[0]


def solution(mesh):
    torus = Mesh(mesh.devices.reshape(4, 4, 2, mesh.shape["tp"]), ("seq_0", "seq_1", "seq_2", "tp"))
    return jax.shard_map(
        body,
        mesh=torus,
        in_specs=(
            P(SEQ, "tp"),
            P(SEQ),
            P(),
            P(None, None, None, "tp"),
            P(),
            P(None, None, "tp"),
            P(None, None, "tp"),
            P(),
            P(None, "tp"),
            P(None, "tp"),
            P(None, "tp"),
            P(None, "tp"),
            P(None, "tp", None),
        ),
        out_specs=P(SEQ, "tp"),
        check_vma=False,
    )
```

```python
import functools

import jax
import jax.numpy as jnp
from jax import lax
from jax.experimental import pallas as pl
from jax.experimental.pallas import tpu as pltpu
from jax.sharding import Mesh
from jax.sharding import PartitionSpec as P

HEAD_DIM = 64
STATE = 128
STRETCH = 128
HEADS = 8
LANES = 512
HALF = 256
HALO = 16
BLOCK = 256
MSG = 144
SEQ = ("seq_0", "seq_1", "seq_2")
TP = 4
epsilon = 1e-05
f32 = jnp.float32
bf16 = jnp.bfloat16
NT = (((1,), (1,)), ((), ()))
TN = (((0,), (0,)), ((), ()))
MIB = 2**20


def dot(a, b, dims=None):
    dims = dims or (((1,), (0,)), ((), ()))
    return lax.dot_general(a, b, dims, preferred_element_type=f32)


def silu(x):
    return x / (1.0 + jnp.exp(-x))


def softplus(x):
    return jnp.maximum(x, 0.0) + jnp.log1p(jnp.exp(-jnp.abs(x)))


def spread_heads(values, fan):
    high = values.astype(bf16)
    low = (values - high.astype(f32)).astype(bf16)
    return dot(jnp.concatenate([high, low], axis=0), fan, TN)


def packed(state, decay, columns):
    high = decay.astype(bf16).astype(f32)
    row = lax.broadcasted_iota(jnp.int32, (8, decay.shape[1]), 0)
    rest = jnp.where(row == 0, high, jnp.where(row == 1, decay - high, 0.0))
    return jnp.concatenate([state, columns, rest], axis=0)


def opened(msg):
    msg = msg[...].astype(f32)
    at = STATE + 8
    return msg[:STATE], msg[at : at + 1] + msg[at + 1 : at + 2]


def columns_in(msg):
    return msg[...].astype(f32)[STATE : STATE + 8]


def after(a, b):
    return b[0] + b[1] * a[0], a[1] * b[1]


def chosen(pred, a, b):
    return jnp.where(pred, a[0], b[0]), jnp.where(pred, a[1], b[1])


def nothing():
    return jnp.zeros((STATE, HALF), f32), jnp.ones((1, HALF), f32)


def head_fan():
    row = lax.broadcasted_iota(jnp.int32, (2 * HEADS, LANES), 0)
    lane = lax.broadcasted_iota(jnp.int32, (2 * HEADS, LANES), 1)
    return (row % HEADS == lane // HEAD_DIM).astype(bf16)


def entry_kernel(first, last, rows, *refs):
    (order, own, left, right, opposite) = refs[:5]
    refs = refs[5:]
    ahead = HALO if first else 0
    columns = ()
    if last:
        columns, refs = refs[:1], refs[1:]
    if not first:
        tail_in, state_in, total_in, refs = *refs[:3], refs[3:]
    (gain, wv, wbcv, wdt, taps, dt_bias, a_log), refs = refs[:7], refs[7:]
    (z_out, xc_out, b_out, c_out, cum_out, step_out, ent_out, pri_out), refs = refs[:8], refs[8:]
    if last:
        (keep_out, send_out), refs = refs[:2], refs[2:]
        columns = columns[0]
    else:
        (tail_out, state_out, total_out), refs = refs[:3], refs[3:]
    nbuf, xbuf = refs

    fan = head_fan()
    k_pos = lax.broadcasted_iota(jnp.int32, (STRETCH, STRETCH), 0)
    q_pos = lax.broadcasted_iota(jnp.int32, (STRETCH, STRETCH), 1)
    upto = (k_pos <= q_pos).astype(f32)
    lane = lax.broadcasted_iota(jnp.int32, (HEADS, STRETCH), 1)
    rate = jnp.exp(a_log[:, 0:1])
    if first:
        state = jnp.zeros((STATE, LANES), f32)
        total = jnp.zeros((HEADS, 1), f32)
    else:
        state = state_in[...]
        total = total_in[:, 0:1]
        xbuf[0:HALO, :] = tail_in[...]
    for i in range(rows // BLOCK):
        span = pl.ds(i * BLOCK, BLOCK)
        above = pl.ds(ahead + i * BLOCK, BLOCK)
        pieces = [r[above, :] for r in (own, left, right, opposite)]
        widen = [x.astype(f32) for x in pieces]
        square = sum(jnp.sum(x * x, axis=1, keepdims=True) for x in widen)
        scale = lax.rsqrt(square * (1.0 / 2048) + epsilon)
        for p in range(4):
            nbuf[HALO : HALO + BLOCK, p * 512 : (p + 1) * 512] = (
                widen[p] * scale * gain[order[p]]
            ).astype(bf16)
        if first and i == 0:
            widen = [r[0:HALO, :].astype(f32) for r in (own, left, right, opposite)]
            square = sum(jnp.sum(x * x, axis=1, keepdims=True) for x in widen)
            scale = lax.rsqrt(square * (1.0 / 2048) + epsilon)
            for p in range(4):
                nbuf[0:HALO, p * 512 : (p + 1) * 512] = (
                    widen[p] * scale * gain[order[p]]
                ).astype(bf16)
        low = 0 if first and i == 0 else HALO
        if low and i > 0:
            xbuf[0:HALO, :] = xbuf[BLOCK : BLOCK + HALO, :]
        normed = nbuf[low : HALO + BLOCK, :]
        xbuf[low : HALO + BLOCK, 0:LANES] = dot(normed, wv[:, 0:LANES]).astype(bf16).astype(f32)
        z_out[span, :] = dot(nbuf[HALO:, :], wv[:, LANES:]).astype(bf16)
        xbuf[low : HALO + BLOCK, LANES:] = dot(normed, wbcv[...]).astype(bf16).astype(f32)
        dt = sum(
            dot(wdt[order[p]], nbuf[HALO:, p * 512 : (p + 1) * 512], NT) for p in range(4)
        )
        mixed = jnp.zeros((BLOCK, LANES + 2 * STATE), f32)
        for k in range(4):
            mixed = mixed + taps[k : k + 1, :] * xbuf[pl.ds(HALO - 3 + k, BLOCK), :]
        mixed = silu(mixed)
        xc = mixed[:, 0:LANES]
        b = mixed[:, LANES : LANES + STATE].astype(bf16)
        xc_out[span, :] = xc.astype(bf16)
        b_out[span, :] = b
        c_out[span, :] = mixed[:, LANES + STATE :].astype(bf16)
        step = softplus(dt + dt_bias[:, 0:1])
        decay = -step * rate
        step_out[:, i * BLOCK : (i + 1) * BLOCK] = step
        cums, marks = [], jnp.zeros((HEADS, STRETCH), f32)
        for j in range(2):
            part = decay[:, j * STRETCH : (j + 1) * STRETCH]
            cum = lax.dot_general(
                part,
                upto,
                (((1,), (0,)), ((), ())),
                preferred_element_type=f32,
                precision=lax.Precision.HIGHEST,
            )
            cum_out[:, i * BLOCK + j * STRETCH : i * BLOCK + (j + 1) * STRETCH] = cum
            end = cum[:, STRETCH - 1 : STRETCH]
            marks = jnp.where(lane == j, end, jnp.where(lane == 2 + j, total, marks))
            total = total + end
            cums.append((cum, end))
        marks = jnp.where(lane == 4, total, marks)
        marks = spread_heads(jnp.exp(marks), fan)
        for j in range(2):
            cum, end = cums[j]
            here = slice(j * STRETCH, (j + 1) * STRETCH)
            weight = spread_heads(step[:, here] * jnp.exp(end - cum), fan)
            fresh = dot(b[here, :], (xc[here, :] * weight).astype(bf16), TN)
            ent_out[2 * i + j] = state
            pri_out[2 * i + j] = marks[2 + j : 3 + j, :]
            state = state * marks[j : j + 1, :] + fresh
    if last:
        decayed = marks[4:5, :]
        near = packed(state[:, 0:HALF], decayed[:, 0:HALF], columns[...])
        far = packed(state[:, HALF:], decayed[:, HALF:], columns[...])
        even = order[4] == 0
        keep_out[...] = jnp.where(even, near, far).astype(bf16)
        send_out[...] = jnp.where(even, far, near).astype(bf16)
    else:
        tail_out[...] = xbuf[BLOCK : BLOCK + HALO, :]
        state_out[...] = state
        total_out[...] = jnp.broadcast_to(total, (HEADS, STRETCH))


def stage_kernel(which, order, w, wbc, w_out, wbc_out, sems):
    copies = []
    for p in range(4):
        source = pl.ds(pl.multiple_of(order[p] * 512, 512), 512)
        target = pl.ds(p * 512, 512)
        copies.append(
            pltpu.make_async_copy(w.at[which, source, :], w_out.at[target, :], sems.at[0, p])
        )
        copies.append(
            pltpu.make_async_copy(wbc.at[which, source, :], wbc_out.at[target, :], sems.at[1, p])
        )
    for c in copies:
        c.start()
    for c in copies:
        c.wait()


def staged(which, order, w, wbc):
    return pl.pallas_call(
        functools.partial(stage_kernel, which),
        out_shape=[pltpu.VMEM((2048, 2 * LANES), bf16), pltpu.VMEM((2048, 2 * STATE), bf16)],
        in_specs=[smem(), in_hbm(), in_hbm()],
        out_specs=[vmem()] * 2,
        scratch_shapes=[pltpu.SemaphoreType.DMA((2, 4))],
        compiler_params=pltpu.CompilerParams(vmem_limit_bytes=2 * MIB),
        name="stage",
    )(order, kept_in_hbm(w), kept_in_hbm(wbc))


def stage_out_kernel(which, order, w, out, sems):
    copies = []
    for p in range(4):
        source = pl.ds(pl.multiple_of(order[(0, 2, 1, 3)[p]] * 512, 512), 512)
        copies.append(pltpu.make_async_copy(w.at[which, :, source], out.at[p], sems.at[p]))
    for c in copies:
        c.start()
    for c in copies:
        c.wait()


def staged_out(which, order, w):
    return pl.pallas_call(
        functools.partial(stage_out_kernel, which),
        out_shape=pltpu.VMEM((4, LANES, LANES), bf16),
        in_specs=[smem(), in_hbm()],
        out_specs=vmem(),
        scratch_shapes=[pltpu.SemaphoreType.DMA((4,))],
        compiler_params=pltpu.CompilerParams(vmem_limit_bytes=2 * MIB),
        name="stage_out",
    )(order, kept_in_hbm(w))


def vmem():
    return pl.BlockSpec(memory_space=pltpu.VMEM)


def smem():
    return pl.BlockSpec(memory_space=pltpu.SMEM)


def in_hbm():
    return pl.BlockSpec(memory_space=pltpu.HBM)


def kept_in_hbm(x):
    return pltpu.with_memory_space_constraint(x, pltpu.HBM)


def entry(order, pieces, columns, carry, gain, w, wbc, wdt, taps, dt_bias, a_log, last):
    first = carry is None
    rows = pieces[0].shape[0] - (HALO if first else 0)
    shape = jax.ShapeDtypeStruct
    outs = [
        pltpu.VMEM((rows, LANES), bf16),
        pltpu.VMEM((rows, LANES), bf16),
        pltpu.VMEM((rows, STATE), bf16),
        pltpu.VMEM((rows, STATE), bf16),
        pltpu.VMEM((HEADS, rows), f32),
        pltpu.VMEM((HEADS, rows), f32),
        pltpu.VMEM((rows // STRETCH, STATE, LANES), f32),
        pltpu.VMEM((rows // STRETCH, 1, LANES), f32),
    ]
    if last:
        outs += [shape((MSG, HALF), bf16)] * 2
    else:
        outs += [
            pltpu.VMEM((HALO, LANES + 2 * STATE), f32),
            pltpu.VMEM((STATE, LANES), f32),
            pltpu.VMEM((HEADS, STRETCH), f32),
        ]
    extra = [] if first else list(carry)
    operands = [order, *pieces, *([columns] if last else []), *extra, gain, w, wbc, wdt, taps, dt_bias, a_log]
    specs = [smem()] + [vmem()] * (len(operands) - 1)
    return pl.pallas_call(
        functools.partial(entry_kernel, first, last, rows),
        out_shape=outs,
        in_specs=specs,
        out_specs=[vmem()] * len(outs),
        scratch_shapes=[
            pltpu.VMEM((HALO + BLOCK, 2048), bf16),
            pltpu.VMEM((HALO + BLOCK, LANES + 2 * STATE), f32),
        ],
        compiler_params=pltpu.CompilerParams(vmem_limit_bytes=8 * MIB),
        name="entry",
    )(*operands)


def inside_kernel(rows, xc, b, c, cum, step, skip, y_out):
    q_pos = lax.broadcasted_iota(jnp.int32, (STRETCH, STRETCH), 0)
    k_pos = lax.broadcasted_iota(jnp.int32, (STRETCH, STRETCH), 1)
    causal = k_pos <= q_pos
    low_half = k_pos < HEAD_DIM
    skips = spread_heads(skip[...], head_fan())[0:1, :]
    for j in range(rows // STRETCH):
        here = slice(j * STRETCH, (j + 1) * STRETCH)
        match = jnp.where(causal, dot(c[here, :], b[here, :], NT), 0.0)
        cum_rows = cum[:, here]
        step_rows = step[:, here]
        cum_cols = jnp.transpose(cum_rows)
        for pair in range(HEADS // 2):
            weights = []
            for h in (2 * pair, 2 * pair + 1):
                gap = jnp.minimum(cum_cols[:, h : h + 1] - cum_rows[h : h + 1, :], 0.0)
                weights.append((match * (jnp.exp(gap) * step_rows[h : h + 1, :])).astype(bf16))
            lanes = slice(pair * STRETCH, (pair + 1) * STRETCH)
            x = xc[here, lanes].astype(f32)
            stacked = jnp.concatenate(
                [jnp.where(low_half, x, 0.0), jnp.where(low_half, 0.0, x)], axis=0
            ).astype(bf16)
            y_out[here, lanes] = (
                dot(jnp.concatenate(weights, axis=1), stacked) + skips[:, lanes] * x
            )


def inside(xc, b, c, cum, step, skip):
    rows = xc.shape[0]
    return pl.pallas_call(
        functools.partial(inside_kernel, rows),
        out_shape=pltpu.VMEM((rows, LANES), f32),
        in_specs=[vmem()] * 6,
        out_specs=vmem(),
        compiler_params=pltpu.CompilerParams(vmem_limit_bytes=4 * MIB),
        name="inside",
    )(xc, b, c, cum, step, skip)


def exit_kernel(chunks, order, mine, other, gain, wv, *refs):
    parts = [refs[6 * i : 6 * i + 6] for i in range(chunks)]
    own, plus_a, plus_b, minus_a, minus_b, opp_a, opp_b = refs[6 * chunks :]
    split = chunks * BLOCK // 2
    outs = ((plus_a, plus_b), (minus_a, minus_b), (opp_a, opp_b))
    fan = head_fan()
    row = lax.broadcasted_iota(jnp.int32, (BLOCK, BLOCK), 0) // HEAD_DIM
    lane = lax.broadcasted_iota(jnp.int32, (BLOCK, BLOCK), 1) // HEAD_DIM
    same_head = (row == lane).astype(bf16)
    here, there = mine[...].astype(f32), other[...].astype(f32)
    even = order[4] == 0
    came = jnp.concatenate([jnp.where(even, here, there), jnp.where(even, there, here)], axis=1)
    for i in range(chunks):
        y, z, c, cum, ent, pri = parts[i]
        mixed = []
        for j in range(2):
            here = slice(j * STRETCH, (j + 1) * STRETCH)
            entering = (ent[j] + pri[j] * came).astype(bf16)
            carried = dot(c[here, :], entering) * spread_heads(jnp.exp(cum[:, here]), fan)
            gated = (y[here, :] + carried) * silu(z[here, :].astype(f32))
            square = (gated * gated).astype(bf16)
            sums = jnp.concatenate(
                [dot(square[:, 0:BLOCK], same_head), dot(square[:, BLOCK:], same_head)], axis=1
            )
            scale = lax.rsqrt(sums * (1.0 / HEAD_DIM) + epsilon)
            mixed.append((gated * scale * gain[...]).astype(bf16))
        mixed = jnp.concatenate(mixed, axis=0)
        own[i * BLOCK : (i + 1) * BLOCK, :] = dot(mixed, wv[0]).astype(bf16)
        for p in range(3):
            product = dot(mixed, wv[p + 1]).astype(bf16)
            for j in range(2):
                at = i * BLOCK + j * STRETCH
                out = outs[p][at // split]
                at = at % split
                out[at : at + STRETCH, :] = product[j * STRETCH : (j + 1) * STRETCH, :]


def leave(order, mine, other, gain, w, parts):
    rows = len(parts) * BLOCK
    shape = jax.ShapeDtypeStruct
    outs = [shape((rows, LANES), bf16)] + [shape((rows // 2, LANES), bf16)] * 6
    operands = [order, mine, other, gain, w, *(a for part in parts for a in part)]
    return pl.pallas_call(
        functools.partial(exit_kernel, len(parts)),
        out_shape=outs,
        in_specs=[smem()] + [vmem()] * (len(operands) - 1),
        out_specs=[vmem()] * len(outs),
        compiler_params=pltpu.CompilerParams(vmem_limit_bytes=6 * MIB),
        name="leave",
    )(*operands)


def small_call(kernel, name, outs, place, *operands):
    return pl.pallas_call(
        kernel,
        out_shape=outs,
        in_specs=[smem()] + [vmem()] * len(operands),
        out_specs=[vmem()] * len(outs),
        compiler_params=pltpu.CompilerParams(vmem_limit_bytes=2 * MIB),
        name=name,
    )(place, *operands)


def chip_kernel(place, keep, got, out):
    even = place[4] == 0
    mine, other = opened(keep), opened(got)
    both = after(chosen(even, mine, other), chosen(even, other, mine))
    out[...] = packed(*both, columns_in(keep) + columns_in(got)).astype(bf16)


def row_kernel(place, chip, one, two, three, row_out, before_out):
    y = place[5]
    ring = [opened(r) for r in (chip, one, two, three)]
    row, before = nothing(), nothing()
    for at in range(4):
        here = ring[0]
        for k in range(1, 4):
            here = chosen((y + 4 - at) % 4 == k, ring[k], here)
        before = chosen(at < y, after(before, here), before)
        row = after(row, here)
    columns = sum(columns_in(r) for r in (chip, one, two, three))
    row_out[...] = packed(*row, columns).astype(bf16)
    before_out[...] = packed(*before, columns)


def arrive_kernel(place, one, two, three, before, keep, got, mine_out, other_out, columns_out):
    even = place[4] == 0
    z = place[6]
    came = nothing()
    for k, r in ((3, three), (2, two), (1, one)):
        came = chosen(z >= k, after(came, opened(r)), came)
    first = after(came, opened(before))
    second = after(first, chosen(even, opened(keep), opened(got)))
    mine_out[...] = jnp.where(even, first[0], second[0]).astype(bf16)
    other_out[...] = jnp.where(even, second[0], first[0]).astype(bf16)
    columns_out[...] = sum(columns_in(r) for r in (before, one, two, three))


def give_kernel(columns, x, out):
    cell = lax.broadcasted_iota(jnp.int32, (512, HALF), 0)
    for part in range(2):
        wanted = 2.0 * columns[2 * part : 2 * part + 1, :] + columns[2 * part + 1 : 2 * part + 2, :]
        pick = (cell == wanted.astype(jnp.int32)).astype(bf16)
        for r in range(2):
            rows = dot(pick, x[r * 512 : (r + 1) * 512, :], TN).astype(bf16)
            out[part * 16 : (part + 1) * 16, r * 16 : (r + 1) * 16, :] = rows.reshape(16, 16, 512)


def given(columns, x):
    return pl.pallas_call(
        give_kernel,
        out_shape=jax.ShapeDtypeStruct((32, 32, 512), bf16),
        in_specs=[vmem()] * 2,
        out_specs=vmem(),
        compiler_params=pltpu.CompilerParams(vmem_limit_bytes=6 * MIB),
        name="give",
    )(columns, x)


def turned(by):
    return [(i, (i + by) % TP) for i in range(TP)]


def around(x, by):
    return lax.ppermute(x, "tp", turned(by))


def swapped(x):
    return lax.ppermute(x, "seq_2", [(0, 1), (1, 0)])


def arriving_state(place, keep, send, beside, wrapped):
    shape = jax.ShapeDtypeStruct
    got = swapped(send)
    msg = shape((MSG, HALF), bf16)
    (chip,) = small_call(chip_kernel, "chip", [msg], place, keep, got)
    ring = [lax.ppermute(chip, "seq_1", turned(k)) for k in (1, 2, 3)]
    row, before = small_call(
        row_kernel, "row", [msg, shape((MSG, HALF), f32)], place, chip, *ring
    )
    earlier = [
        lax.ppermute(row, "seq_0", turned(k)[: 4 if wrapped else 4 - k]) for k in (1, 2, 3)
    ]
    mine, other, columns = small_call(
        arrive_kernel,
        "arrive",
        [shape((STATE, HALF), bf16)] * 2 + [shape((8, HALF), f32)],
        behind(place, *beside),
        *earlier,
        before,
        keep,
        got,
    )
    return mine, swapped(other), columns


def behind(x, *done):
    return lax.optimization_barrier((x, *done))[0]


def with_halo(shard):
    count = lax.axis_size(SEQ)
    halo = lax.ppermute(shard[-HALO:], SEQ, [(i, i + 1) for i in range(count - 1)])
    return jnp.concatenate([halo, shard[:BLOCK]], axis=0)


def gathered(shard, first, ahead, early):
    count = shard.shape[0] // BLOCK
    rows = [shard[i * BLOCK : (i + 1) * BLOCK] for i in range(count)]
    own, left, right, opposite = [first], [], [], []
    for i in range(count):
        up = down = first
        if i:
            gates_up = [left[i - ahead], right[i - ahead]] if i >= ahead else []
            gates_down = list(gates_up)
            if i > ahead:
                gates_up.append(opposite[i - ahead - 1])
            if i == ahead:
                gates_up += early
                gates_down += early
            own.append(rows[i])
            up = behind(rows[i], first, *gates_up)
            down = behind(rows[i], first, *gates_down)
        left.append(around(up, 1))
        right.append(around(down, -1))
        opposite.append(around(left[i], 1) if i % 2 == 0 else around(right[i], -1))
    return list(zip(own, left, right, opposite)), rows


def layer(which, shard, first, place, params, large, columns, ahead, early=()):
    gain, wdt, taps, dt_bias, a_log, skip, out_gain = params
    w, wbc, w_out = large
    blocks, rows = gathered(shard, first, ahead, list(early))
    wv, wbcv = staged(which, behind(place, first), w, wbc)
    carry = None
    kept = []
    for i, pieces in enumerate(blocks):
        last = i == len(blocks) - 1
        out = entry(place, pieces, columns, carry, gain, wv, wbcv, wdt, taps, dt_bias, a_log, last)
        z, xc, b, c, cum, step, ent, pri = out[:8]
        carry = out[8:]
        kept.append((inside(xc, b, c, cum, step, skip), z, c, cum, ent, pri))
    wov = staged_out(which, behind(place, carry[0]), w_out)
    mine, other, columns = arriving_state(place, *carry, [k[0] for k in kept], which == 0)
    results = []
    for low, high in ((0, 1), (1, 4)):
        own_part, plus_a, plus_b, minus_a, minus_b, opp_a, opp_b = leave(
            place, mine, other, out_gain, wov, kept[low:high]
        )
        across_a, across_b = around(opp_a, 1), around(opp_b, -1)
        down_a, up_b = around(minus_a, -1), around(plus_b, 1)
        up_a = around((plus_a.astype(f32) + across_a.astype(f32)).astype(bf16), 1)
        down_b = around((minus_b.astype(f32) + across_b.astype(f32)).astype(bf16), -1)
        here = jnp.concatenate(rows[low:high], axis=0).astype(f32) + own_part.astype(f32)
        half = here.shape[0] // 2
        for span, up, down in ((slice(0, half), up_a, down_a), (slice(half, 2 * half), up_b, down_b)):
            results.append(here[span] + up.astype(f32) + down.astype(f32))
    return jnp.concatenate(results, axis=0).astype(bf16), columns


def permuted(x, source):
    pick = (source[:, None] == jnp.arange(x.shape[0])[None, :]).astype(bf16)
    return jnp.dot(pick, x, preferred_element_type=f32).astype(bf16)


def body(
    tokens,
    col_order,
    in_gain,
    w_in,
    w_bc,
    w_dt,
    conv_x,
    conv_bc,
    dt_bias,
    a_log,
    d_skip,
    out_gain,
    w_out,
):
    first = with_halo(tokens)
    arguments = (in_gain, w_in, w_dt, conv_x, conv_bc, dt_bias, a_log, d_skip, out_gain, col_order)
    in_gain, w_in, w_dt, conv_x, conv_bc, dt_bias, a_log, d_skip, out_gain, col_order = behind(
        arguments, first
    )
    x = lax.axis_index("tp")
    core, y, z = (lax.axis_index(a) for a in ("seq_2", "seq_1", "seq_0"))
    place = jnp.stack([x, (x + 3) & 3, (x + 1) & 3, (x + 2) & 3, core, y, z]).astype(jnp.int32)
    w = w_in.reshape(2, 2048, 2 * LANES)

    def on_lanes(heads):
        return jnp.broadcast_to(heads[:, None], (HEADS, STRETCH))

    def params(which):
        return (
            in_gain[which].reshape(TP, 1, 512),
            w_dt[which].T.reshape(HEADS, TP, 512).transpose(1, 0, 2),
            jnp.concatenate([conv_x[which], conv_bc[which]], axis=1),
            on_lanes(dt_bias[which]),
            on_lanes(a_log[which]),
            on_lanes(d_skip[which]),
            out_gain[which].reshape(1, LANES),
        )

    starts = col_order.reshape(16, 64)[:, 0]
    slot = jnp.arange(512)
    columns = jnp.where(
        slot // 16 == lax.axis_index(SEQ), jnp.tile(starts % 512, 32), 0
    ).reshape(2, 256)
    columns = jnp.stack([columns[0] // 2, columns[0] % 2, columns[1] // 2, columns[1] % 2])
    columns = jnp.pad(columns.astype(f32), ((0, 4), (0, 0)))
    visit = jnp.arange(16)[:, None]
    along = jnp.arange(64)[None, :]
    row = jnp.where((starts >= 512)[:, None], 63 - along, along)
    take = ((row // 2) * 32 + (row % 2) * 16 + visit).reshape(1024)
    place, small, w, columns, take = lax.optimization_barrier(
        (place, [params(0), params(1)], w, columns, take)
    )
    large = (w, w_bc, w_out)

    row_result, columns = layer(0, tokens, first, place, small[0], large, columns, 3, (w,))
    payload = given(columns, row_result)
    arrived = lax.all_to_all(payload, SEQ, 0, 0, tiled=True).reshape(1024, 512)
    own_rows = permuted(arrived, take)
    return layer(1, own_rows, with_halo(own_rows), place, small[1], large, columns, 3)[0]


def solution(mesh):
    torus = Mesh(mesh.devices.reshape(4, 4, 2, mesh.shape["tp"]), ("seq_0", "seq_1", "seq_2", "tp"))
    return jax.shard_map(
        body,
        mesh=torus,
        in_specs=(
            P(SEQ, "tp"),
            P(SEQ),
            P(),
            P(None, None, None, "tp"),
            P(),
            P(None, None, "tp"),
            P(None, None, "tp"),
            P(),
            P(None, "tp"),
            P(None, "tp"),
            P(None, "tp"),
            P(None, "tp"),
            P(None, "tp", None),
        ),
        out_specs=P(SEQ, "tp"),
        check_vma=False,
    )
```

```python
import functools

import jax
import jax.numpy as jnp
from jax import lax
from jax.experimental import pallas as pl
from jax.experimental.pallas import tpu as pltpu
from jax.sharding import Mesh
from jax.sharding import PartitionSpec as P

HEAD_DIM = 64
STATE = 128
STRETCH = 128
HEADS = 8
LANES = 512
HALF = 256
HALO = 16
BLOCK = 256
MSG = 144
SEQ = ("seq_0", "seq_1", "seq_2")
TP = 4
epsilon = 1e-05
f32 = jnp.float32
bf16 = jnp.bfloat16
NT = (((1,), (1,)), ((), ()))
TN = (((0,), (0,)), ((), ()))
MIB = 2**20


def dot(a, b, dims=None):
    dims = dims or (((1,), (0,)), ((), ()))
    return lax.dot_general(a, b, dims, preferred_element_type=f32)


def silu(x):
    return x / (1.0 + jnp.exp(-x))


def softplus(x):
    return jnp.maximum(x, 0.0) + jnp.log1p(jnp.exp(-jnp.abs(x)))


def spread_heads(values, fan):
    high = values.astype(bf16)
    low = (values - high.astype(f32)).astype(bf16)
    return dot(jnp.concatenate([high, low], axis=0), fan, TN)


def packed(state, decay, columns):
    high = decay.astype(bf16).astype(f32)
    row = lax.broadcasted_iota(jnp.int32, (8, decay.shape[1]), 0)
    rest = jnp.where(row == 0, high, jnp.where(row == 1, decay - high, 0.0))
    return jnp.concatenate([state, columns, rest], axis=0)


def opened(msg):
    msg = msg[...].astype(f32)
    at = STATE + 8
    return msg[:STATE], msg[at : at + 1] + msg[at + 1 : at + 2]


def columns_in(msg):
    return msg[...].astype(f32)[STATE : STATE + 8]


def after(a, b):
    return b[0] + b[1] * a[0], a[1] * b[1]


def chosen(pred, a, b):
    return jnp.where(pred, a[0], b[0]), jnp.where(pred, a[1], b[1])


def nothing():
    return jnp.zeros((STATE, HALF), f32), jnp.ones((1, HALF), f32)


def head_fan():
    row = lax.broadcasted_iota(jnp.int32, (2 * HEADS, LANES), 0)
    lane = lax.broadcasted_iota(jnp.int32, (2 * HEADS, LANES), 1)
    return (row % HEADS == lane // HEAD_DIM).astype(bf16)


def entry_kernel(first, last, rows, *refs):
    (order, own, left, right, opposite) = refs[:5]
    refs = refs[5:]
    ahead = HALO if first else 0
    columns = ()
    if last:
        columns, refs = refs[:1], refs[1:]
    if not first:
        tail_in, state_in, total_in, refs = *refs[:3], refs[3:]
    (gain, wv, wbcv, wdt, taps, dt_bias, a_log), refs = refs[:7], refs[7:]
    (z_out, xc_out, b_out, c_out, cum_out, step_out, ent_out, pri_out), refs = refs[:8], refs[8:]
    if last:
        (keep_out, send_out), refs = refs[:2], refs[2:]
        columns = columns[0]
    else:
        (tail_out, state_out, total_out), refs = refs[:3], refs[3:]
    nbuf, xbuf = refs

    fan = head_fan()
    k_pos = lax.broadcasted_iota(jnp.int32, (STRETCH, STRETCH), 0)
    q_pos = lax.broadcasted_iota(jnp.int32, (STRETCH, STRETCH), 1)
    upto = (k_pos <= q_pos).astype(f32)
    lane = lax.broadcasted_iota(jnp.int32, (HEADS, STRETCH), 1)
    rate = jnp.exp(a_log[:, 0:1])
    if first:
        state = jnp.zeros((STATE, LANES), f32)
        total = jnp.zeros((HEADS, 1), f32)
    else:
        state = state_in[...]
        total = total_in[:, 0:1]
        xbuf[0:HALO, :] = tail_in[...]
    for i in range(rows // BLOCK):
        span = pl.ds(i * BLOCK, BLOCK)
        above = pl.ds(ahead + i * BLOCK, BLOCK)
        pieces = [r[above, :] for r in (own, left, right, opposite)]
        widen = [x.astype(f32) for x in pieces]
        square = sum(jnp.sum(x * x, axis=1, keepdims=True) for x in widen)
        scale = lax.rsqrt(square * (1.0 / 2048) + epsilon)
        for p in range(4):
            nbuf[HALO : HALO + BLOCK, p * 512 : (p + 1) * 512] = (
                widen[p] * scale * gain[order[p]]
            ).astype(bf16)
        if first and i == 0:
            widen = [r[0:HALO, :].astype(f32) for r in (own, left, right, opposite)]
            square = sum(jnp.sum(x * x, axis=1, keepdims=True) for x in widen)
            scale = lax.rsqrt(square * (1.0 / 2048) + epsilon)
            for p in range(4):
                nbuf[0:HALO, p * 512 : (p + 1) * 512] = (
                    widen[p] * scale * gain[order[p]]
                ).astype(bf16)
        low = 0 if first and i == 0 else HALO
        if low and i > 0:
            xbuf[0:HALO, :] = xbuf[BLOCK : BLOCK + HALO, :]
        normed = nbuf[low : HALO + BLOCK, :]
        xbuf[low : HALO + BLOCK, 0:LANES] = dot(normed, wv[:, 0:LANES]).astype(bf16).astype(f32)
        z_out[span, :] = dot(nbuf[HALO:, :], wv[:, LANES:]).astype(bf16)
        xbuf[low : HALO + BLOCK, LANES:] = dot(normed, wbcv[...]).astype(bf16).astype(f32)
        dt = sum(
            dot(wdt[order[p]], nbuf[HALO:, p * 512 : (p + 1) * 512], NT) for p in range(4)
        )
        mixed = jnp.zeros((BLOCK, LANES + 2 * STATE), f32)
        for k in range(4):
            mixed = mixed + taps[k : k + 1, :] * xbuf[pl.ds(HALO - 3 + k, BLOCK), :]
        mixed = silu(mixed)
        xc = mixed[:, 0:LANES]
        b = mixed[:, LANES : LANES + STATE].astype(bf16)
        xc_out[span, :] = xc.astype(bf16)
        b_out[span, :] = b
        c_out[span, :] = mixed[:, LANES + STATE :].astype(bf16)
        step = softplus(dt + dt_bias[:, 0:1])
        decay = -step * rate
        step_out[:, i * BLOCK : (i + 1) * BLOCK] = step
        cums, marks = [], jnp.zeros((HEADS, STRETCH), f32)
        for j in range(2):
            part = decay[:, j * STRETCH : (j + 1) * STRETCH]
            cum = lax.dot_general(
                part,
                upto,
                (((1,), (0,)), ((), ())),
                preferred_element_type=f32,
                precision=lax.Precision.HIGHEST,
            )
            cum_out[:, i * BLOCK + j * STRETCH : i * BLOCK + (j + 1) * STRETCH] = cum
            end = cum[:, STRETCH - 1 : STRETCH]
            marks = jnp.where(lane == j, end, jnp.where(lane == 2 + j, total, marks))
            total = total + end
            cums.append((cum, end))
        marks = jnp.where(lane == 4, total, marks)
        marks = spread_heads(jnp.exp(marks), fan)
        for j in range(2):
            cum, end = cums[j]
            here = slice(j * STRETCH, (j + 1) * STRETCH)
            weight = spread_heads(step[:, here] * jnp.exp(end - cum), fan)
            fresh = dot(b[here, :], (xc[here, :] * weight).astype(bf16), TN)
            ent_out[2 * i + j] = state
            pri_out[2 * i + j] = marks[2 + j : 3 + j, :]
            state = state * marks[j : j + 1, :] + fresh
    if last:
        decayed = marks[4:5, :]
        near = packed(state[:, 0:HALF], decayed[:, 0:HALF], columns[...])
        far = packed(state[:, HALF:], decayed[:, HALF:], columns[...])
        even = order[4] == 0
        keep_out[...] = jnp.where(even, near, far).astype(bf16)
        send_out[...] = jnp.where(even, far, near).astype(bf16)
    else:
        tail_out[...] = xbuf[BLOCK : BLOCK + HALO, :]
        state_out[...] = state
        total_out[...] = jnp.broadcast_to(total, (HEADS, STRETCH))


def stage_kernel(which, order, w, wbc, w_out, wbc_out, sems):
    copies = []
    for p in range(4):
        source = pl.ds(pl.multiple_of(order[p] * 512, 512), 512)
        target = pl.ds(p * 512, 512)
        copies.append(
            pltpu.make_async_copy(w.at[which, source, :], w_out.at[target, :], sems.at[0, p])
        )
        copies.append(
            pltpu.make_async_copy(wbc.at[which, source, :], wbc_out.at[target, :], sems.at[1, p])
        )
    for c in copies:
        c.start()
    for c in copies:
        c.wait()


def staged(which, order, w, wbc):
    return pl.pallas_call(
        functools.partial(stage_kernel, which),
        out_shape=[pltpu.VMEM((2048, 2 * LANES), bf16), pltpu.VMEM((2048, 2 * STATE), bf16)],
        in_specs=[smem(), in_hbm(), in_hbm()],
        out_specs=[vmem()] * 2,
        scratch_shapes=[pltpu.SemaphoreType.DMA((2, 4))],
        compiler_params=pltpu.CompilerParams(vmem_limit_bytes=2 * MIB),
        name="stage",
    )(order, kept_in_hbm(w), kept_in_hbm(wbc))


def stage_out_kernel(which, order, w, out, sems):
    copies = []
    for p in range(4):
        source = pl.ds(pl.multiple_of(order[(0, 2, 1, 3)[p]] * 512, 512), 512)
        copies.append(pltpu.make_async_copy(w.at[which, :, source], out.at[p], sems.at[p]))
    for c in copies:
        c.start()
    for c in copies:
        c.wait()


def staged_out(which, order, w):
    return pl.pallas_call(
        functools.partial(stage_out_kernel, which),
        out_shape=pltpu.VMEM((4, LANES, LANES), bf16),
        in_specs=[smem(), in_hbm()],
        out_specs=vmem(),
        scratch_shapes=[pltpu.SemaphoreType.DMA((4,))],
        compiler_params=pltpu.CompilerParams(vmem_limit_bytes=2 * MIB),
        name="stage_out",
    )(order, kept_in_hbm(w))


def vmem():
    return pl.BlockSpec(memory_space=pltpu.VMEM)


def smem():
    return pl.BlockSpec(memory_space=pltpu.SMEM)


def in_hbm():
    return pl.BlockSpec(memory_space=pltpu.HBM)


def kept_in_hbm(x):
    return pltpu.with_memory_space_constraint(x, pltpu.HBM)


def entry(order, pieces, columns, carry, gain, w, wbc, wdt, taps, dt_bias, a_log, last):
    first = carry is None
    rows = pieces[0].shape[0] - (HALO if first else 0)
    shape = jax.ShapeDtypeStruct
    outs = [
        pltpu.VMEM((rows, LANES), bf16),
        pltpu.VMEM((rows, LANES), bf16),
        pltpu.VMEM((rows, STATE), bf16),
        pltpu.VMEM((rows, STATE), bf16),
        pltpu.VMEM((HEADS, rows), f32),
        pltpu.VMEM((HEADS, rows), f32),
        pltpu.VMEM((rows // STRETCH, STATE, LANES), f32),
        pltpu.VMEM((rows // STRETCH, 1, LANES), f32),
    ]
    if last:
        outs += [shape((MSG, HALF), bf16)] * 2
    else:
        outs += [
            pltpu.VMEM((HALO, LANES + 2 * STATE), f32),
            pltpu.VMEM((STATE, LANES), f32),
            pltpu.VMEM((HEADS, STRETCH), f32),
        ]
    extra = [] if first else list(carry)
    operands = [order, *pieces, *([columns] if last else []), *extra, gain, w, wbc, wdt, taps, dt_bias, a_log]
    specs = [smem()] + [vmem()] * (len(operands) - 1)
    return pl.pallas_call(
        functools.partial(entry_kernel, first, last, rows),
        out_shape=outs,
        in_specs=specs,
        out_specs=[vmem()] * len(outs),
        scratch_shapes=[
            pltpu.VMEM((HALO + BLOCK, 2048), bf16),
            pltpu.VMEM((HALO + BLOCK, LANES + 2 * STATE), f32),
        ],
        compiler_params=pltpu.CompilerParams(vmem_limit_bytes=8 * MIB),
        name="entry",
    )(*operands)


def inside_kernel(rows, xc, b, c, cum, step, skip, y_out):
    q_pos = lax.broadcasted_iota(jnp.int32, (STRETCH, STRETCH), 0)
    k_pos = lax.broadcasted_iota(jnp.int32, (STRETCH, STRETCH), 1)
    causal = k_pos <= q_pos
    low_half = k_pos < HEAD_DIM
    skips = spread_heads(skip[...], head_fan())[0:1, :]
    for j in range(rows // STRETCH):
        here = slice(j * STRETCH, (j + 1) * STRETCH)
        match = jnp.where(causal, dot(c[here, :], b[here, :], NT), 0.0)
        cum_rows = cum[:, here]
        step_rows = step[:, here]
        cum_cols = jnp.transpose(cum_rows)
        for pair in range(HEADS // 2):
            weights = []
            for h in (2 * pair, 2 * pair + 1):
                gap = jnp.minimum(cum_cols[:, h : h + 1] - cum_rows[h : h + 1, :], 0.0)
                weights.append((match * (jnp.exp(gap) * step_rows[h : h + 1, :])).astype(bf16))
            lanes = slice(pair * STRETCH, (pair + 1) * STRETCH)
            x = xc[here, lanes].astype(f32)
            stacked = jnp.concatenate(
                [jnp.where(low_half, x, 0.0), jnp.where(low_half, 0.0, x)], axis=0
            ).astype(bf16)
            y_out[here, lanes] = (
                dot(jnp.concatenate(weights, axis=1), stacked) + skips[:, lanes] * x
            )


def inside(xc, b, c, cum, step, skip):
    rows = xc.shape[0]
    return pl.pallas_call(
        functools.partial(inside_kernel, rows),
        out_shape=pltpu.VMEM((rows, LANES), f32),
        in_specs=[vmem()] * 6,
        out_specs=vmem(),
        compiler_params=pltpu.CompilerParams(vmem_limit_bytes=4 * MIB),
        name="inside",
    )(xc, b, c, cum, step, skip)


def exit_kernel(chunks, order, mine, other, gain, wv, *refs):
    parts = [refs[6 * i : 6 * i + 6] for i in range(chunks)]
    own, plus_a, plus_b, minus_a, minus_b, opp_a, opp_b = refs[6 * chunks :]
    split = chunks * BLOCK // 2
    outs = ((plus_a, plus_b), (minus_a, minus_b), (opp_a, opp_b))
    fan = head_fan()
    row = lax.broadcasted_iota(jnp.int32, (BLOCK, BLOCK), 0) // HEAD_DIM
    lane = lax.broadcasted_iota(jnp.int32, (BLOCK, BLOCK), 1) // HEAD_DIM
    same_head = (row == lane).astype(bf16)
    here, there = mine[...].astype(f32), other[...].astype(f32)
    even = order[4] == 0
    came = jnp.concatenate([jnp.where(even, here, there), jnp.where(even, there, here)], axis=1)
    for i in range(chunks):
        y, z, c, cum, ent, pri = parts[i]
        mixed = []
        for j in range(2):
            here = slice(j * STRETCH, (j + 1) * STRETCH)
            entering = (ent[j] + pri[j] * came).astype(bf16)
            carried = dot(c[here, :], entering) * spread_heads(jnp.exp(cum[:, here]), fan)
            gated = (y[here, :] + carried) * silu(z[here, :].astype(f32))
            square = (gated * gated).astype(bf16)
            sums = jnp.concatenate(
                [dot(square[:, 0:BLOCK], same_head), dot(square[:, BLOCK:], same_head)], axis=1
            )
            scale = lax.rsqrt(sums * (1.0 / HEAD_DIM) + epsilon)
            mixed.append((gated * scale * gain[...]).astype(bf16))
        mixed = jnp.concatenate(mixed, axis=0)
        own[i * BLOCK : (i + 1) * BLOCK, :] = dot(mixed, wv[0]).astype(bf16)
        for p in range(3):
            product = dot(mixed, wv[p + 1]).astype(bf16)
            for j in range(2):
                at = i * BLOCK + j * STRETCH
                out = outs[p][at // split]
                at = at % split
                out[at : at + STRETCH, :] = product[j * STRETCH : (j + 1) * STRETCH, :]


def leave(order, mine, other, gain, w, parts):
    rows = len(parts) * BLOCK
    shape = jax.ShapeDtypeStruct
    outs = [shape((rows, LANES), bf16)] + [shape((rows // 2, LANES), bf16)] * 6
    operands = [order, mine, other, gain, w, *(a for part in parts for a in part)]
    return pl.pallas_call(
        functools.partial(exit_kernel, len(parts)),
        out_shape=outs,
        in_specs=[smem()] + [vmem()] * (len(operands) - 1),
        out_specs=[vmem()] * len(outs),
        compiler_params=pltpu.CompilerParams(vmem_limit_bytes=6 * MIB),
        name="leave",
    )(*operands)


def small_call(kernel, name, outs, place, *operands):
    return pl.pallas_call(
        kernel,
        out_shape=outs,
        in_specs=[smem()] + [vmem()] * len(operands),
        out_specs=[vmem()] * len(outs),
        compiler_params=pltpu.CompilerParams(vmem_limit_bytes=2 * MIB),
        name=name,
    )(place, *operands)


def chip_kernel(place, keep, got, out):
    even = place[4] == 0
    mine, other = opened(keep), opened(got)
    both = after(chosen(even, mine, other), chosen(even, other, mine))
    out[...] = packed(*both, columns_in(keep) + columns_in(got)).astype(bf16)


def row_kernel(place, chip, one, two, three, row_out, before_out):
    y = place[5]
    ring = [opened(r) for r in (chip, one, two, three)]
    row, before = nothing(), nothing()
    for at in range(4):
        here = ring[0]
        for k in range(1, 4):
            here = chosen((y + 4 - at) % 4 == k, ring[k], here)
        before = chosen(at < y, after(before, here), before)
        row = after(row, here)
    columns = sum(columns_in(r) for r in (chip, one, two, three))
    row_out[...] = packed(*row, columns).astype(bf16)
    before_out[...] = packed(*before, columns)


def arrive_kernel(place, one, two, three, before, keep, got, mine_out, other_out, columns_out):
    even = place[4] == 0
    z = place[6]
    came = nothing()
    for k, r in ((3, three), (2, two), (1, one)):
        came = chosen(z >= k, after(came, opened(r)), came)
    first = after(came, opened(before))
    second = after(first, chosen(even, opened(keep), opened(got)))
    mine_out[...] = jnp.where(even, first[0], second[0]).astype(bf16)
    other_out[...] = jnp.where(even, second[0], first[0]).astype(bf16)
    columns_out[...] = sum(columns_in(r) for r in (before, one, two, three))


def give_kernel(columns, x, out):
    cell = lax.broadcasted_iota(jnp.int32, (512, HALF), 0)
    for part in range(2):
        wanted = 2.0 * columns[2 * part : 2 * part + 1, :] + columns[2 * part + 1 : 2 * part + 2, :]
        pick = (cell == wanted.astype(jnp.int32)).astype(bf16)
        for r in range(2):
            rows = dot(pick, x[r * 512 : (r + 1) * 512, :], TN).astype(bf16)
            out[part * 16 : (part + 1) * 16, r * 16 : (r + 1) * 16, :] = rows.reshape(16, 16, 512)


def given(columns, x):
    return pl.pallas_call(
        give_kernel,
        out_shape=jax.ShapeDtypeStruct((32, 32, 512), bf16),
        in_specs=[vmem()] * 2,
        out_specs=vmem(),
        compiler_params=pltpu.CompilerParams(vmem_limit_bytes=6 * MIB),
        name="give",
    )(columns, x)


def turned(by):
    return [(i, (i + by) % TP) for i in range(TP)]


def around(x, by):
    return lax.ppermute(x, "tp", turned(by))


def swapped(x):
    return lax.ppermute(x, "seq_2", [(0, 1), (1, 0)])


def arriving_state(place, keep, send, weights, beside, wrapped):
    shape = jax.ShapeDtypeStruct
    got = swapped(send)
    msg = shape((MSG, HALF), bf16)
    (chip,) = small_call(chip_kernel, "chip", [msg], place, keep, got)
    ring = [lax.ppermute(chip, "seq_1", turned(k)) for k in (1, 2, 3)]
    row, before = small_call(
        row_kernel,
        "row",
        [msg, shape((MSG, HALF), f32)],
        behind(place, weights),
        chip,
        *ring,
    )
    earlier = [
        lax.ppermute(row, "seq_0", turned(k)[: 4 if wrapped else 4 - k]) for k in (1, 2, 3)
    ]
    mine, other, columns = small_call(
        arrive_kernel,
        "arrive",
        [shape((STATE, HALF), bf16)] * 2 + [shape((8, HALF), f32)],
        behind(place, *beside),
        *earlier,
        before,
        keep,
        got,
    )
    return mine, swapped(other), columns


def behind(x, *done):
    return lax.optimization_barrier((x, *done))[0]


def with_halo(shard):
    count = lax.axis_size(SEQ)
    halo = lax.ppermute(shard[-HALO:], SEQ, [(i, i + 1) for i in range(count - 1)])
    return jnp.concatenate([halo, shard[:BLOCK]], axis=0)


def layer(which, shard, first, place, params, large, columns, early=()):
    gain, wdt, taps, dt_bias, a_log, skip, out_gain = params
    w, wbc, w_out = large
    count = shard.shape[0] // BLOCK
    rows = [shard[i * BLOCK : (i + 1) * BLOCK] for i in range(count)]
    wv, wbcv = staged(which, behind(place, first), w, wbc)
    own, left, right, opposite = [first], [], [], []
    carry, kept, gate = None, [], place

    def send(i):
        if i:
            own.append(behind(rows[i], first, *early_gates.get(i, ())))
        left.append(around(own[i], 1))
        right.append(around(own[i], -1))

    def forward(i, *gates):
        source = left[i] if i % 2 == 0 else right[i]
        source = behind(source, *gates) if gates else source
        opposite.append(around(source, 1 if i % 2 == 0 else -1))

    def enter(i):
        nonlocal carry, gate
        last = i == count - 1
        out = entry(
            gate,
            (own[i], left[i], right[i], opposite[i]),
            columns,
            carry,
            gain,
            wv,
            wbcv,
            wdt,
            taps,
            dt_bias,
            a_log,
            last,
        )
        z, xc, b, c, cum, step, ent, pri = out[:8]
        carry = out[8:]
        y = inside(xc, b, c, cum, step, skip)
        kept.append((y, z, c, cum, ent, pri))
        if i < 2:
            gate = behind(place, y)

    early_gates = {count - 1: early} if early else {count - 2: (wbcv,)}
    for i in range(count - 1):
        send(i)
    forward(0)
    if which == 0:
        send(count - 1)
        forward(1)
        forward(2)
        enter(0)
        forward(3, carry[0])
        enter(1)
    else:
        enter(0)
        early_gates[count - 1] = (carry[0],)
        send(count - 1)
        forward(1)
        enter(1)
        forward(2)
        forward(3, carry[0])
    enter(2)
    enter(3)
    wov = staged_out(which, behind(place, carry[0]), w_out)
    mine, other, columns = arriving_state(
        place, *carry, wov, [k[0] for k in kept], which == 0
    )
    results = []
    for low, high in ((0, 2), (2, 4)):
        own_part, plus_a, plus_b, minus_a, minus_b, opp_a, opp_b = leave(
            place, mine, other, out_gain, wov, kept[low:high]
        )
        across_a, across_b = around(opp_a, 1), around(opp_b, -1)
        down_a, up_b = around(minus_a, -1), around(plus_b, 1)
        up_a = around((plus_a.astype(f32) + across_a.astype(f32)).astype(bf16), 1)
        down_b = around((minus_b.astype(f32) + across_b.astype(f32)).astype(bf16), -1)
        here = jnp.concatenate(rows[low:high], axis=0).astype(f32) + own_part.astype(f32)
        half = here.shape[0] // 2
        for span, up, down in ((slice(0, half), up_a, down_a), (slice(half, 2 * half), up_b, down_b)):
            results.append(here[span] + up.astype(f32) + down.astype(f32))
    return jnp.concatenate(results, axis=0).astype(bf16), columns


def permuted(x, source):
    pick = (source[:, None] == jnp.arange(x.shape[0])[None, :]).astype(bf16)
    return jnp.dot(pick, x, preferred_element_type=f32).astype(bf16)


def body(
    tokens,
    col_order,
    in_gain,
    w_in,
    w_bc,
    w_dt,
    conv_x,
    conv_bc,
    dt_bias,
    a_log,
    d_skip,
    out_gain,
    w_out,
):
    first = with_halo(tokens)
    arguments = (in_gain, w_in, w_dt, conv_x, conv_bc, dt_bias, a_log, d_skip, out_gain, col_order)
    in_gain, w_in, w_dt, conv_x, conv_bc, dt_bias, a_log, d_skip, out_gain, col_order = behind(
        arguments, first
    )
    x = lax.axis_index("tp")
    core, y, z = (lax.axis_index(a) for a in ("seq_2", "seq_1", "seq_0"))
    place = jnp.stack([x, (x + 3) & 3, (x + 1) & 3, (x + 2) & 3, core, y, z]).astype(jnp.int32)
    w = w_in.reshape(2, 2048, 2 * LANES)

    def on_lanes(heads):
        return jnp.broadcast_to(heads[:, None], (HEADS, STRETCH))

    def params(which):
        return (
            in_gain[which].reshape(TP, 1, 512),
            w_dt[which].T.reshape(HEADS, TP, 512).transpose(1, 0, 2),
            jnp.concatenate([conv_x[which], conv_bc[which]], axis=1),
            on_lanes(dt_bias[which]),
            on_lanes(a_log[which]),
            on_lanes(d_skip[which]),
            out_gain[which].reshape(1, LANES),
        )

    starts = col_order.reshape(16, 64)[:, 0]
    slot = jnp.arange(512)
    columns = jnp.where(
        slot // 16 == lax.axis_index(SEQ), jnp.tile(starts % 512, 32), 0
    ).reshape(2, 256)
    columns = jnp.stack([columns[0] // 2, columns[0] % 2, columns[1] // 2, columns[1] % 2])
    columns = jnp.pad(columns.astype(f32), ((0, 4), (0, 0)))
    visit = jnp.arange(16)[:, None]
    along = jnp.arange(64)[None, :]
    row = jnp.where((starts >= 512)[:, None], 63 - along, along)
    take = ((row // 2) * 32 + (row % 2) * 16 + visit).reshape(1024)
    place, small, w, columns, take = lax.optimization_barrier(
        (place, [params(0), params(1)], w, columns, take)
    )
    large = (w, w_bc, w_out)

    row_result, columns = layer(0, tokens, first, place, small[0], large, columns, (w,))
    payload = given(columns, row_result)
    arrived = lax.all_to_all(payload, SEQ, 0, 0, tiled=True).reshape(1024, 512)
    own_rows = permuted(arrived, take)
    return layer(1, own_rows, with_halo(own_rows), place, small[1], large, columns)[0]


def solution(mesh):
    torus = Mesh(mesh.devices.reshape(4, 4, 2, mesh.shape["tp"]), ("seq_0", "seq_1", "seq_2", "tp"))
    return jax.shard_map(
        body,
        mesh=torus,
        in_specs=(
            P(SEQ, "tp"),
            P(SEQ),
            P(),
            P(None, None, None, "tp"),
            P(),
            P(None, None, "tp"),
            P(None, None, "tp"),
            P(),
            P(None, "tp"),
            P(None, "tp"),
            P(None, "tp"),
            P(None, "tp"),
            P(None, "tp", None),
        ),
        out_specs=P(SEQ, "tp"),
        check_vma=False,
    )
```

```python
import functools

import jax
import jax.numpy as jnp
from jax import lax
from jax.experimental import pallas as pl
from jax.experimental.pallas import tpu as pltpu
from jax.sharding import Mesh
from jax.sharding import PartitionSpec as P

HEAD_DIM = 64
STATE = 128
STRETCH = 128
HEADS = 8
LANES = 512
HALF = 256
HALO = 16
BLOCK = 256
MSG = 144
SEQ = ("seq_0", "seq_1", "seq_2")
TP = 4
epsilon = 1e-05
f32 = jnp.float32
bf16 = jnp.bfloat16
NT = (((1,), (1,)), ((), ()))
TN = (((0,), (0,)), ((), ()))
MIB = 2**20


def dot(a, b, dims=None):
    dims = dims or (((1,), (0,)), ((), ()))
    return lax.dot_general(a, b, dims, preferred_element_type=f32)


def silu(x):
    return x / (1.0 + jnp.exp(-x))


def softplus(x):
    return jnp.maximum(x, 0.0) + jnp.log1p(jnp.exp(-jnp.abs(x)))


def spread_heads(values, fan):
    high = values.astype(bf16)
    low = (values - high.astype(f32)).astype(bf16)
    return dot(jnp.concatenate([high, low], axis=0), fan, TN)


def packed(state, decay, columns):
    high = decay.astype(bf16).astype(f32)
    row = lax.broadcasted_iota(jnp.int32, (8, decay.shape[1]), 0)
    rest = jnp.where(row == 0, high, jnp.where(row == 1, decay - high, 0.0))
    return jnp.concatenate([state, columns, rest], axis=0)


def opened(msg):
    msg = msg[...].astype(f32)
    at = STATE + 8
    return msg[:STATE], msg[at : at + 1] + msg[at + 1 : at + 2]


def columns_in(msg):
    return msg[...].astype(f32)[STATE : STATE + 8]


def after(a, b):
    return b[0] + b[1] * a[0], a[1] * b[1]


def chosen(pred, a, b):
    return jnp.where(pred, a[0], b[0]), jnp.where(pred, a[1], b[1])


def nothing():
    return jnp.zeros((STATE, HALF), f32), jnp.ones((1, HALF), f32)


def head_fan():
    row = lax.broadcasted_iota(jnp.int32, (2 * HEADS, LANES), 0)
    lane = lax.broadcasted_iota(jnp.int32, (2 * HEADS, LANES), 1)
    return (row % HEADS == lane // HEAD_DIM).astype(bf16)


def entry_kernel(first, last, offset, rows, *refs):
    (order, own, left, right, opposite) = refs[:5]
    refs = refs[5:]
    columns = ()
    if last:
        columns, refs = refs[:1], refs[1:]
    if not first:
        tail_in, state_in, total_in, refs = *refs[:3], refs[3:]
    (gain, wv, wbcv, wdt, taps, dt_bias, a_log), refs = refs[:7], refs[7:]
    (z_out, xc_out, b_out, c_out, cum_out, step_out, ent_out, pri_out), refs = refs[:8], refs[8:]
    if last:
        (keep_out, send_out), refs = refs[:2], refs[2:]
        columns = columns[0]
    else:
        (tail_out, state_out, total_out), refs = refs[:3], refs[3:]
    nbuf, xbuf = refs

    fan = head_fan()
    k_pos = lax.broadcasted_iota(jnp.int32, (STRETCH, STRETCH), 0)
    q_pos = lax.broadcasted_iota(jnp.int32, (STRETCH, STRETCH), 1)
    upto = (k_pos <= q_pos).astype(f32)
    lane = lax.broadcasted_iota(jnp.int32, (HEADS, STRETCH), 1)
    rate = jnp.exp(a_log[:, 0:1])
    if first:
        state = jnp.zeros((STATE, LANES), f32)
        total = jnp.zeros((HEADS, 1), f32)
    else:
        state = state_in[...]
        total = total_in[:, 0:1]
        xbuf[0:HALO, :] = tail_in[...]
    for i in range(rows // BLOCK):
        span = pl.ds(i * BLOCK, BLOCK)
        above = pl.ds(offset + i * BLOCK, BLOCK)
        pieces = [r[above, :] for r in (own, left, right, opposite)]
        widen = [x.astype(f32) for x in pieces]
        square = sum(jnp.sum(x * x, axis=1, keepdims=True) for x in widen)
        scale = lax.rsqrt(square * (1.0 / 2048) + epsilon)
        for p in range(4):
            nbuf[HALO : HALO + BLOCK, p * 512 : (p + 1) * 512] = (
                widen[p] * scale * gain[order[p]]
            ).astype(bf16)
        if first and i == 0:
            widen = [r[0:HALO, :].astype(f32) for r in (own, left, right, opposite)]
            square = sum(jnp.sum(x * x, axis=1, keepdims=True) for x in widen)
            scale = lax.rsqrt(square * (1.0 / 2048) + epsilon)
            for p in range(4):
                nbuf[0:HALO, p * 512 : (p + 1) * 512] = (
                    widen[p] * scale * gain[order[p]]
                ).astype(bf16)
        low = 0 if first and i == 0 else HALO
        if low and i > 0:
            xbuf[0:HALO, :] = xbuf[BLOCK : BLOCK + HALO, :]
        normed = nbuf[low : HALO + BLOCK, :]
        xbuf[low : HALO + BLOCK, 0:LANES] = dot(normed, wv[:, 0:LANES]).astype(bf16).astype(f32)
        z_out[span, :] = dot(nbuf[HALO:, :], wv[:, LANES:]).astype(bf16)
        xbuf[low : HALO + BLOCK, LANES:] = dot(normed, wbcv[...]).astype(bf16).astype(f32)
        dt = sum(
            dot(wdt[order[p]], nbuf[HALO:, p * 512 : (p + 1) * 512], NT) for p in range(4)
        )
        mixed = jnp.zeros((BLOCK, LANES + 2 * STATE), f32)
        for k in range(4):
            mixed = mixed + taps[k : k + 1, :] * xbuf[pl.ds(HALO - 3 + k, BLOCK), :]
        mixed = silu(mixed)
        xc = mixed[:, 0:LANES]
        b = mixed[:, LANES : LANES + STATE].astype(bf16)
        xc_out[span, :] = xc.astype(bf16)
        b_out[span, :] = b
        c_out[span, :] = mixed[:, LANES + STATE :].astype(bf16)
        step = softplus(dt + dt_bias[:, 0:1])
        decay = -step * rate
        step_out[:, i * BLOCK : (i + 1) * BLOCK] = step
        cums, marks = [], jnp.zeros((HEADS, STRETCH), f32)
        for j in range(2):
            part = decay[:, j * STRETCH : (j + 1) * STRETCH]
            cum = lax.dot_general(
                part,
                upto,
                (((1,), (0,)), ((), ())),
                preferred_element_type=f32,
                precision=lax.Precision.HIGHEST,
            )
            cum_out[:, i * BLOCK + j * STRETCH : i * BLOCK + (j + 1) * STRETCH] = cum
            end = cum[:, STRETCH - 1 : STRETCH]
            marks = jnp.where(lane == j, end, jnp.where(lane == 2 + j, total, marks))
            total = total + end
            cums.append((cum, end))
        marks = jnp.where(lane == 4, total, marks)
        marks = spread_heads(jnp.exp(marks), fan)
        for j in range(2):
            cum, end = cums[j]
            here = slice(j * STRETCH, (j + 1) * STRETCH)
            weight = spread_heads(step[:, here] * jnp.exp(end - cum), fan)
            fresh = dot(b[here, :], (xc[here, :] * weight).astype(bf16), TN)
            ent_out[2 * i + j] = state
            pri_out[2 * i + j] = marks[2 + j : 3 + j, :]
            state = state * marks[j : j + 1, :] + fresh
    if last:
        decayed = marks[4:5, :]
        near = packed(state[:, 0:HALF], decayed[:, 0:HALF], columns[...])
        far = packed(state[:, HALF:], decayed[:, HALF:], columns[...])
        even = order[4] == 0
        keep_out[...] = jnp.where(even, near, far).astype(bf16)
        send_out[...] = jnp.where(even, far, near).astype(bf16)
    else:
        tail_out[...] = xbuf[BLOCK : BLOCK + HALO, :]
        state_out[...] = state
        total_out[...] = jnp.broadcast_to(total, (HEADS, STRETCH))


def stage_kernel(which, order, w, wbc, w_out, wbc_out, sems):
    copies = []
    for p in range(4):
        source = pl.ds(pl.multiple_of(order[p] * 512, 512), 512)
        target = pl.ds(p * 512, 512)
        copies.append(
            pltpu.make_async_copy(w.at[which, source, :], w_out.at[target, :], sems.at[0, p])
        )
        copies.append(
            pltpu.make_async_copy(wbc.at[which, source, :], wbc_out.at[target, :], sems.at[1, p])
        )
    for c in copies:
        c.start()
    for c in copies:
        c.wait()


def staged(which, order, w, wbc):
    return pl.pallas_call(
        functools.partial(stage_kernel, which),
        out_shape=[pltpu.VMEM((2048, 2 * LANES), bf16), pltpu.VMEM((2048, 2 * STATE), bf16)],
        in_specs=[smem(), in_hbm(), in_hbm()],
        out_specs=[vmem()] * 2,
        scratch_shapes=[pltpu.SemaphoreType.DMA((2, 4))],
        compiler_params=pltpu.CompilerParams(vmem_limit_bytes=2 * MIB),
        name="stage",
    )(order, kept_in_hbm(w), kept_in_hbm(wbc))


def stage_out_kernel(which, order, w, out, sems):
    copies = []
    for p in range(4):
        source = pl.ds(pl.multiple_of(order[(0, 2, 1, 3)[p]] * 512, 512), 512)
        copies.append(pltpu.make_async_copy(w.at[which, :, source], out.at[p], sems.at[p]))
    for c in copies:
        c.start()
    for c in copies:
        c.wait()


def staged_out(which, order, w):
    return pl.pallas_call(
        functools.partial(stage_out_kernel, which),
        out_shape=pltpu.VMEM((4, LANES, LANES), bf16),
        in_specs=[smem(), in_hbm()],
        out_specs=vmem(),
        scratch_shapes=[pltpu.SemaphoreType.DMA((4,))],
        compiler_params=pltpu.CompilerParams(vmem_limit_bytes=2 * MIB),
        name="stage_out",
    )(order, kept_in_hbm(w))


def vmem():
    return pl.BlockSpec(memory_space=pltpu.VMEM)


def smem():
    return pl.BlockSpec(memory_space=pltpu.SMEM)


def in_hbm():
    return pl.BlockSpec(memory_space=pltpu.HBM)


def kept_in_hbm(x):
    return pltpu.with_memory_space_constraint(x, pltpu.HBM)


def entry(order, pieces, offset, columns, carry, gain, w, wbc, wdt, taps, dt_bias, a_log, last):
    first = carry is None
    rows = BLOCK
    shape = jax.ShapeDtypeStruct
    outs = [
        pltpu.VMEM((rows, LANES), bf16),
        pltpu.VMEM((rows, LANES), bf16),
        pltpu.VMEM((rows, STATE), bf16),
        pltpu.VMEM((rows, STATE), bf16),
        pltpu.VMEM((HEADS, rows), f32),
        pltpu.VMEM((HEADS, rows), f32),
        pltpu.VMEM((rows // STRETCH, STATE, LANES), f32),
        pltpu.VMEM((rows // STRETCH, 1, LANES), f32),
    ]
    if last:
        outs += [shape((MSG, HALF), bf16)] * 2
    else:
        outs += [
            pltpu.VMEM((HALO, LANES + 2 * STATE), f32),
            pltpu.VMEM((STATE, LANES), f32),
            pltpu.VMEM((HEADS, STRETCH), f32),
        ]
    extra = [] if first else list(carry)
    operands = [order, *pieces, *([columns] if last else []), *extra, gain, w, wbc, wdt, taps, dt_bias, a_log]
    specs = [smem()] + [vmem()] * (len(operands) - 1)
    return pl.pallas_call(
        functools.partial(entry_kernel, first, last, offset, rows),
        out_shape=outs,
        in_specs=specs,
        out_specs=[vmem()] * len(outs),
        scratch_shapes=[
            pltpu.VMEM((HALO + BLOCK, 2048), bf16),
            pltpu.VMEM((HALO + BLOCK, LANES + 2 * STATE), f32),
        ],
        compiler_params=pltpu.CompilerParams(vmem_limit_bytes=8 * MIB),
        name="entry",
    )(*operands)


def inside_kernel(rows, xc, b, c, cum, step, skip, y_out):
    q_pos = lax.broadcasted_iota(jnp.int32, (STRETCH, STRETCH), 0)
    k_pos = lax.broadcasted_iota(jnp.int32, (STRETCH, STRETCH), 1)
    causal = k_pos <= q_pos
    low_half = k_pos < HEAD_DIM
    skips = spread_heads(skip[...], head_fan())[0:1, :]
    for j in range(rows // STRETCH):
        here = slice(j * STRETCH, (j + 1) * STRETCH)
        match = jnp.where(causal, dot(c[here, :], b[here, :], NT), 0.0)
        cum_rows = cum[:, here]
        step_rows = step[:, here]
        cum_cols = jnp.transpose(cum_rows)
        for pair in range(HEADS // 2):
            weights = []
            for h in (2 * pair, 2 * pair + 1):
                gap = jnp.minimum(cum_cols[:, h : h + 1] - cum_rows[h : h + 1, :], 0.0)
                weights.append((match * (jnp.exp(gap) * step_rows[h : h + 1, :])).astype(bf16))
            lanes = slice(pair * STRETCH, (pair + 1) * STRETCH)
            x = xc[here, lanes].astype(f32)
            stacked = jnp.concatenate(
                [jnp.where(low_half, x, 0.0), jnp.where(low_half, 0.0, x)], axis=0
            ).astype(bf16)
            y_out[here, lanes] = (
                dot(jnp.concatenate(weights, axis=1), stacked) + skips[:, lanes] * x
            )


def inside(xc, b, c, cum, step, skip):
    rows = xc.shape[0]
    return pl.pallas_call(
        functools.partial(inside_kernel, rows),
        out_shape=pltpu.VMEM((rows, LANES), f32),
        in_specs=[vmem()] * 6,
        out_specs=vmem(),
        compiler_params=pltpu.CompilerParams(vmem_limit_bytes=4 * MIB),
        name="inside",
    )(xc, b, c, cum, step, skip)


def exit_kernel(chunks, order, mine, other, gain, wv, *refs):
    parts = [refs[6 * i : 6 * i + 6] for i in range(chunks)]
    own, up, down, plus_a, minus_b = refs[6 * chunks :]
    split = chunks * BLOCK // 2
    outs = (((plus_a, 0), (up, split)), ((down, split), (minus_b, 0)), ((up, 0), (down, 0)))
    fan = head_fan()
    row = lax.broadcasted_iota(jnp.int32, (BLOCK, BLOCK), 0) // HEAD_DIM
    lane = lax.broadcasted_iota(jnp.int32, (BLOCK, BLOCK), 1) // HEAD_DIM
    same_head = (row == lane).astype(bf16)
    here, there = mine[...].astype(f32), other[...].astype(f32)
    even = order[4] == 0
    came = jnp.concatenate([jnp.where(even, here, there), jnp.where(even, there, here)], axis=1)
    for i in range(chunks):
        y, z, c, cum, ent, pri = parts[i]
        mixed = []
        for j in range(2):
            here = slice(j * STRETCH, (j + 1) * STRETCH)
            entering = (ent[j] + pri[j] * came).astype(bf16)
            carried = dot(c[here, :], entering) * spread_heads(jnp.exp(cum[:, here]), fan)
            gated = (y[here, :] + carried) * silu(z[here, :].astype(f32))
            square = (gated * gated).astype(bf16)
            sums = jnp.concatenate(
                [dot(square[:, 0:BLOCK], same_head), dot(square[:, BLOCK:], same_head)], axis=1
            )
            scale = lax.rsqrt(sums * (1.0 / HEAD_DIM) + epsilon)
            mixed.append((gated * scale * gain[...]).astype(bf16))
        mixed = jnp.concatenate(mixed, axis=0)
        own[i * BLOCK : (i + 1) * BLOCK, :] = dot(mixed, wv[0]).astype(bf16)
        for p in range(3):
            product = dot(mixed, wv[p + 1]).astype(bf16)
            for j in range(2):
                at = i * BLOCK + j * STRETCH
                out, base = outs[p][at // split]
                at = base + at % split
                out[at : at + STRETCH, :] = product[j * STRETCH : (j + 1) * STRETCH, :]


def leave(order, mine, other, gain, w, parts):
    rows = len(parts) * BLOCK
    shape = jax.ShapeDtypeStruct
    outs = [shape((rows, LANES), bf16)] * 3 + [shape((rows // 2, LANES), bf16)] * 2
    operands = [order, mine, other, gain, w, *(a for part in parts for a in part)]
    return pl.pallas_call(
        functools.partial(exit_kernel, len(parts)),
        out_shape=outs,
        in_specs=[smem()] + [vmem()] * (len(operands) - 1),
        out_specs=[vmem()] * len(outs),
        compiler_params=pltpu.CompilerParams(vmem_limit_bytes=6 * MIB),
        name="leave",
    )(*operands)


def small_call(kernel, name, outs, place, *operands):
    return pl.pallas_call(
        kernel,
        out_shape=outs,
        in_specs=[smem()] + [vmem()] * len(operands),
        out_specs=[vmem()] * len(outs),
        compiler_params=pltpu.CompilerParams(vmem_limit_bytes=2 * MIB),
        name=name,
    )(place, *operands)


def chip_kernel(place, keep, got, out):
    even = place[4] == 0
    mine, other = opened(keep), opened(got)
    both = after(chosen(even, mine, other), chosen(even, other, mine))
    out[...] = packed(*both, columns_in(keep) + columns_in(got)).astype(bf16)


def pair_kernel(axis, place, mine, other, pair_out, before_out):
    odd = place[axis] % 2 == 1
    here, there = opened(mine), opened(other)
    pair = after(chosen(odd, there, here), chosen(odd, here, there))
    columns = columns_in(mine) + columns_in(other)
    pair_out[...] = packed(*pair, columns).astype(bf16)
    before_out[...] = packed(*chosen(odd, there, nothing()), columns)


def ring_kernel(axis, place, mine, other, before, ring_out, before_out):
    upper = place[axis] >= 2
    here, there = opened(mine), opened(other)
    ring = after(chosen(upper, there, here), chosen(upper, here, there))
    columns = columns_in(mine) + columns_in(other)
    ring_out[...] = packed(*ring, columns).astype(bf16)
    came = after(chosen(upper, there, nothing()), opened(before))
    before_out[...] = packed(*came, columns)


def arrive_kernel(
    place, mine, other, before_z, before_y, keep, got, mine_out, other_out, columns_out
):
    even = place[4] == 0
    upper = place[6] >= 2
    came = after(chosen(upper, opened(other), nothing()), opened(before_z))
    first = after(came, opened(before_y))
    second = after(first, chosen(even, opened(keep), opened(got)))
    mine_out[...] = jnp.where(even, first[0], second[0]).astype(bf16)
    other_out[...] = jnp.where(even, second[0], first[0]).astype(bf16)
    columns_out[...] = columns_in(mine) + columns_in(other)


def give_kernel(columns, x, out):
    cell = lax.broadcasted_iota(jnp.int32, (512, HALF), 0)
    for part in range(2):
        wanted = 2.0 * columns[2 * part : 2 * part + 1, :] + columns[2 * part + 1 : 2 * part + 2, :]
        pick = (cell == wanted.astype(jnp.int32)).astype(bf16)
        for r in range(2):
            rows = dot(pick, x[r * 512 : (r + 1) * 512, :], TN).astype(bf16)
            out[part * 16 : (part + 1) * 16, r * 16 : (r + 1) * 16, :] = rows.reshape(16, 16, 512)


def given(columns, x):
    return pl.pallas_call(
        give_kernel,
        out_shape=jax.ShapeDtypeStruct((32, 32, 512), bf16),
        in_specs=[vmem()] * 2,
        out_specs=vmem(),
        compiler_params=pltpu.CompilerParams(vmem_limit_bytes=6 * MIB),
        name="give",
    )(columns, x)


def turned(by):
    return [(i, (i + by) % TP) for i in range(TP)]


def around(x, by):
    return lax.ppermute(x, "tp", turned(by))


def swapped(x):
    return lax.ppermute(x, "seq_2", [(0, 1), (1, 0)])


def arriving_state(place, keep, send, weights, beside):
    shape = jax.ShapeDtypeStruct
    msg, wide = shape((MSG, HALF), bf16), shape((MSG, HALF), f32)
    within, across = [(0, 1), (1, 0), (2, 3), (3, 2)], [(0, 3), (3, 0), (1, 2), (2, 1)]

    def scanned(kernel, axis, name, place, *operands):
        return small_call(functools.partial(kernel, axis), name, [msg, wide], place, *operands)

    got = swapped(send)
    (chip,) = small_call(chip_kernel, "chip", [msg], place, keep, got)
    pair, before = scanned(
        pair_kernel, 5, "pair_y", behind(place, weights), chip, lax.ppermute(chip, "seq_1", within)
    )
    ring, before = scanned(
        ring_kernel, 5, "ring_y", place, pair, lax.ppermute(pair, "seq_1", across), before
    )
    pair, before_z = scanned(
        pair_kernel, 6, "pair_z", behind(place, *beside[:1]), ring, lax.ppermute(ring, "seq_0", within)
    )
    mine, other, columns = small_call(
        arrive_kernel,
        "arrive",
        [shape((STATE, HALF), bf16)] * 2 + [shape((8, HALF), f32)],
        behind(place, *beside),
        pair,
        lax.ppermute(pair, "seq_0", across),
        before_z,
        before,
        keep,
        got,
    )
    return mine, swapped(other), columns


def behind(x, *done):
    return lax.optimization_barrier((x, *done))[0]


def with_halo(shard):
    count = lax.axis_size(SEQ)
    halo = lax.ppermute(shard[-HALO:], SEQ, [(i, i + 1) for i in range(count - 1)])
    return jnp.concatenate([halo, shard[: 2 * BLOCK]], axis=0)


def layer(which, shard, first, place, params, large, columns, early):
    gain, wdt, taps, dt_bias, a_log, skip, out_gain = params
    w, wbc, w_out = large
    rows = [first, shard[2 * BLOCK : 3 * BLOCK], shard[3 * BLOCK :]]
    wv, wbcv = staged(which, behind(place, first), w, wbc)
    carry, kept, gate = None, [], place

    def enter(i, pieces, offset, last=False):
        nonlocal carry, gate
        out = entry(
            gate, pieces, offset, columns, carry, gain, wv, wbcv, wdt, taps, dt_bias, a_log, last
        )
        z, xc, b, c, cum, step, ent, pri = out[:8]
        carry = out[8:]
        y = inside(xc, b, c, cum, step, skip)
        kept.append((y, z, c, cum, ent, pri))
        if i < 2:
            gate = behind(place, y)

    own = [first, behind(rows[1], first), behind(rows[2], first)]
    left, right = [around(first, 1)], [around(first, -1)]
    right.append(around(own[1], -1))
    opposite = [around(left[0], 1)]
    right.append(around(behind(rows[2], right[0], wbcv) if which else own[2], -1))
    left.append(around(behind(rows[1], right[1], *early), 1))
    opposite.append(around(right[1], -1))
    pieces = (own[0], left[0], right[0], opposite[0])
    enter(0, pieces, HALO)
    left.append(around(behind(rows[2], carry[0]), 1))
    opposite.append(around(right[2], -1))
    enter(1, pieces, HALO + BLOCK)
    enter(2, (own[1], left[1], right[1], opposite[1]), 0)
    enter(3, (own[2], left[2], right[2], opposite[2]), 0, True)
    wov = staged_out(which, behind(place, carry[0]), w_out)
    mine, other, columns = arriving_state(place, *carry, wov, [k[0] for k in kept])
    results = []
    for low in (0, 2):
        own_part, up, down, plus_a, minus_b = leave(
            place, mine, other, out_gain, wov, kept[low : low + 2]
        )
        up, down = around(up, 1), around(down, -1)
        plus_a = around((plus_a.astype(f32) + up[:BLOCK].astype(f32)).astype(bf16), 1)
        minus_b = around((minus_b.astype(f32) + down[:BLOCK].astype(f32)).astype(bf16), -1)
        here = shard[low * BLOCK : (low + 2) * BLOCK].astype(f32) + own_part.astype(f32)
        results.append(here[:BLOCK] + plus_a.astype(f32) + down[BLOCK:].astype(f32))
        results.append(here[BLOCK:] + up[BLOCK:].astype(f32) + minus_b.astype(f32))
    return jnp.concatenate(results, axis=0).astype(bf16), columns


def permuted(x, source):
    pick = (source[:, None] == jnp.arange(x.shape[0])[None, :]).astype(bf16)
    return jnp.dot(pick, x, preferred_element_type=f32).astype(bf16)


def body(
    tokens,
    col_order,
    in_gain,
    w_in,
    w_bc,
    w_dt,
    conv_x,
    conv_bc,
    dt_bias,
    a_log,
    d_skip,
    out_gain,
    w_out,
):
    first = with_halo(tokens)
    arguments = (in_gain, w_in, w_dt, conv_x, conv_bc, dt_bias, a_log, d_skip, out_gain, col_order)
    in_gain, w_in, w_dt, conv_x, conv_bc, dt_bias, a_log, d_skip, out_gain, col_order = behind(
        arguments, first
    )
    x = lax.axis_index("tp")
    core, y, z = (lax.axis_index(a) for a in ("seq_2", "seq_1", "seq_0"))
    place = jnp.stack([x, (x + 3) & 3, (x + 1) & 3, (x + 2) & 3, core, y, z]).astype(jnp.int32)
    w = w_in.reshape(2, 2048, 2 * LANES)

    def on_lanes(heads):
        return jnp.broadcast_to(heads[:, None], (HEADS, STRETCH))

    def params(which):
        return (
            in_gain[which].reshape(TP, 1, 512),
            w_dt[which].T.reshape(HEADS, TP, 512).transpose(1, 0, 2),
            jnp.concatenate([conv_x[which], conv_bc[which]], axis=1),
            on_lanes(dt_bias[which]),
            on_lanes(a_log[which]),
            on_lanes(d_skip[which]),
            out_gain[which].reshape(1, LANES),
        )

    starts = col_order.reshape(16, 64)[:, 0]
    slot = jnp.arange(512)
    columns = jnp.where(
        slot // 16 == lax.axis_index(SEQ), jnp.tile(starts % 512, 32), 0
    ).reshape(2, 256)
    columns = jnp.stack([columns[0] // 2, columns[0] % 2, columns[1] // 2, columns[1] % 2])
    columns = jnp.pad(columns.astype(f32), ((0, 4), (0, 0)))
    visit = jnp.arange(16)[:, None]
    along = jnp.arange(64)[None, :]
    row = jnp.where((starts >= 512)[:, None], 63 - along, along)
    take = ((row // 2) * 32 + (row % 2) * 16 + visit).reshape(1024)
    place, small, w, columns, take = lax.optimization_barrier(
        (place, [params(0), params(1)], w, columns, take)
    )
    large = (w, w_bc, w_out)

    row_result, columns = layer(0, tokens, first, place, small[0], large, columns, (w,))
    payload = given(columns, row_result)
    arrived = lax.all_to_all(payload, SEQ, 0, 0, tiled=True).reshape(1024, 512)
    own_rows = permuted(arrived, take)
    return layer(1, own_rows, with_halo(own_rows), place, small[1], large, columns, ())[0]


def solution(mesh):
    torus = Mesh(mesh.devices.reshape(4, 4, 2, mesh.shape["tp"]), ("seq_0", "seq_1", "seq_2", "tp"))
    return jax.shard_map(
        body,
        mesh=torus,
        in_specs=(
            P(SEQ, "tp"),
            P(SEQ),
            P(),
            P(None, None, None, "tp"),
            P(),
            P(None, None, "tp"),
            P(None, None, "tp"),
            P(),
            P(None, "tp"),
            P(None, "tp"),
            P(None, "tp"),
            P(None, "tp"),
            P(None, "tp", None),
        ),
        out_specs=P(SEQ, "tp"),
        check_vma=False,
    )
```

```python
import functools

import jax
import jax.numpy as jnp
from jax import lax
from jax.experimental import pallas as pl
from jax.experimental.pallas import tpu as pltpu
from jax.sharding import Mesh
from jax.sharding import PartitionSpec as P

HEAD_DIM = 64
STATE = 128
STRETCH = 128
HEADS = 8
LANES = 512
HALF = 256
HALO = 16
BLOCK = 256
MSG = 144
SEQ = ("seq_0", "seq_1", "seq_2")
TP = 4
epsilon = 1e-05
f32 = jnp.float32
bf16 = jnp.bfloat16
NT = (((1,), (1,)), ((), ()))
TN = (((0,), (0,)), ((), ()))
MIB = 2**20


def dot(a, b, dims=None):
    dims = dims or (((1,), (0,)), ((), ()))
    return lax.dot_general(a, b, dims, preferred_element_type=f32)


def silu(x):
    return x / (1.0 + jnp.exp(-x))


def softplus(x):
    return jnp.maximum(x, 0.0) + jnp.log1p(jnp.exp(-jnp.abs(x)))


def spread_heads(values, fan):
    high = values.astype(bf16)
    low = (values - high.astype(f32)).astype(bf16)
    return dot(jnp.concatenate([high, low], axis=0), fan, TN)


def packed(state, decay, columns):
    high = decay.astype(bf16).astype(f32)
    row = lax.broadcasted_iota(jnp.int32, (8, decay.shape[1]), 0)
    rest = jnp.where(row == 0, high, jnp.where(row == 1, decay - high, 0.0))
    return jnp.concatenate([state, columns, rest], axis=0)


def opened(msg):
    msg = msg[...].astype(f32)
    at = STATE + 8
    return msg[:STATE], msg[at : at + 1] + msg[at + 1 : at + 2]


def columns_in(msg):
    return msg[...].astype(f32)[STATE : STATE + 8]


def after(a, b):
    return b[0] + b[1] * a[0], a[1] * b[1]


def chosen(pred, a, b):
    return jnp.where(pred, a[0], b[0]), jnp.where(pred, a[1], b[1])


def nothing():
    return jnp.zeros((STATE, HALF), f32), jnp.ones((1, HALF), f32)


def head_fan():
    row = lax.broadcasted_iota(jnp.int32, (2 * HEADS, LANES), 0)
    lane = lax.broadcasted_iota(jnp.int32, (2 * HEADS, LANES), 1)
    return (row % HEADS == lane // HEAD_DIM).astype(bf16)


def entry_kernel(first, last, offset, rows, *refs):
    (order, own, left, right, opposite) = refs[:5]
    refs = refs[5:]
    columns = ()
    if last:
        columns, refs = refs[:1], refs[1:]
    if not first:
        tail_in, state_in, total_in, refs = *refs[:3], refs[3:]
    (gain, wv, wbcv, wdt, taps, dt_bias, a_log), refs = refs[:7], refs[7:]
    (z_out, xc_out, b_out, c_out, cum_out, step_out, ent_out, pri_out), refs = refs[:8], refs[8:]
    if last:
        (keep_out, send_out), refs = refs[:2], refs[2:]
        columns = columns[0]
    else:
        (tail_out, state_out, total_out), refs = refs[:3], refs[3:]
    nbuf, xbuf = refs

    fan = head_fan()
    k_pos = lax.broadcasted_iota(jnp.int32, (STRETCH, STRETCH), 0)
    q_pos = lax.broadcasted_iota(jnp.int32, (STRETCH, STRETCH), 1)
    upto = (k_pos <= q_pos).astype(f32)
    lane = lax.broadcasted_iota(jnp.int32, (HEADS, STRETCH), 1)
    rate = jnp.exp(a_log[:, 0:1])
    if first:
        state = jnp.zeros((STATE, LANES), f32)
        total = jnp.zeros((HEADS, 1), f32)
    else:
        state = state_in[...]
        total = total_in[:, 0:1]
        xbuf[0:HALO, :] = tail_in[...]
    for i in range(rows // BLOCK):
        span = pl.ds(i * BLOCK, BLOCK)
        above = pl.ds(offset + i * BLOCK, BLOCK)
        pieces = [r[above, :] for r in (own, left, right, opposite)]
        widen = [x.astype(f32) for x in pieces]
        square = sum(jnp.sum(x * x, axis=1, keepdims=True) for x in widen)
        scale = lax.rsqrt(square * (1.0 / 2048) + epsilon)
        for p in range(4):
            nbuf[HALO : HALO + BLOCK, p * 512 : (p + 1) * 512] = (
                widen[p] * scale * gain[order[p]]
            ).astype(bf16)
        if first and i == 0:
            widen = [r[0:HALO, :].astype(f32) for r in (own, left, right, opposite)]
            square = sum(jnp.sum(x * x, axis=1, keepdims=True) for x in widen)
            scale = lax.rsqrt(square * (1.0 / 2048) + epsilon)
            for p in range(4):
                nbuf[0:HALO, p * 512 : (p + 1) * 512] = (
                    widen[p] * scale * gain[order[p]]
                ).astype(bf16)
        low = 0 if first and i == 0 else HALO
        if low and i > 0:
            xbuf[0:HALO, :] = xbuf[BLOCK : BLOCK + HALO, :]
        normed = nbuf[low : HALO + BLOCK, :]
        xbuf[low : HALO + BLOCK, 0:LANES] = dot(normed, wv[:, 0:LANES]).astype(bf16).astype(f32)
        z_out[span, :] = dot(nbuf[HALO:, :], wv[:, LANES:]).astype(bf16)
        xbuf[low : HALO + BLOCK, LANES:] = dot(normed, wbcv[...]).astype(bf16).astype(f32)
        dt = sum(
            dot(wdt[order[p]], nbuf[HALO:, p * 512 : (p + 1) * 512], NT) for p in range(4)
        )
        mixed = jnp.zeros((BLOCK, LANES + 2 * STATE), f32)
        for k in range(4):
            mixed = mixed + taps[k : k + 1, :] * xbuf[pl.ds(HALO - 3 + k, BLOCK), :]
        mixed = silu(mixed)
        xc = mixed[:, 0:LANES]
        b = mixed[:, LANES : LANES + STATE].astype(bf16)
        xc_out[span, :] = xc.astype(bf16)
        b_out[span, :] = b
        c_out[span, :] = mixed[:, LANES + STATE :].astype(bf16)
        step = softplus(dt + dt_bias[:, 0:1])
        decay = -step * rate
        step_out[:, i * BLOCK : (i + 1) * BLOCK] = step
        cums, marks = [], jnp.zeros((HEADS, STRETCH), f32)
        for j in range(2):
            part = decay[:, j * STRETCH : (j + 1) * STRETCH]
            cum = lax.dot_general(
                part,
                upto,
                (((1,), (0,)), ((), ())),
                preferred_element_type=f32,
                precision=lax.Precision.HIGHEST,
            )
            cum_out[:, i * BLOCK + j * STRETCH : i * BLOCK + (j + 1) * STRETCH] = cum
            end = cum[:, STRETCH - 1 : STRETCH]
            marks = jnp.where(lane == j, end, jnp.where(lane == 2 + j, total, marks))
            total = total + end
            cums.append((cum, end))
        marks = jnp.where(lane == 4, total, marks)
        marks = spread_heads(jnp.exp(marks), fan)
        for j in range(2):
            cum, end = cums[j]
            here = slice(j * STRETCH, (j + 1) * STRETCH)
            weight = spread_heads(step[:, here] * jnp.exp(end - cum), fan)
            fresh = dot(b[here, :], (xc[here, :] * weight).astype(bf16), TN)
            ent_out[2 * i + j] = state
            pri_out[2 * i + j] = marks[2 + j : 3 + j, :]
            state = state * marks[j : j + 1, :] + fresh
    if last:
        decayed = marks[4:5, :]
        near = packed(state[:, 0:HALF], decayed[:, 0:HALF], columns[...])
        far = packed(state[:, HALF:], decayed[:, HALF:], columns[...])
        even = order[4] == 0
        keep_out[...] = jnp.where(even, near, far).astype(bf16)
        send_out[...] = jnp.where(even, far, near).astype(bf16)
    else:
        tail_out[...] = xbuf[BLOCK : BLOCK + HALO, :]
        state_out[...] = state
        total_out[...] = jnp.broadcast_to(total, (HEADS, STRETCH))


def stage_kernel(which, order, w, wbc, w_out, wbc_out, sems):
    copies = []
    for p in range(4):
        source = pl.ds(pl.multiple_of(order[p] * 512, 512), 512)
        target = pl.ds(p * 512, 512)
        copies.append(
            pltpu.make_async_copy(w.at[which, source, :], w_out.at[target, :], sems.at[0, p])
        )
        copies.append(
            pltpu.make_async_copy(wbc.at[which, source, :], wbc_out.at[target, :], sems.at[1, p])
        )
    for c in copies:
        c.start()
    for c in copies:
        c.wait()


def staged(which, order, w, wbc):
    return pl.pallas_call(
        functools.partial(stage_kernel, which),
        out_shape=[pltpu.VMEM((2048, 2 * LANES), bf16), pltpu.VMEM((2048, 2 * STATE), bf16)],
        in_specs=[smem(), in_hbm(), in_hbm()],
        out_specs=[vmem()] * 2,
        scratch_shapes=[pltpu.SemaphoreType.DMA((2, 4))],
        compiler_params=pltpu.CompilerParams(vmem_limit_bytes=2 * MIB),
        name="stage",
    )(order, kept_in_hbm(w), kept_in_hbm(wbc))


def stage_out_kernel(which, order, w, out, sems):
    copies = []
    for p in range(4):
        source = pl.ds(pl.multiple_of(order[(0, 2, 1, 3)[p]] * 512, 512), 512)
        copies.append(pltpu.make_async_copy(w.at[which, :, source], out.at[p], sems.at[p]))
    for c in copies:
        c.start()
    for c in copies:
        c.wait()


def staged_out(which, order, w):
    return pl.pallas_call(
        functools.partial(stage_out_kernel, which),
        out_shape=pltpu.VMEM((4, LANES, LANES), bf16),
        in_specs=[smem(), in_hbm()],
        out_specs=vmem(),
        scratch_shapes=[pltpu.SemaphoreType.DMA((4,))],
        compiler_params=pltpu.CompilerParams(vmem_limit_bytes=2 * MIB),
        name="stage_out",
    )(order, kept_in_hbm(w))


def vmem():
    return pl.BlockSpec(memory_space=pltpu.VMEM)


def smem():
    return pl.BlockSpec(memory_space=pltpu.SMEM)


def in_hbm():
    return pl.BlockSpec(memory_space=pltpu.HBM)


def kept_in_hbm(x):
    return pltpu.with_memory_space_constraint(x, pltpu.HBM)


def entry(order, pieces, offset, columns, carry, gain, w, wbc, wdt, taps, dt_bias, a_log, last):
    first = carry is None
    rows = BLOCK
    shape = jax.ShapeDtypeStruct
    outs = [
        pltpu.VMEM((rows, LANES), bf16),
        pltpu.VMEM((rows, LANES), bf16),
        pltpu.VMEM((rows, STATE), bf16),
        pltpu.VMEM((rows, STATE), bf16),
        pltpu.VMEM((HEADS, rows), f32),
        pltpu.VMEM((HEADS, rows), f32),
        pltpu.VMEM((rows // STRETCH, STATE, LANES), f32),
        pltpu.VMEM((rows // STRETCH, 1, LANES), f32),
    ]
    if last:
        outs += [shape((MSG, HALF), bf16)] * 2
    else:
        outs += [
            pltpu.VMEM((HALO, LANES + 2 * STATE), f32),
            pltpu.VMEM((STATE, LANES), f32),
            pltpu.VMEM((HEADS, STRETCH), f32),
        ]
    extra = [] if first else list(carry)
    operands = [order, *pieces, *([columns] if last else []), *extra, gain, w, wbc, wdt, taps, dt_bias, a_log]
    specs = [smem()] + [vmem()] * (len(operands) - 1)
    return pl.pallas_call(
        functools.partial(entry_kernel, first, last, offset, rows),
        out_shape=outs,
        in_specs=specs,
        out_specs=[vmem()] * len(outs),
        scratch_shapes=[
            pltpu.VMEM((HALO + BLOCK, 2048), bf16),
            pltpu.VMEM((HALO + BLOCK, LANES + 2 * STATE), f32),
        ],
        compiler_params=pltpu.CompilerParams(vmem_limit_bytes=8 * MIB),
        name="entry",
    )(*operands)


def inside_kernel(rows, xc, b, c, cum, step, skip, y_out):
    q_pos = lax.broadcasted_iota(jnp.int32, (STRETCH, STRETCH), 0)
    k_pos = lax.broadcasted_iota(jnp.int32, (STRETCH, STRETCH), 1)
    causal = k_pos <= q_pos
    low_half = k_pos < HEAD_DIM
    skips = spread_heads(skip[...], head_fan())[0:1, :]
    for j in range(rows // STRETCH):
        here = slice(j * STRETCH, (j + 1) * STRETCH)
        match = jnp.where(causal, dot(c[here, :], b[here, :], NT), 0.0)
        cum_rows = cum[:, here]
        step_rows = step[:, here]
        cum_cols = jnp.transpose(cum_rows)
        for pair in range(HEADS // 2):
            weights = []
            for h in (2 * pair, 2 * pair + 1):
                gap = jnp.minimum(cum_cols[:, h : h + 1] - cum_rows[h : h + 1, :], 0.0)
                weights.append((match * (jnp.exp(gap) * step_rows[h : h + 1, :])).astype(bf16))
            lanes = slice(pair * STRETCH, (pair + 1) * STRETCH)
            x = xc[here, lanes].astype(f32)
            stacked = jnp.concatenate(
                [jnp.where(low_half, x, 0.0), jnp.where(low_half, 0.0, x)], axis=0
            ).astype(bf16)
            y_out[here, lanes] = (
                dot(jnp.concatenate(weights, axis=1), stacked) + skips[:, lanes] * x
            )


def inside(xc, b, c, cum, step, skip):
    rows = xc.shape[0]
    return pl.pallas_call(
        functools.partial(inside_kernel, rows),
        out_shape=pltpu.VMEM((rows, LANES), f32),
        in_specs=[vmem()] * 6,
        out_specs=vmem(),
        compiler_params=pltpu.CompilerParams(vmem_limit_bytes=4 * MIB),
        name="inside",
    )(xc, b, c, cum, step, skip)


def exit_kernel(chunks, order, mine, other, gain, wv, *refs):
    parts = [refs[6 * i : 6 * i + 6] for i in range(chunks)]
    own, up, down, plus_a, minus_b = refs[6 * chunks :]
    split = chunks * BLOCK // 2
    outs = (((plus_a, 0), (up, split)), ((down, split), (minus_b, 0)), ((up, 0), (down, 0)))
    fan = head_fan()
    row = lax.broadcasted_iota(jnp.int32, (BLOCK, BLOCK), 0) // HEAD_DIM
    lane = lax.broadcasted_iota(jnp.int32, (BLOCK, BLOCK), 1) // HEAD_DIM
    same_head = (row == lane).astype(bf16)
    here, there = mine[...].astype(f32), other[...].astype(f32)
    even = order[4] == 0
    came = jnp.concatenate([jnp.where(even, here, there), jnp.where(even, there, here)], axis=1)
    for i in range(chunks):
        y, z, c, cum, ent, pri = parts[i]
        mixed = []
        for j in range(2):
            here = slice(j * STRETCH, (j + 1) * STRETCH)
            entering = (ent[j] + pri[j] * came).astype(bf16)
            carried = dot(c[here, :], entering) * spread_heads(jnp.exp(cum[:, here]), fan)
            gated = (y[here, :] + carried) * silu(z[here, :].astype(f32))
            square = (gated * gated).astype(bf16)
            sums = jnp.concatenate(
                [dot(square[:, 0:BLOCK], same_head), dot(square[:, BLOCK:], same_head)], axis=1
            )
            scale = lax.rsqrt(sums * (1.0 / HEAD_DIM) + epsilon)
            mixed.append((gated * scale * gain[...]).astype(bf16))
        mixed = jnp.concatenate(mixed, axis=0)
        own[i * BLOCK : (i + 1) * BLOCK, :] = dot(mixed, wv[0]).astype(bf16)
        for p in range(3):
            product = dot(mixed, wv[p + 1]).astype(bf16)
            for j in range(2):
                at = i * BLOCK + j * STRETCH
                out, base = outs[p][at // split]
                at = base + at % split
                out[at : at + STRETCH, :] = product[j * STRETCH : (j + 1) * STRETCH, :]


def leave(order, mine, other, gain, w, parts):
    rows = len(parts) * BLOCK
    shape = jax.ShapeDtypeStruct
    outs = [shape((rows, LANES), bf16)] * 3 + [shape((rows // 2, LANES), bf16)] * 2
    operands = [order, mine, other, gain, w, *(a for part in parts for a in part)]
    return pl.pallas_call(
        functools.partial(exit_kernel, len(parts)),
        out_shape=outs,
        in_specs=[smem()] + [vmem()] * (len(operands) - 1),
        out_specs=[vmem()] * len(outs),
        compiler_params=pltpu.CompilerParams(vmem_limit_bytes=6 * MIB),
        name="leave",
    )(*operands)


def small_call(kernel, name, outs, place, *operands):
    return pl.pallas_call(
        kernel,
        out_shape=outs,
        in_specs=[smem()] + [vmem()] * len(operands),
        out_specs=[vmem()] * len(outs),
        compiler_params=pltpu.CompilerParams(vmem_limit_bytes=2 * MIB),
        name=name,
    )(place, *operands)


def chip_kernel(place, keep, got, out):
    even = place[4] == 0
    mine, other = opened(keep), opened(got)
    both = after(chosen(even, mine, other), chosen(even, other, mine))
    out[...] = packed(*both, columns_in(keep) + columns_in(got)).astype(bf16)


def row_kernel(place, chip, one, two, three, row_out, before_out):
    y = place[5]
    ring = [opened(r) for r in (chip, one, two, three)]
    row, before = nothing(), nothing()
    for at in range(4):
        here = ring[0]
        for k in range(1, 4):
            here = chosen((y + 4 - at) % 4 == k, ring[k], here)
        before = chosen(at < y, after(before, here), before)
        row = after(row, here)
    columns = sum(columns_in(r) for r in (chip, one, two, three))
    row_out[...] = packed(*row, columns).astype(bf16)
    before_out[...] = packed(*before, columns)


def arrive_kernel(place, one, two, three, before, keep, got, mine_out, other_out, columns_out):
    even = place[4] == 0
    z = place[6]
    came = nothing()
    for k, r in ((3, three), (2, two), (1, one)):
        came = chosen(z >= k, after(came, opened(r)), came)
    first = after(came, opened(before))
    second = after(first, chosen(even, opened(keep), opened(got)))
    mine_out[...] = jnp.where(even, first[0], second[0]).astype(bf16)
    other_out[...] = jnp.where(even, second[0], first[0]).astype(bf16)
    columns_out[...] = sum(columns_in(r) for r in (before, one, two, three))


def give_kernel(columns, x, out):
    cell = lax.broadcasted_iota(jnp.int32, (512, HALF), 0)
    for part in range(2):
        wanted = 2.0 * columns[2 * part : 2 * part + 1, :] + columns[2 * part + 1 : 2 * part + 2, :]
        pick = (cell == wanted.astype(jnp.int32)).astype(bf16)
        for r in range(2):
            rows = dot(pick, x[r * 512 : (r + 1) * 512, :], TN).astype(bf16)
            out[part * 16 : (part + 1) * 16, r * 16 : (r + 1) * 16, :] = rows.reshape(16, 16, 512)


def given(columns, x):
    return pl.pallas_call(
        give_kernel,
        out_shape=jax.ShapeDtypeStruct((32, 32, 512), bf16),
        in_specs=[vmem()] * 2,
        out_specs=vmem(),
        compiler_params=pltpu.CompilerParams(vmem_limit_bytes=6 * MIB),
        name="give",
    )(columns, x)


def turned(by):
    return [(i, (i + by) % TP) for i in range(TP)]


def around(x, by):
    return lax.ppermute(x, "tp", turned(by))


def swapped(x):
    return lax.ppermute(x, "seq_2", [(0, 1), (1, 0)])


def arriving_state(place, keep, send, weights, beside, wrapped):
    shape = jax.ShapeDtypeStruct
    got = swapped(send)
    msg = shape((MSG, HALF), bf16)
    (chip,) = small_call(chip_kernel, "chip", [msg], place, keep, got)
    ring = [lax.ppermute(chip, "seq_1", turned(k)) for k in (1, 2, 3)]
    row, before = small_call(
        row_kernel,
        "row",
        [msg, shape((MSG, HALF), f32)],
        behind(place, weights),
        chip,
        *ring,
    )
    earlier = [
        lax.ppermute(row, "seq_0", turned(k)[: 4 if wrapped else 4 - k]) for k in (1, 2, 3)
    ]
    mine, other, columns = small_call(
        arrive_kernel,
        "arrive",
        [shape((STATE, HALF), bf16)] * 2 + [shape((8, HALF), f32)],
        behind(place, *beside),
        *earlier,
        before,
        keep,
        got,
    )
    return mine, swapped(other), columns


def behind(x, *done):
    return lax.optimization_barrier((x, *done))[0]


def with_halo(shard, count):
    pairs = [(i, i + 1) for i in range(lax.axis_size(SEQ) - 1)]
    return jnp.concatenate([lax.ppermute(shard[-HALO:], SEQ, pairs), shard[:count]], axis=0)


def layer(which, shard, first, place, params, large, columns, early=()):
    gain, wdt, taps, dt_bias, a_log, skip, out_gain = params
    w, wbc, w_out = large
    rows = [shard[i * BLOCK : (i + 1) * BLOCK] for i in range(shard.shape[0] // BLOCK)]
    wv, wbcv = staged(which, behind(place, first), w, wbc)
    carry, kept, gate = None, [], place

    def enter(i, pieces, offset=0):
        nonlocal carry, gate
        out = entry(
            gate, pieces, offset, columns, carry, gain, wv, wbcv, wdt, taps, dt_bias, a_log, i == 3
        )
        z, xc, b, c, cum, step, ent, pri = out[:8]
        carry = out[8:]
        y = inside(xc, b, c, cum, step, skip)
        kept.append((y, z, c, cum, ent, pri))
        if i < 2:
            gate = behind(place, y)

    if which == 0:
        own = [first, behind(rows[2], first), behind(rows[3], first)]
        left, right = [around(first, 1)], [around(first, -1)]
        right.append(around(own[1], -1))
        opposite = [around(behind(left[0], *early), 1)]
        right.append(around(own[2], -1))
        left.append(around(behind(rows[2], right[1]), 1))
        opposite.append(around(right[1], -1))
        pieces = (own[0], left[0], right[0], opposite[0])
        enter(0, pieces, HALO)
        left.append(around(behind(rows[3], carry[0]), 1))
        opposite.append(around(right[2], -1))
        enter(1, pieces, HALO + BLOCK)
        for i in (1, 2):
            enter(i + 1, (own[i], left[i], right[i], opposite[i]))
    else:
        own = [first, behind(rows[1], first), behind(rows[2], first, wbcv)]
        left, right = [around(x, 1) for x in own], [around(x, -1) for x in own]
        opposite = [around(left[0], 1)]
        enter(0, (own[0], left[0], right[0], opposite[0]), HALO)
        own.append(behind(rows[3], first, carry[0]))
        left.append(around(own[3], 1))
        right.append(around(own[3], -1))
        opposite.append(around(right[1], -1))
        enter(1, (own[1], left[1], right[1], opposite[1]))
        opposite.append(around(left[2], 1))
        opposite.append(around(behind(right[3], carry[0]), -1))
        for i in (2, 3):
            enter(i, (own[i], left[i], right[i], opposite[i]))
    wov = staged_out(which, behind(place, carry[0]), w_out)
    mine, other, columns = arriving_state(
        place, *carry, wov, [k[0] for k in kept], which == 0
    )
    results = []
    for low in (0, 2):
        own_part, up, down, plus_a, minus_b = leave(
            place, mine, other, out_gain, wov, kept[low : low + 2]
        )
        up, down = around(up, 1), around(down, -1)
        plus_a = around((plus_a.astype(f32) + up[:BLOCK].astype(f32)).astype(bf16), 1)
        minus_b = around((minus_b.astype(f32) + down[:BLOCK].astype(f32)).astype(bf16), -1)
        here = shard[low * BLOCK : (low + 2) * BLOCK].astype(f32) + own_part.astype(f32)
        results.append(here[:BLOCK] + plus_a.astype(f32) + down[BLOCK:].astype(f32))
        results.append(here[BLOCK:] + up[BLOCK:].astype(f32) + minus_b.astype(f32))
    return jnp.concatenate(results, axis=0).astype(bf16), columns


def permuted(x, source):
    pick = (source[:, None] == jnp.arange(x.shape[0])[None, :]).astype(bf16)
    return jnp.dot(pick, x, preferred_element_type=f32).astype(bf16)


def body(
    tokens,
    col_order,
    in_gain,
    w_in,
    w_bc,
    w_dt,
    conv_x,
    conv_bc,
    dt_bias,
    a_log,
    d_skip,
    out_gain,
    w_out,
):
    first = with_halo(tokens, 2 * BLOCK)
    arguments = (in_gain, w_in, w_dt, conv_x, conv_bc, dt_bias, a_log, d_skip, out_gain, col_order)
    in_gain, w_in, w_dt, conv_x, conv_bc, dt_bias, a_log, d_skip, out_gain, col_order = behind(
        arguments, first
    )
    x = lax.axis_index("tp")
    core, y, z = (lax.axis_index(a) for a in ("seq_2", "seq_1", "seq_0"))
    place = jnp.stack([x, (x + 3) & 3, (x + 1) & 3, (x + 2) & 3, core, y, z]).astype(jnp.int32)
    w = w_in.reshape(2, 2048, 2 * LANES)

    def on_lanes(heads):
        return jnp.broadcast_to(heads[:, None], (HEADS, STRETCH))

    def params(which):
        return (
            in_gain[which].reshape(TP, 1, 512),
            w_dt[which].T.reshape(HEADS, TP, 512).transpose(1, 0, 2),
            jnp.concatenate([conv_x[which], conv_bc[which]], axis=1),
            on_lanes(dt_bias[which]),
            on_lanes(a_log[which]),
            on_lanes(d_skip[which]),
            out_gain[which].reshape(1, LANES),
        )

    starts = col_order.reshape(16, 64)[:, 0]
    slot = jnp.arange(512)
    columns = jnp.where(
        slot // 16 == lax.axis_index(SEQ), jnp.tile(starts % 512, 32), 0
    ).reshape(2, 256)
    columns = jnp.stack([columns[0] // 2, columns[0] % 2, columns[1] // 2, columns[1] % 2])
    columns = jnp.pad(columns.astype(f32), ((0, 4), (0, 0)))
    visit = jnp.arange(16)[:, None]
    along = jnp.arange(64)[None, :]
    row = jnp.where((starts >= 512)[:, None], 63 - along, along)
    take = ((row // 2) * 32 + (row % 2) * 16 + visit).reshape(1024)
    place, small, w, columns, take = lax.optimization_barrier(
        (place, [params(0), params(1)], w, columns, take)
    )
    large = (w, w_bc, w_out)

    row_result, columns = layer(0, tokens, first, place, small[0], large, columns, (w,))
    payload = given(columns, row_result)
    arrived = lax.all_to_all(payload, SEQ, 0, 0, tiled=True).reshape(1024, 512)
    own_rows = permuted(arrived, take)
    return layer(1, own_rows, with_halo(own_rows, BLOCK), place, small[1], large, columns)[0]


def solution(mesh):
    torus = Mesh(mesh.devices.reshape(4, 4, 2, mesh.shape["tp"]), ("seq_0", "seq_1", "seq_2", "tp"))
    return jax.shard_map(
        body,
        mesh=torus,
        in_specs=(
            P(SEQ, "tp"),
            P(SEQ),
            P(),
            P(None, None, None, "tp"),
            P(),
            P(None, None, "tp"),
            P(None, None, "tp"),
            P(),
            P(None, "tp"),
            P(None, "tp"),
            P(None, "tp"),
            P(None, "tp"),
            P(None, "tp", None),
        ),
        out_specs=P(SEQ, "tp"),
        check_vma=False,
    )
```

```python
import functools

import jax
import jax.numpy as jnp
from jax import lax
from jax.experimental import pallas as pl
from jax.experimental.pallas import tpu as pltpu
from jax.sharding import Mesh
from jax.sharding import PartitionSpec as P

HEAD_DIM = 64
STATE = 128
STRETCH = 128
HEADS = 8
LANES = 512
HALF = 256
HALO = 16
BLOCK = 256
MSG = 144
SEQ = ("seq_0", "seq_1", "seq_2")
TP = 4
epsilon = 1e-05
f32 = jnp.float32
bf16 = jnp.bfloat16
NT = (((1,), (1,)), ((), ()))
TN = (((0,), (0,)), ((), ()))
MIB = 2**20


def dot(a, b, dims=None):
    dims = dims or (((1,), (0,)), ((), ()))
    return lax.dot_general(a, b, dims, preferred_element_type=f32)


def silu(x):
    return x / (1.0 + jnp.exp(-x))


def softplus(x):
    return jnp.maximum(x, 0.0) + jnp.log1p(jnp.exp(-jnp.abs(x)))


def spread_heads(values, fan):
    high = values.astype(bf16)
    low = (values - high.astype(f32)).astype(bf16)
    return dot(jnp.concatenate([high, low], axis=0), fan, TN)


def packed(state, decay, columns):
    high = decay.astype(bf16).astype(f32)
    row = lax.broadcasted_iota(jnp.int32, (8, decay.shape[1]), 0)
    rest = jnp.where(row == 0, high, jnp.where(row == 1, decay - high, 0.0))
    return jnp.concatenate([state, columns, rest], axis=0)


def opened(msg):
    msg = msg[...].astype(f32)
    at = STATE + 8
    return msg[:STATE], msg[at : at + 1] + msg[at + 1 : at + 2]


def columns_in(msg):
    return msg[...].astype(f32)[STATE : STATE + 8]


def after(a, b):
    return b[0] + b[1] * a[0], a[1] * b[1]


def chosen(pred, a, b):
    return jnp.where(pred, a[0], b[0]), jnp.where(pred, a[1], b[1])


def nothing():
    return jnp.zeros((STATE, HALF), f32), jnp.ones((1, HALF), f32)


def head_fan():
    row = lax.broadcasted_iota(jnp.int32, (2 * HEADS, LANES), 0)
    lane = lax.broadcasted_iota(jnp.int32, (2 * HEADS, LANES), 1)
    return (row % HEADS == lane // HEAD_DIM).astype(bf16)


def entry_kernel(first, last, offset, rows, *refs):
    (order, own, left, right, opposite) = refs[:5]
    refs = refs[5:]
    columns = ()
    if last:
        columns, refs = refs[:1], refs[1:]
    if not first:
        tail_in, state_in, total_in, refs = *refs[:3], refs[3:]
    (gain, wv, wbcv, wdt, taps, dt_bias, a_log), refs = refs[:7], refs[7:]
    (z_out, xc_out, b_out, c_out, cum_out, step_out, ent_out, pri_out), refs = refs[:8], refs[8:]
    if last:
        (keep_out, send_out), refs = refs[:2], refs[2:]
        columns = columns[0]
    else:
        (tail_out, state_out, total_out), refs = refs[:3], refs[3:]
    nbuf, xbuf = refs

    fan = head_fan()
    k_pos = lax.broadcasted_iota(jnp.int32, (STRETCH, STRETCH), 0)
    q_pos = lax.broadcasted_iota(jnp.int32, (STRETCH, STRETCH), 1)
    upto = (k_pos <= q_pos).astype(f32)
    lane = lax.broadcasted_iota(jnp.int32, (HEADS, STRETCH), 1)
    rate = jnp.exp(a_log[:, 0:1])
    if first:
        state = jnp.zeros((STATE, LANES), f32)
        total = jnp.zeros((HEADS, 1), f32)
    else:
        state = state_in[...]
        total = total_in[:, 0:1]
        xbuf[0:HALO, :] = tail_in[...]
    for i in range(rows // BLOCK):
        span = pl.ds(i * BLOCK, BLOCK)
        above = pl.ds(offset + i * BLOCK, BLOCK)
        pieces = [r[above, :] for r in (own, left, right, opposite)]
        widen = [x.astype(f32) for x in pieces]
        square = sum(jnp.sum(x * x, axis=1, keepdims=True) for x in widen)
        scale = lax.rsqrt(square * (1.0 / 2048) + epsilon)
        for p in range(4):
            nbuf[HALO : HALO + BLOCK, p * 512 : (p + 1) * 512] = (
                widen[p] * scale * gain[order[p]]
            ).astype(bf16)
        if first and i == 0:
            widen = [r[0:HALO, :].astype(f32) for r in (own, left, right, opposite)]
            square = sum(jnp.sum(x * x, axis=1, keepdims=True) for x in widen)
            scale = lax.rsqrt(square * (1.0 / 2048) + epsilon)
            for p in range(4):
                nbuf[0:HALO, p * 512 : (p + 1) * 512] = (
                    widen[p] * scale * gain[order[p]]
                ).astype(bf16)
        low = 0 if first and i == 0 else HALO
        if low and i > 0:
            xbuf[0:HALO, :] = xbuf[BLOCK : BLOCK + HALO, :]
        normed = nbuf[low : HALO + BLOCK, :]
        xbuf[low : HALO + BLOCK, 0:LANES] = dot(normed, wv[:, 0:LANES]).astype(bf16).astype(f32)
        z_out[span, :] = dot(nbuf[HALO:, :], wv[:, LANES:]).astype(bf16)
        xbuf[low : HALO + BLOCK, LANES:] = dot(normed, wbcv[...]).astype(bf16).astype(f32)
        dt = sum(
            dot(wdt[order[p]], nbuf[HALO:, p * 512 : (p + 1) * 512], NT) for p in range(4)
        )
        mixed = jnp.zeros((BLOCK, LANES + 2 * STATE), f32)
        for k in range(4):
            mixed = mixed + taps[k : k + 1, :] * xbuf[pl.ds(HALO - 3 + k, BLOCK), :]
        mixed = silu(mixed)
        xc = mixed[:, 0:LANES]
        b = mixed[:, LANES : LANES + STATE].astype(bf16)
        xc_out[span, :] = xc.astype(bf16)
        b_out[span, :] = b
        c_out[span, :] = mixed[:, LANES + STATE :].astype(bf16)
        step = softplus(dt + dt_bias[:, 0:1])
        decay = -step * rate
        step_out[:, i * BLOCK : (i + 1) * BLOCK] = step
        cums, marks = [], jnp.zeros((HEADS, STRETCH), f32)
        for j in range(2):
            part = decay[:, j * STRETCH : (j + 1) * STRETCH]
            cum = lax.dot_general(
                part,
                upto,
                (((1,), (0,)), ((), ())),
                preferred_element_type=f32,
                precision=lax.Precision.HIGHEST,
            )
            cum_out[:, i * BLOCK + j * STRETCH : i * BLOCK + (j + 1) * STRETCH] = cum
            end = cum[:, STRETCH - 1 : STRETCH]
            marks = jnp.where(lane == j, end, jnp.where(lane == 2 + j, total, marks))
            total = total + end
            cums.append((cum, end))
        marks = jnp.where(lane == 4, total, marks)
        marks = spread_heads(jnp.exp(marks), fan)
        for j in range(2):
            cum, end = cums[j]
            here = slice(j * STRETCH, (j + 1) * STRETCH)
            weight = spread_heads(step[:, here] * jnp.exp(end - cum), fan)
            fresh = dot(b[here, :], (xc[here, :] * weight).astype(bf16), TN)
            ent_out[2 * i + j] = state
            pri_out[2 * i + j] = marks[2 + j : 3 + j, :]
            state = state * marks[j : j + 1, :] + fresh
    if last:
        decayed = marks[4:5, :]
        near = packed(state[:, 0:HALF], decayed[:, 0:HALF], columns[...])
        far = packed(state[:, HALF:], decayed[:, HALF:], columns[...])
        even = order[4] == 0
        keep_out[...] = jnp.where(even, near, far).astype(bf16)
        send_out[...] = jnp.where(even, far, near).astype(bf16)
    else:
        tail_out[...] = xbuf[BLOCK : BLOCK + HALO, :]
        state_out[...] = state
        total_out[...] = jnp.broadcast_to(total, (HEADS, STRETCH))


def stage_kernel(which, order, w, wbc, w_out, wbc_out, sems):
    copies = []
    for p in range(4):
        source = pl.ds(pl.multiple_of(order[p] * 512, 512), 512)
        target = pl.ds(p * 512, 512)
        copies.append(
            pltpu.make_async_copy(w.at[which, source, :], w_out.at[target, :], sems.at[0, p])
        )
        copies.append(
            pltpu.make_async_copy(wbc.at[which, source, :], wbc_out.at[target, :], sems.at[1, p])
        )
    for c in copies:
        c.start()
    for c in copies:
        c.wait()


def staged(which, order, w, wbc):
    return pl.pallas_call(
        functools.partial(stage_kernel, which),
        out_shape=[pltpu.VMEM((2048, 2 * LANES), bf16), pltpu.VMEM((2048, 2 * STATE), bf16)],
        in_specs=[smem(), in_hbm(), in_hbm()],
        out_specs=[vmem()] * 2,
        scratch_shapes=[pltpu.SemaphoreType.DMA((2, 4))],
        compiler_params=pltpu.CompilerParams(vmem_limit_bytes=2 * MIB),
        name="stage",
    )(order, kept_in_hbm(w), kept_in_hbm(wbc))


def stage_out_kernel(which, order, w, out, sems):
    copies = []
    for p in range(4):
        source = pl.ds(pl.multiple_of(order[(0, 2, 1, 3)[p]] * 512, 512), 512)
        copies.append(pltpu.make_async_copy(w.at[which, :, source], out.at[p], sems.at[p]))
    for c in copies:
        c.start()
    for c in copies:
        c.wait()


def staged_out(which, order, w):
    return pl.pallas_call(
        functools.partial(stage_out_kernel, which),
        out_shape=pltpu.VMEM((4, LANES, LANES), bf16),
        in_specs=[smem(), in_hbm()],
        out_specs=vmem(),
        scratch_shapes=[pltpu.SemaphoreType.DMA((4,))],
        compiler_params=pltpu.CompilerParams(vmem_limit_bytes=2 * MIB),
        name="stage_out",
    )(order, kept_in_hbm(w))


def vmem():
    return pl.BlockSpec(memory_space=pltpu.VMEM)


def smem():
    return pl.BlockSpec(memory_space=pltpu.SMEM)


def in_hbm():
    return pl.BlockSpec(memory_space=pltpu.HBM)


def kept_in_hbm(x):
    return pltpu.with_memory_space_constraint(x, pltpu.HBM)


def entry(order, pieces, offset, columns, carry, gain, w, wbc, wdt, taps, dt_bias, a_log, last):
    first = carry is None
    rows = BLOCK
    shape = jax.ShapeDtypeStruct
    outs = [
        pltpu.VMEM((rows, LANES), bf16),
        pltpu.VMEM((rows, LANES), bf16),
        pltpu.VMEM((rows, STATE), bf16),
        pltpu.VMEM((rows, STATE), bf16),
        pltpu.VMEM((HEADS, rows), f32),
        pltpu.VMEM((HEADS, rows), f32),
        pltpu.VMEM((rows // STRETCH, STATE, LANES), f32),
        pltpu.VMEM((rows // STRETCH, 1, LANES), f32),
    ]
    if last:
        outs += [shape((MSG, HALF), bf16)] * 2
    else:
        outs += [
            pltpu.VMEM((HALO, LANES + 2 * STATE), f32),
            pltpu.VMEM((STATE, LANES), f32),
            pltpu.VMEM((HEADS, STRETCH), f32),
        ]
    extra = [] if first else list(carry)
    operands = [order, *pieces, *([columns] if last else []), *extra, gain, w, wbc, wdt, taps, dt_bias, a_log]
    specs = [smem()] + [vmem()] * (len(operands) - 1)
    return pl.pallas_call(
        functools.partial(entry_kernel, first, last, offset, rows),
        out_shape=outs,
        in_specs=specs,
        out_specs=[vmem()] * len(outs),
        scratch_shapes=[
            pltpu.VMEM((HALO + BLOCK, 2048), bf16),
            pltpu.VMEM((HALO + BLOCK, LANES + 2 * STATE), f32),
        ],
        compiler_params=pltpu.CompilerParams(vmem_limit_bytes=8 * MIB),
        name="entry",
    )(*operands)


def inside_kernel(rows, xc, b, c, cum, step, skip, y_out):
    q_pos = lax.broadcasted_iota(jnp.int32, (STRETCH, STRETCH), 0)
    k_pos = lax.broadcasted_iota(jnp.int32, (STRETCH, STRETCH), 1)
    causal = k_pos <= q_pos
    low_half = k_pos < HEAD_DIM
    skips = spread_heads(skip[...], head_fan())[0:1, :]
    for j in range(rows // STRETCH):
        here = slice(j * STRETCH, (j + 1) * STRETCH)
        match = jnp.where(causal, dot(c[here, :], b[here, :], NT), 0.0)
        cum_rows = cum[:, here]
        step_rows = step[:, here]
        cum_cols = jnp.transpose(cum_rows)
        for pair in range(HEADS // 2):
            weights = []
            for h in (2 * pair, 2 * pair + 1):
                gap = jnp.minimum(cum_cols[:, h : h + 1] - cum_rows[h : h + 1, :], 0.0)
                weights.append((match * (jnp.exp(gap) * step_rows[h : h + 1, :])).astype(bf16))
            lanes = slice(pair * STRETCH, (pair + 1) * STRETCH)
            x = xc[here, lanes].astype(f32)
            stacked = jnp.concatenate(
                [jnp.where(low_half, x, 0.0), jnp.where(low_half, 0.0, x)], axis=0
            ).astype(bf16)
            y_out[here, lanes] = (
                dot(jnp.concatenate(weights, axis=1), stacked) + skips[:, lanes] * x
            )


def inside(xc, b, c, cum, step, skip):
    rows = xc.shape[0]
    return pl.pallas_call(
        functools.partial(inside_kernel, rows),
        out_shape=pltpu.VMEM((rows, LANES), f32),
        in_specs=[vmem()] * 6,
        out_specs=vmem(),
        compiler_params=pltpu.CompilerParams(vmem_limit_bytes=4 * MIB),
        name="inside",
    )(xc, b, c, cum, step, skip)


def exit_kernel(chunks, order, mine, other, gain, wv, *refs):
    parts = [refs[6 * i : 6 * i + 6] for i in range(chunks)]
    own, up, down, plus_a, minus_b = refs[6 * chunks :]
    split = chunks * BLOCK // 2
    outs = (((plus_a, 0), (up, split)), ((down, split), (minus_b, 0)), ((up, 0), (down, 0)))
    fan = head_fan()
    row = lax.broadcasted_iota(jnp.int32, (BLOCK, BLOCK), 0) // HEAD_DIM
    lane = lax.broadcasted_iota(jnp.int32, (BLOCK, BLOCK), 1) // HEAD_DIM
    same_head = (row == lane).astype(bf16)
    here, there = mine[...].astype(f32), other[...].astype(f32)
    even = order[4] == 0
    came = jnp.concatenate([jnp.where(even, here, there), jnp.where(even, there, here)], axis=1)
    for i in range(chunks):
        y, z, c, cum, ent, pri = parts[i]
        mixed = []
        for j in range(2):
            here = slice(j * STRETCH, (j + 1) * STRETCH)
            entering = (ent[j] + pri[j] * came).astype(bf16)
            carried = dot(c[here, :], entering) * spread_heads(jnp.exp(cum[:, here]), fan)
            gated = (y[here, :] + carried) * silu(z[here, :].astype(f32))
            square = (gated * gated).astype(bf16)
            sums = jnp.concatenate(
                [dot(square[:, 0:BLOCK], same_head), dot(square[:, BLOCK:], same_head)], axis=1
            )
            scale = lax.rsqrt(sums * (1.0 / HEAD_DIM) + epsilon)
            mixed.append((gated * scale * gain[...]).astype(bf16))
        mixed = jnp.concatenate(mixed, axis=0)
        own[i * BLOCK : (i + 1) * BLOCK, :] = dot(mixed, wv[0]).astype(bf16)
        for p in range(3):
            product = dot(mixed, wv[p + 1]).astype(bf16)
            for j in range(2):
                at = i * BLOCK + j * STRETCH
                out, base = outs[p][at // split]
                at = base + at % split
                out[at : at + STRETCH, :] = product[j * STRETCH : (j + 1) * STRETCH, :]


def leave(order, mine, other, gain, w, parts):
    rows = len(parts) * BLOCK
    shape = jax.ShapeDtypeStruct
    outs = [shape((rows, LANES), bf16)] * 3 + [shape((rows // 2, LANES), bf16)] * 2
    operands = [order, mine, other, gain, w, *(a for part in parts for a in part)]
    return pl.pallas_call(
        functools.partial(exit_kernel, len(parts)),
        out_shape=outs,
        in_specs=[smem()] + [vmem()] * (len(operands) - 1),
        out_specs=[vmem()] * len(outs),
        compiler_params=pltpu.CompilerParams(vmem_limit_bytes=6 * MIB),
        name="leave",
    )(*operands)


def small_call(kernel, name, outs, place, *operands):
    return pl.pallas_call(
        kernel,
        out_shape=outs,
        in_specs=[smem()] + [vmem()] * len(operands),
        out_specs=[vmem()] * len(outs),
        compiler_params=pltpu.CompilerParams(vmem_limit_bytes=2 * MIB),
        name=name,
    )(place, *operands)


def chip_kernel(place, keep, got, out):
    even = place[4] == 0
    mine, other = opened(keep), opened(got)
    both = after(chosen(even, mine, other), chosen(even, other, mine))
    out[...] = packed(*both, columns_in(keep) + columns_in(got)).astype(bf16)


def row_kernel(place, chip, one, two, three, row_out, before_out):
    y = place[5]
    ring = [opened(r) for r in (chip, one, two, three)]
    row, before = nothing(), nothing()
    for at in range(4):
        here = ring[0]
        for k in range(1, 4):
            here = chosen((y + 4 - at) % 4 == k, ring[k], here)
        before = chosen(at < y, after(before, here), before)
        row = after(row, here)
    columns = sum(columns_in(r) for r in (chip, one, two, three))
    row_out[...] = packed(*row, columns).astype(bf16)
    before_out[...] = packed(*before, columns)


def arrive_kernel(place, one, two, three, before, keep, got, mine_out, other_out, columns_out):
    even = place[4] == 0
    z = place[6]
    came = nothing()
    for k, r in ((3, three), (2, two), (1, one)):
        came = chosen(z >= k, after(came, opened(r)), came)
    first = after(came, opened(before))
    second = after(first, chosen(even, opened(keep), opened(got)))
    mine_out[...] = jnp.where(even, first[0], second[0]).astype(bf16)
    other_out[...] = jnp.where(even, second[0], first[0]).astype(bf16)
    columns_out[...] = sum(columns_in(r) for r in (before, one, two, three))


def give_kernel(columns, x, out):
    cell = lax.broadcasted_iota(jnp.int32, (512, HALF), 0)
    for part in range(2):
        wanted = 2.0 * columns[2 * part : 2 * part + 1, :] + columns[2 * part + 1 : 2 * part + 2, :]
        pick = (cell == wanted.astype(jnp.int32)).astype(bf16)
        for r in range(2):
            rows = dot(pick, x[r * 512 : (r + 1) * 512, :], TN).astype(bf16)
            out[part * 16 : (part + 1) * 16, r * 16 : (r + 1) * 16, :] = rows.reshape(16, 16, 512)


def given(columns, x):
    return pl.pallas_call(
        give_kernel,
        out_shape=jax.ShapeDtypeStruct((32, 32, 512), bf16),
        in_specs=[vmem()] * 2,
        out_specs=vmem(),
        compiler_params=pltpu.CompilerParams(vmem_limit_bytes=6 * MIB),
        name="give",
    )(columns, x)


def turned(by):
    return [(i, (i + by) % TP) for i in range(TP)]


def around(x, by):
    return lax.ppermute(x, "tp", turned(by))


def swapped(x):
    return lax.ppermute(x, "seq_2", [(0, 1), (1, 0)])


def arriving_state(place, keep, send, weights, beside, wrapped):
    shape = jax.ShapeDtypeStruct
    got = swapped(send)
    msg = shape((MSG, HALF), bf16)
    (chip,) = small_call(chip_kernel, "chip", [msg], place, keep, got)
    ring = [lax.ppermute(chip, "seq_1", turned(k)) for k in (1, 2, 3)]
    row, before = small_call(
        row_kernel,
        "row",
        [msg, shape((MSG, HALF), f32)],
        behind(place, weights),
        chip,
        *ring,
    )
    earlier = [
        lax.ppermute(row, "seq_0", turned(k)[: 4 if wrapped else 4 - k]) for k in (1, 2, 3)
    ]
    mine, other, columns = small_call(
        arrive_kernel,
        "arrive",
        [shape((STATE, HALF), bf16)] * 2 + [shape((8, HALF), f32)],
        behind(place, *beside),
        *earlier,
        before,
        keep,
        got,
    )
    return mine, swapped(other), columns


def behind(x, *done):
    return lax.optimization_barrier((x, *done))[0]


def with_halo(shard, count):
    pairs = [(i, i + 1) for i in range(lax.axis_size(SEQ) - 1)]
    return jnp.concatenate([lax.ppermute(shard[-HALO:], SEQ, pairs), shard[:count]], axis=0)


def layer(which, shard, first, place, params, large, columns, early=()):
    gain, wdt, taps, dt_bias, a_log, skip, out_gain = params
    w, wbc, w_out = large
    rows = [shard[i * BLOCK : (i + 1) * BLOCK] for i in range(shard.shape[0] // BLOCK)]
    wv, wbcv = staged(which, behind(place, first), w, wbc)
    carry, kept, gate = None, [], place

    def enter(i, pieces, offset=0):
        nonlocal carry, gate
        out = entry(
            gate, pieces, offset, columns, carry, gain, wv, wbcv, wdt, taps, dt_bias, a_log, i == 3
        )
        z, xc, b, c, cum, step, ent, pri = out[:8]
        carry = out[8:]
        y = inside(xc, b, c, cum, step, skip)
        kept.append((y, z, c, cum, ent, pri))
        if i < 2:
            gate = behind(place, y)

    if which == 0:
        own = [first, rows[2], rows[3]]
        left, right = [around(rows[2], 1)], [around(rows[2], -1)]
        left.insert(0, around(first, 1))
        right.insert(0, around(first, -1))
        opposite = [around(behind(left[0], *early), 1), around(right[1], -1)]
        right.append(around(behind(rows[3], right[0]), -1))
        left.append(around(behind(rows[3], right[2]), 1))
        opposite.append(around(right[2], -1))
        pieces = (own[0], left[0], right[0], opposite[0])
        enter(0, pieces, HALO)
        enter(1, pieces, HALO + BLOCK)
        for i in (1, 2):
            enter(i + 1, (own[i], left[i], right[i], opposite[i]))
    else:
        own = [first, rows[1], behind(rows[2], first, wbcv)]
        left, right = [around(x, 1) for x in own], [around(x, -1) for x in own]
        opposite = [around(left[0], 1)]
        enter(0, (own[0], left[0], right[0], opposite[0]), HALO)
        own.append(behind(rows[3], first, carry[0]))
        left.append(around(own[3], 1))
        right.append(around(own[3], -1))
        opposite.append(around(right[1], -1))
        enter(1, (own[1], left[1], right[1], opposite[1]))
        opposite.append(around(left[2], 1))
        opposite.append(around(behind(right[3], carry[0]), -1))
        for i in (2, 3):
            enter(i, (own[i], left[i], right[i], opposite[i]))
    wov = staged_out(which, behind(place, carry[0]), w_out)
    mine, other, columns = arriving_state(
        place, *carry, wov, [k[0] for k in kept], which == 0
    )
    results = []
    for low in (0, 2):
        own_part, up, down, plus_a, minus_b = leave(
            place, mine, other, out_gain, wov, kept[low : low + 2]
        )
        up, down = around(up, 1), around(down, -1)
        plus_a = around((plus_a.astype(f32) + up[:BLOCK].astype(f32)).astype(bf16), 1)
        minus_b = around((minus_b.astype(f32) + down[:BLOCK].astype(f32)).astype(bf16), -1)
        here = shard[low * BLOCK : (low + 2) * BLOCK].astype(f32) + own_part.astype(f32)
        results.append(here[:BLOCK] + plus_a.astype(f32) + down[BLOCK:].astype(f32))
        results.append(here[BLOCK:] + up[BLOCK:].astype(f32) + minus_b.astype(f32))
    return jnp.concatenate(results, axis=0).astype(bf16), columns


def permuted(x, source):
    pick = (source[:, None] == jnp.arange(x.shape[0])[None, :]).astype(bf16)
    return jnp.dot(pick, x, preferred_element_type=f32).astype(bf16)


def body(
    tokens,
    col_order,
    in_gain,
    w_in,
    w_bc,
    w_dt,
    conv_x,
    conv_bc,
    dt_bias,
    a_log,
    d_skip,
    out_gain,
    w_out,
):
    first = with_halo(tokens, 2 * BLOCK)
    arguments = (in_gain, w_in, w_dt, conv_x, conv_bc, dt_bias, a_log, d_skip, out_gain, col_order)
    in_gain, w_in, w_dt, conv_x, conv_bc, dt_bias, a_log, d_skip, out_gain, col_order = behind(
        arguments, first
    )
    x = lax.axis_index("tp")
    core, y, z = (lax.axis_index(a) for a in ("seq_2", "seq_1", "seq_0"))
    place = jnp.stack([x, (x + 3) & 3, (x + 1) & 3, (x + 2) & 3, core, y, z]).astype(jnp.int32)
    w = w_in.reshape(2, 2048, 2 * LANES)

    def on_lanes(heads):
        return jnp.broadcast_to(heads[:, None], (HEADS, STRETCH))

    def params(which):
        return (
            in_gain[which].reshape(TP, 1, 512),
            w_dt[which].T.reshape(HEADS, TP, 512).transpose(1, 0, 2),
            jnp.concatenate([conv_x[which], conv_bc[which]], axis=1),
            on_lanes(dt_bias[which]),
            on_lanes(a_log[which]),
            on_lanes(d_skip[which]),
            out_gain[which].reshape(1, LANES),
        )

    starts = col_order.reshape(16, 64)[:, 0]
    slot = jnp.arange(512)
    columns = jnp.where(
        slot // 16 == lax.axis_index(SEQ), jnp.tile(starts % 512, 32), 0
    ).reshape(2, 256)
    columns = jnp.stack([columns[0] // 2, columns[0] % 2, columns[1] // 2, columns[1] % 2])
    columns = jnp.pad(columns.astype(f32), ((0, 4), (0, 0)))
    visit = jnp.arange(16)[:, None]
    along = jnp.arange(64)[None, :]
    row = jnp.where((starts >= 512)[:, None], 63 - along, along)
    take = ((row // 2) * 32 + (row % 2) * 16 + visit).reshape(1024)
    place, small, w, columns, take = lax.optimization_barrier(
        (place, [params(0), params(1)], w, columns, take)
    )
    large = (w, w_bc, w_out)

    row_result, columns = layer(0, tokens, first, place, small[0], large, columns, (w,))
    payload = given(columns, row_result)
    arrived = lax.all_to_all(payload, SEQ, 0, 0, tiled=True).reshape(1024, 512)
    own_rows = permuted(arrived, take)
    return layer(1, own_rows, with_halo(own_rows, BLOCK), place, small[1], large, columns)[0]


def solution(mesh):
    torus = Mesh(mesh.devices.reshape(4, 4, 2, mesh.shape["tp"]), ("seq_0", "seq_1", "seq_2", "tp"))
    return jax.shard_map(
        body,
        mesh=torus,
        in_specs=(
            P(SEQ, "tp"),
            P(SEQ),
            P(),
            P(None, None, None, "tp"),
            P(),
            P(None, None, "tp"),
            P(None, None, "tp"),
            P(),
            P(None, "tp"),
            P(None, "tp"),
            P(None, "tp"),
            P(None, "tp"),
            P(None, "tp", None),
        ),
        out_specs=P(SEQ, "tp"),
        check_vma=False,
    )
```

```python
import functools

import jax
import jax.numpy as jnp
from jax import lax
from jax.experimental import pallas as pl
from jax.experimental.pallas import tpu as pltpu
from jax.sharding import Mesh
from jax.sharding import PartitionSpec as P

HEAD_DIM = 64
STATE = 128
STRETCH = 128
HEADS = 8
LANES = 512
HALF = 256
HALO = 16
BLOCK = 256
MSG = 144
SEQ = ("seq_0", "seq_1", "seq_2")
TP = 4
epsilon = 1e-05
f32 = jnp.float32
bf16 = jnp.bfloat16
NT = (((1,), (1,)), ((), ()))
TN = (((0,), (0,)), ((), ()))
MIB = 2**20


def dot(a, b, dims=None):
    dims = dims or (((1,), (0,)), ((), ()))
    return lax.dot_general(a, b, dims, preferred_element_type=f32)


def silu(x):
    return x / (1.0 + jnp.exp(-x))


def softplus(x):
    return jnp.maximum(x, 0.0) + jnp.log1p(jnp.exp(-jnp.abs(x)))


def spread_heads(values, fan):
    high = values.astype(bf16)
    low = (values - high.astype(f32)).astype(bf16)
    return dot(jnp.concatenate([high, low], axis=0), fan, TN)


def packed(state, decay, columns):
    high = decay.astype(bf16).astype(f32)
    row = lax.broadcasted_iota(jnp.int32, (8, decay.shape[1]), 0)
    rest = jnp.where(row == 0, high, jnp.where(row == 1, decay - high, 0.0))
    return jnp.concatenate([state, columns, rest], axis=0)


def opened(msg):
    msg = msg[...].astype(f32)
    at = STATE + 8
    return msg[:STATE], msg[at : at + 1] + msg[at + 1 : at + 2]


def columns_in(msg):
    return msg[...].astype(f32)[STATE : STATE + 8]


def after(a, b):
    return b[0] + b[1] * a[0], a[1] * b[1]


def chosen(pred, a, b):
    return jnp.where(pred, a[0], b[0]), jnp.where(pred, a[1], b[1])


def nothing():
    return jnp.zeros((STATE, HALF), f32), jnp.ones((1, HALF), f32)


def head_fan():
    row = lax.broadcasted_iota(jnp.int32, (2 * HEADS, LANES), 0)
    lane = lax.broadcasted_iota(jnp.int32, (2 * HEADS, LANES), 1)
    return (row % HEADS == lane // HEAD_DIM).astype(bf16)


def entry_kernel(first, last, offset, rows, *refs):
    (order, own, left, right, opposite) = refs[:5]
    refs = refs[5:]
    columns = ()
    if last:
        columns, refs = refs[:1], refs[1:]
    if not first:
        tail_in, state_in, total_in, refs = *refs[:3], refs[3:]
    (gain, wv, wbcv, wdt, taps, dt_bias, a_log), refs = refs[:7], refs[7:]
    (z_out, xc_out, b_out, c_out, cum_out, step_out, ent_out, pri_out), refs = refs[:8], refs[8:]
    if last:
        (keep_out, send_out), refs = refs[:2], refs[2:]
        columns = columns[0]
    else:
        (tail_out, state_out, total_out), refs = refs[:3], refs[3:]
    nbuf, xbuf = refs

    fan = head_fan()
    k_pos = lax.broadcasted_iota(jnp.int32, (STRETCH, STRETCH), 0)
    q_pos = lax.broadcasted_iota(jnp.int32, (STRETCH, STRETCH), 1)
    upto = (k_pos <= q_pos).astype(f32)
    lane = lax.broadcasted_iota(jnp.int32, (HEADS, STRETCH), 1)
    rate = jnp.exp(a_log[:, 0:1])
    if first:
        state = jnp.zeros((STATE, LANES), f32)
        total = jnp.zeros((HEADS, 1), f32)
    else:
        state = state_in[...]
        total = total_in[:, 0:1]
        xbuf[0:HALO, :] = tail_in[...]
    for i in range(rows // BLOCK):
        span = pl.ds(i * BLOCK, BLOCK)
        above = pl.ds(offset + i * BLOCK, BLOCK)
        pieces = [r[above, :] for r in (own, left, right, opposite)]
        widen = [x.astype(f32) for x in pieces]
        square = sum(jnp.sum(x * x, axis=1, keepdims=True) for x in widen)
        scale = lax.rsqrt(square * (1.0 / 2048) + epsilon)
        for p in range(4):
            nbuf[HALO : HALO + BLOCK, p * 512 : (p + 1) * 512] = (
                widen[p] * scale * gain[order[p]]
            ).astype(bf16)
        if first and i == 0:
            widen = [r[0:HALO, :].astype(f32) for r in (own, left, right, opposite)]
            square = sum(jnp.sum(x * x, axis=1, keepdims=True) for x in widen)
            scale = lax.rsqrt(square * (1.0 / 2048) + epsilon)
            for p in range(4):
                nbuf[0:HALO, p * 512 : (p + 1) * 512] = (
                    widen[p] * scale * gain[order[p]]
                ).astype(bf16)
        low = 0 if first and i == 0 else HALO
        if low and i > 0:
            xbuf[0:HALO, :] = xbuf[BLOCK : BLOCK + HALO, :]
        normed = nbuf[low : HALO + BLOCK, :]
        xbuf[low : HALO + BLOCK, 0:LANES] = dot(normed, wv[:, 0:LANES]).astype(bf16).astype(f32)
        z_out[span, :] = dot(nbuf[HALO:, :], wv[:, LANES:]).astype(bf16)
        xbuf[low : HALO + BLOCK, LANES:] = dot(normed, wbcv[...]).astype(bf16).astype(f32)
        dt = sum(
            dot(wdt[order[p]], nbuf[HALO:, p * 512 : (p + 1) * 512], NT) for p in range(4)
        )
        mixed = jnp.zeros((BLOCK, LANES + 2 * STATE), f32)
        for k in range(4):
            mixed = mixed + taps[k : k + 1, :] * xbuf[pl.ds(HALO - 3 + k, BLOCK), :]
        mixed = silu(mixed)
        xc = mixed[:, 0:LANES]
        b = mixed[:, LANES : LANES + STATE].astype(bf16)
        xc_out[span, :] = xc.astype(bf16)
        b_out[span, :] = b
        c_out[span, :] = mixed[:, LANES + STATE :].astype(bf16)
        step = softplus(dt + dt_bias[:, 0:1])
        decay = -step * rate
        step_out[:, i * BLOCK : (i + 1) * BLOCK] = step
        cums, marks = [], jnp.zeros((HEADS, STRETCH), f32)
        for j in range(2):
            part = decay[:, j * STRETCH : (j + 1) * STRETCH]
            cum = lax.dot_general(
                part,
                upto,
                (((1,), (0,)), ((), ())),
                preferred_element_type=f32,
                precision=lax.Precision.HIGHEST,
            )
            cum_out[:, i * BLOCK + j * STRETCH : i * BLOCK + (j + 1) * STRETCH] = cum
            end = cum[:, STRETCH - 1 : STRETCH]
            marks = jnp.where(lane == j, end, jnp.where(lane == 2 + j, total, marks))
            total = total + end
            cums.append((cum, end))
        marks = jnp.where(lane == 4, total, marks)
        marks = spread_heads(jnp.exp(marks), fan)
        for j in range(2):
            cum, end = cums[j]
            here = slice(j * STRETCH, (j + 1) * STRETCH)
            weight = spread_heads(step[:, here] * jnp.exp(end - cum), fan)
            fresh = dot(b[here, :], (xc[here, :] * weight).astype(bf16), TN)
            ent_out[2 * i + j] = state
            pri_out[2 * i + j] = marks[2 + j : 3 + j, :]
            state = state * marks[j : j + 1, :] + fresh
    if last:
        decayed = marks[4:5, :]
        near = packed(state[:, 0:HALF], decayed[:, 0:HALF], columns[...])
        far = packed(state[:, HALF:], decayed[:, HALF:], columns[...])
        even = order[4] == 0
        keep_out[...] = jnp.where(even, near, far).astype(bf16)
        send_out[...] = jnp.where(even, far, near).astype(bf16)
    else:
        tail_out[...] = xbuf[BLOCK : BLOCK + HALO, :]
        state_out[...] = state
        total_out[...] = jnp.broadcast_to(total, (HEADS, STRETCH))


def stage_kernel(which, order, w, wbc, w_out, wbc_out, sems):
    copies = []
    for p in range(4):
        source = pl.ds(pl.multiple_of(order[p] * 512, 512), 512)
        target = pl.ds(p * 512, 512)
        copies.append(
            pltpu.make_async_copy(w.at[which, source, :], w_out.at[target, :], sems.at[0, p])
        )
        copies.append(
            pltpu.make_async_copy(wbc.at[which, source, :], wbc_out.at[target, :], sems.at[1, p])
        )
    for c in copies:
        c.start()
    for c in copies:
        c.wait()


def staged(which, order, w, wbc):
    return pl.pallas_call(
        functools.partial(stage_kernel, which),
        out_shape=[pltpu.VMEM((2048, 2 * LANES), bf16), pltpu.VMEM((2048, 2 * STATE), bf16)],
        in_specs=[smem(), in_hbm(), in_hbm()],
        out_specs=[vmem()] * 2,
        scratch_shapes=[pltpu.SemaphoreType.DMA((2, 4))],
        compiler_params=pltpu.CompilerParams(vmem_limit_bytes=2 * MIB),
        name="stage",
    )(order, kept_in_hbm(w), kept_in_hbm(wbc))


def stage_out_kernel(which, order, w, out, sems):
    copies = []
    for p in range(4):
        source = pl.ds(pl.multiple_of(order[(0, 2, 1, 3)[p]] * 512, 512), 512)
        copies.append(pltpu.make_async_copy(w.at[which, :, source], out.at[p], sems.at[p]))
    for c in copies:
        c.start()
    for c in copies:
        c.wait()


def staged_out(which, order, w):
    return pl.pallas_call(
        functools.partial(stage_out_kernel, which),
        out_shape=pltpu.VMEM((4, LANES, LANES), bf16),
        in_specs=[smem(), in_hbm()],
        out_specs=vmem(),
        scratch_shapes=[pltpu.SemaphoreType.DMA((4,))],
        compiler_params=pltpu.CompilerParams(vmem_limit_bytes=2 * MIB),
        name="stage_out",
    )(order, kept_in_hbm(w))


def vmem():
    return pl.BlockSpec(memory_space=pltpu.VMEM)


def smem():
    return pl.BlockSpec(memory_space=pltpu.SMEM)


def in_hbm():
    return pl.BlockSpec(memory_space=pltpu.HBM)


def kept_in_hbm(x):
    return pltpu.with_memory_space_constraint(x, pltpu.HBM)


def entry(order, pieces, offset, columns, carry, gain, w, wbc, wdt, taps, dt_bias, a_log, last):
    first = carry is None
    rows = BLOCK
    shape = jax.ShapeDtypeStruct
    outs = [
        pltpu.VMEM((rows, LANES), bf16),
        pltpu.VMEM((rows, LANES), bf16),
        pltpu.VMEM((rows, STATE), bf16),
        pltpu.VMEM((rows, STATE), bf16),
        pltpu.VMEM((HEADS, rows), f32),
        pltpu.VMEM((HEADS, rows), f32),
        pltpu.VMEM((rows // STRETCH, STATE, LANES), f32),
        pltpu.VMEM((rows // STRETCH, 1, LANES), f32),
    ]
    if last:
        outs += [shape((MSG, HALF), bf16)] * 2
    else:
        outs += [
            pltpu.VMEM((HALO, LANES + 2 * STATE), f32),
            pltpu.VMEM((STATE, LANES), f32),
            pltpu.VMEM((HEADS, STRETCH), f32),
        ]
    extra = [] if first else list(carry)
    operands = [order, *pieces, *([columns] if last else []), *extra, gain, w, wbc, wdt, taps, dt_bias, a_log]
    specs = [smem()] + [vmem()] * (len(operands) - 1)
    return pl.pallas_call(
        functools.partial(entry_kernel, first, last, offset, rows),
        out_shape=outs,
        in_specs=specs,
        out_specs=[vmem()] * len(outs),
        scratch_shapes=[
            pltpu.VMEM((HALO + BLOCK, 2048), bf16),
            pltpu.VMEM((HALO + BLOCK, LANES + 2 * STATE), f32),
        ],
        compiler_params=pltpu.CompilerParams(vmem_limit_bytes=8 * MIB),
        name="entry",
    )(*operands)


def inside_kernel(rows, xc, b, c, cum, step, skip, y_out):
    q_pos = lax.broadcasted_iota(jnp.int32, (STRETCH, STRETCH), 0)
    k_pos = lax.broadcasted_iota(jnp.int32, (STRETCH, STRETCH), 1)
    causal = k_pos <= q_pos
    low_half = k_pos < HEAD_DIM
    skips = spread_heads(skip[...], head_fan())[0:1, :]
    for j in range(rows // STRETCH):
        here = slice(j * STRETCH, (j + 1) * STRETCH)
        match = jnp.where(causal, dot(c[here, :], b[here, :], NT), 0.0)
        cum_rows = cum[:, here]
        step_rows = step[:, here]
        cum_cols = jnp.transpose(cum_rows)
        for pair in range(HEADS // 2):
            weights = []
            for h in (2 * pair, 2 * pair + 1):
                gap = jnp.minimum(cum_cols[:, h : h + 1] - cum_rows[h : h + 1, :], 0.0)
                weights.append((match * (jnp.exp(gap) * step_rows[h : h + 1, :])).astype(bf16))
            lanes = slice(pair * STRETCH, (pair + 1) * STRETCH)
            x = xc[here, lanes].astype(f32)
            stacked = jnp.concatenate(
                [jnp.where(low_half, x, 0.0), jnp.where(low_half, 0.0, x)], axis=0
            ).astype(bf16)
            y_out[here, lanes] = (
                dot(jnp.concatenate(weights, axis=1), stacked) + skips[:, lanes] * x
            )


def inside(xc, b, c, cum, step, skip):
    rows = xc.shape[0]
    return pl.pallas_call(
        functools.partial(inside_kernel, rows),
        out_shape=pltpu.VMEM((rows, LANES), f32),
        in_specs=[vmem()] * 6,
        out_specs=vmem(),
        compiler_params=pltpu.CompilerParams(vmem_limit_bytes=4 * MIB),
        name="inside",
    )(xc, b, c, cum, step, skip)


def exit_kernel(chunks, order, mine, other, gain, wv, *refs):
    parts = [refs[6 * i : 6 * i + 6] for i in range(chunks)]
    own, up, down, plus_a, minus_b = refs[6 * chunks :]
    split = chunks * BLOCK // 2
    outs = (((plus_a, 0), (up, split)), ((down, split), (minus_b, 0)), ((up, 0), (down, 0)))
    fan = head_fan()
    row = lax.broadcasted_iota(jnp.int32, (BLOCK, BLOCK), 0) // HEAD_DIM
    lane = lax.broadcasted_iota(jnp.int32, (BLOCK, BLOCK), 1) // HEAD_DIM
    same_head = (row == lane).astype(bf16)
    here, there = mine[...].astype(f32), other[...].astype(f32)
    even = order[4] == 0
    came = jnp.concatenate([jnp.where(even, here, there), jnp.where(even, there, here)], axis=1)
    for i in range(chunks):
        y, z, c, cum, ent, pri = parts[i]
        mixed = []
        for j in range(2):
            here = slice(j * STRETCH, (j + 1) * STRETCH)
            entering = (ent[j] + pri[j] * came).astype(bf16)
            carried = dot(c[here, :], entering) * spread_heads(jnp.exp(cum[:, here]), fan)
            gated = (y[here, :] + carried) * silu(z[here, :].astype(f32))
            square = (gated * gated).astype(bf16)
            sums = jnp.concatenate(
                [dot(square[:, 0:BLOCK], same_head), dot(square[:, BLOCK:], same_head)], axis=1
            )
            scale = lax.rsqrt(sums * (1.0 / HEAD_DIM) + epsilon)
            mixed.append((gated * scale * gain[...]).astype(bf16))
        mixed = jnp.concatenate(mixed, axis=0)
        own[i * BLOCK : (i + 1) * BLOCK, :] = dot(mixed, wv[0]).astype(bf16)
        for p in range(3):
            product = dot(mixed, wv[p + 1]).astype(bf16)
            for j in range(2):
                at = i * BLOCK + j * STRETCH
                out, base = outs[p][at // split]
                at = base + at % split
                out[at : at + STRETCH, :] = product[j * STRETCH : (j + 1) * STRETCH, :]


def leave(order, mine, other, gain, w, parts):
    rows = len(parts) * BLOCK
    shape = jax.ShapeDtypeStruct
    outs = [shape((rows, LANES), bf16)] * 3 + [shape((rows // 2, LANES), bf16)] * 2
    operands = [order, mine, other, gain, w, *(a for part in parts for a in part)]
    return pl.pallas_call(
        functools.partial(exit_kernel, len(parts)),
        out_shape=outs,
        in_specs=[smem()] + [vmem()] * (len(operands) - 1),
        out_specs=[vmem()] * len(outs),
        compiler_params=pltpu.CompilerParams(vmem_limit_bytes=6 * MIB),
        name="leave",
    )(*operands)


def small_call(kernel, name, outs, place, *operands):
    return pl.pallas_call(
        kernel,
        out_shape=outs,
        in_specs=[smem()] + [vmem()] * len(operands),
        out_specs=[vmem()] * len(outs),
        compiler_params=pltpu.CompilerParams(vmem_limit_bytes=2 * MIB),
        name=name,
    )(place, *operands)


def chip_kernel(place, keep, got, out):
    even = place[4] == 0
    mine, other = opened(keep), opened(got)
    both = after(chosen(even, mine, other), chosen(even, other, mine))
    out[...] = packed(*both, columns_in(keep) + columns_in(got)).astype(bf16)


def row_kernel(place, chip, one, two, three, row_out, before_out):
    y = place[5]
    ring = [opened(r) for r in (chip, one, two, three)]
    row, before = nothing(), nothing()
    for at in range(4):
        here = ring[0]
        for k in range(1, 4):
            here = chosen((y + 4 - at) % 4 == k, ring[k], here)
        before = chosen(at < y, after(before, here), before)
        row = after(row, here)
    columns = sum(columns_in(r) for r in (chip, one, two, three))
    row_out[...] = packed(*row, columns).astype(bf16)
    before_out[...] = packed(*before, columns)


def arrive_kernel(place, one, two, three, before, keep, got, mine_out, other_out, columns_out):
    even = place[4] == 0
    z = place[6]
    came = nothing()
    for k, r in ((3, three), (2, two), (1, one)):
        came = chosen(z >= k, after(came, opened(r)), came)
    first = after(came, opened(before))
    second = after(first, chosen(even, opened(keep), opened(got)))
    mine_out[...] = jnp.where(even, first[0], second[0]).astype(bf16)
    other_out[...] = jnp.where(even, second[0], first[0]).astype(bf16)
    columns_out[...] = sum(columns_in(r) for r in (before, one, two, three))


def give_kernel(columns, x, out):
    cell = lax.broadcasted_iota(jnp.int32, (512, HALF), 0)
    for part in range(2):
        wanted = 2.0 * columns[2 * part : 2 * part + 1, :] + columns[2 * part + 1 : 2 * part + 2, :]
        pick = (cell == wanted.astype(jnp.int32)).astype(bf16)
        for r in range(2):
            rows = dot(pick, x[r * 512 : (r + 1) * 512, :], TN).astype(bf16)
            out[part * 16 : (part + 1) * 16, r * 16 : (r + 1) * 16, :] = rows.reshape(16, 16, 512)


def given(columns, x):
    return pl.pallas_call(
        give_kernel,
        out_shape=jax.ShapeDtypeStruct((32, 32, 512), bf16),
        in_specs=[vmem()] * 2,
        out_specs=vmem(),
        compiler_params=pltpu.CompilerParams(vmem_limit_bytes=6 * MIB),
        name="give",
    )(columns, x)


def turned(by):
    return [(i, (i + by) % TP) for i in range(TP)]


def around(x, by):
    return lax.ppermute(x, "tp", turned(by))


def swapped(x):
    return lax.ppermute(x, "seq_2", [(0, 1), (1, 0)])


def arriving_state(place, keep, send, weights, beside, wrapped):
    shape = jax.ShapeDtypeStruct
    got = swapped(send)
    msg = shape((MSG, HALF), bf16)
    (chip,) = small_call(chip_kernel, "chip", [msg], place, keep, got)
    ring = [lax.ppermute(chip, "seq_1", turned(k)) for k in (1, 2, 3)]
    row, before = small_call(
        row_kernel,
        "row",
        [msg, shape((MSG, HALF), f32)],
        behind(place, weights),
        chip,
        *ring,
    )
    earlier = [
        lax.ppermute(row, "seq_0", turned(k)[: 4 if wrapped else 4 - k]) for k in (1, 2, 3)
    ]
    mine, other, columns = small_call(
        arrive_kernel,
        "arrive",
        [shape((STATE, HALF), bf16)] * 2 + [shape((8, HALF), f32)],
        behind(place, *beside),
        *earlier,
        before,
        keep,
        got,
    )
    return mine, swapped(other), columns


def behind(x, *done):
    return lax.optimization_barrier((x, *done))[0]


def with_halo(shard, count):
    pairs = [(i, i + 1) for i in range(lax.axis_size(SEQ) - 1)]
    return jnp.concatenate([lax.ppermute(shard[-HALO:], SEQ, pairs), shard[:count]], axis=0)


def layer(which, shard, first, place, params, large, columns, early=()):
    gain, wdt, taps, dt_bias, a_log, skip, out_gain = params
    w, wbc, w_out = large
    rows = [shard[i * BLOCK : (i + 1) * BLOCK] for i in range(shard.shape[0] // BLOCK)]
    wv, wbcv = staged(which, behind(place, first), w, wbc)
    carry, kept, gate = None, [], place

    def enter(i, pieces, offset=0):
        nonlocal carry, gate
        out = entry(
            gate, pieces, offset, columns, carry, gain, wv, wbcv, wdt, taps, dt_bias, a_log, i == 3
        )
        z, xc, b, c, cum, step, ent, pri = out[:8]
        carry = out[8:]
        y = inside(xc, b, c, cum, step, skip)
        kept.append((y, z, c, cum, ent, pri))
        if i < 2:
            gate = behind(place, y)

    if which == 0:
        own = [first, behind(rows[2], first), behind(rows[3], first)]
        left, right = [around(first, 1)], [around(first, -1)]
        right.append(around(own[1], -1))
        opposite = [around(behind(left[0], *early), 1)]
        right.append(around(own[2], -1))
        left.append(around(behind(rows[2], right[1]), 1))
        opposite.append(around(right[1], -1))
        pieces = (own[0], left[0], right[0], opposite[0])
        enter(0, pieces, HALO)
        left.append(around(behind(rows[3], carry[0]), 1))
        opposite.append(around(behind(right[2], carry[0]), -1))
        enter(1, pieces, HALO + BLOCK)
        for i in (1, 2):
            enter(i + 1, (own[i], left[i], right[i], opposite[i]))
    else:
        own = [first, behind(rows[1], first), behind(rows[2], first, wbcv)]
        left, right = [around(x, 1) for x in own], [around(x, -1) for x in own]
        opposite = [around(left[0], 1)]
        enter(0, (own[0], left[0], right[0], opposite[0]), HALO)
        own.append(behind(rows[3], first, carry[0]))
        left.append(around(own[3], 1))
        right.append(around(own[3], -1))
        opposite.append(around(right[1], -1))
        enter(1, (own[1], left[1], right[1], opposite[1]))
        opposite.append(around(left[2], 1))
        opposite.append(around(behind(right[3], carry[0]), -1))
        for i in (2, 3):
            enter(i, (own[i], left[i], right[i], opposite[i]))
    wov = staged_out(which, behind(place, carry[0]), w_out)
    mine, other, columns = arriving_state(
        place, *carry, wov, [k[0] for k in kept], which == 0
    )
    results = []
    for low in (0, 2):
        own_part, up, down, plus_a, minus_b = leave(
            place, mine, other, out_gain, wov, kept[low : low + 2]
        )
        up, down = around(up, 1), around(down, -1)
        plus_a = around((plus_a.astype(f32) + up[:BLOCK].astype(f32)).astype(bf16), 1)
        minus_b = around((minus_b.astype(f32) + down[:BLOCK].astype(f32)).astype(bf16), -1)
        here = shard[low * BLOCK : (low + 2) * BLOCK].astype(f32) + own_part.astype(f32)
        results.append(here[:BLOCK] + plus_a.astype(f32) + down[BLOCK:].astype(f32))
        results.append(here[BLOCK:] + up[BLOCK:].astype(f32) + minus_b.astype(f32))
    return jnp.concatenate(results, axis=0).astype(bf16), columns


def permuted(x, source):
    pick = (source[:, None] == jnp.arange(x.shape[0])[None, :]).astype(bf16)
    return jnp.dot(pick, x, preferred_element_type=f32).astype(bf16)


def body(
    tokens,
    col_order,
    in_gain,
    w_in,
    w_bc,
    w_dt,
    conv_x,
    conv_bc,
    dt_bias,
    a_log,
    d_skip,
    out_gain,
    w_out,
):
    first = with_halo(tokens, 2 * BLOCK)
    arguments = (in_gain, w_in, w_dt, conv_x, conv_bc, dt_bias, a_log, d_skip, out_gain, col_order)
    in_gain, w_in, w_dt, conv_x, conv_bc, dt_bias, a_log, d_skip, out_gain, col_order = behind(
        arguments, first
    )
    x = lax.axis_index("tp")
    core, y, z = (lax.axis_index(a) for a in ("seq_2", "seq_1", "seq_0"))
    place = jnp.stack([x, (x + 3) & 3, (x + 1) & 3, (x + 2) & 3, core, y, z]).astype(jnp.int32)
    w = w_in.reshape(2, 2048, 2 * LANES)

    def on_lanes(heads):
        return jnp.broadcast_to(heads[:, None], (HEADS, STRETCH))

    def params(which):
        return (
            in_gain[which].reshape(TP, 1, 512),
            w_dt[which].T.reshape(HEADS, TP, 512).transpose(1, 0, 2),
            jnp.concatenate([conv_x[which], conv_bc[which]], axis=1),
            on_lanes(dt_bias[which]),
            on_lanes(a_log[which]),
            on_lanes(d_skip[which]),
            out_gain[which].reshape(1, LANES),
        )

    starts = col_order.reshape(16, 64)[:, 0]
    slot = jnp.arange(512)
    columns = jnp.where(
        slot // 16 == lax.axis_index(SEQ), jnp.tile(starts % 512, 32), 0
    ).reshape(2, 256)
    columns = jnp.stack([columns[0] // 2, columns[0] % 2, columns[1] // 2, columns[1] % 2])
    columns = jnp.pad(columns.astype(f32), ((0, 4), (0, 0)))
    visit = jnp.arange(16)[:, None]
    along = jnp.arange(64)[None, :]
    row = jnp.where((starts >= 512)[:, None], 63 - along, along)
    take = ((row // 2) * 32 + (row % 2) * 16 + visit).reshape(1024)
    place, small, w, columns, take = lax.optimization_barrier(
        (place, [params(0), params(1)], w, columns, take)
    )
    large = (w, w_bc, w_out)

    row_result, columns = layer(0, tokens, first, place, small[0], large, columns, (w,))
    payload = given(columns, row_result)
    arrived = lax.all_to_all(payload, SEQ, 0, 0, tiled=True).reshape(1024, 512)
    own_rows = permuted(arrived, take)
    return layer(1, own_rows, with_halo(own_rows, BLOCK), place, small[1], large, columns)[0]


def solution(mesh):
    torus = Mesh(mesh.devices.reshape(4, 4, 2, mesh.shape["tp"]), ("seq_0", "seq_1", "seq_2", "tp"))
    return jax.shard_map(
        body,
        mesh=torus,
        in_specs=(
            P(SEQ, "tp"),
            P(SEQ),
            P(),
            P(None, None, None, "tp"),
            P(),
            P(None, None, "tp"),
            P(None, None, "tp"),
            P(),
            P(None, "tp"),
            P(None, "tp"),
            P(None, "tp"),
            P(None, "tp"),
            P(None, "tp", None),
        ),
        out_specs=P(SEQ, "tp"),
        check_vma=False,
    )
```

```python
import functools

import jax
import jax.numpy as jnp
from jax import lax
from jax.experimental import pallas as pl
from jax.experimental.pallas import tpu as pltpu
from jax.sharding import Mesh
from jax.sharding import PartitionSpec as P

HEAD_DIM = 64
STATE = 128
STRETCH = 128
HEADS = 8
LANES = 512
HALF = 256
HALO = 16
BLOCK = 256
MSG = 144
SEQ = ("seq_0", "seq_1", "seq_2")
TP = 4
epsilon = 1e-05
f32 = jnp.float32
bf16 = jnp.bfloat16
NT = (((1,), (1,)), ((), ()))
TN = (((0,), (0,)), ((), ()))
MIB = 2**20


def dot(a, b, dims=None):
    dims = dims or (((1,), (0,)), ((), ()))
    return lax.dot_general(a, b, dims, preferred_element_type=f32)


def silu(x):
    return x / (1.0 + jnp.exp(-x))


def softplus(x):
    return jnp.maximum(x, 0.0) + jnp.log1p(jnp.exp(-jnp.abs(x)))


def spread_heads(values, fan):
    high = values.astype(bf16)
    low = (values - high.astype(f32)).astype(bf16)
    return dot(jnp.concatenate([high, low], axis=0), fan, TN)


def packed(state, decay, columns):
    high = decay.astype(bf16).astype(f32)
    row = lax.broadcasted_iota(jnp.int32, (8, decay.shape[1]), 0)
    rest = jnp.where(row == 0, high, jnp.where(row == 1, decay - high, 0.0))
    return jnp.concatenate([state, columns, rest], axis=0)


def opened(msg):
    msg = msg[...].astype(f32)
    at = STATE + 8
    return msg[:STATE], msg[at : at + 1] + msg[at + 1 : at + 2]


def columns_in(msg):
    return msg[...].astype(f32)[STATE : STATE + 8]


def after(a, b):
    return b[0] + b[1] * a[0], a[1] * b[1]


def chosen(pred, a, b):
    return jnp.where(pred, a[0], b[0]), jnp.where(pred, a[1], b[1])


def nothing():
    return jnp.zeros((STATE, HALF), f32), jnp.ones((1, HALF), f32)


def head_fan():
    row = lax.broadcasted_iota(jnp.int32, (2 * HEADS, LANES), 0)
    lane = lax.broadcasted_iota(jnp.int32, (2 * HEADS, LANES), 1)
    return (row % HEADS == lane // HEAD_DIM).astype(bf16)


def entry_kernel(first, last, offset, rows, *refs):
    (order, own, left, right, opposite) = refs[:5]
    refs = refs[5:]
    columns = ()
    if last:
        columns, refs = refs[:1], refs[1:]
    if not first:
        tail_in, state_in, total_in, refs = *refs[:3], refs[3:]
    (gain, wv, wbcv, wdt, taps, dt_bias, a_log), refs = refs[:7], refs[7:]
    (z_out, xc_out, b_out, c_out, cum_out, step_out, ent_out, pri_out), refs = refs[:8], refs[8:]
    if last:
        (keep_out, send_out), refs = refs[:2], refs[2:]
        columns = columns[0]
    else:
        (tail_out, state_out, total_out), refs = refs[:3], refs[3:]
    nbuf, xbuf = refs

    fan = head_fan()
    k_pos = lax.broadcasted_iota(jnp.int32, (STRETCH, STRETCH), 0)
    q_pos = lax.broadcasted_iota(jnp.int32, (STRETCH, STRETCH), 1)
    upto = (k_pos <= q_pos).astype(f32)
    lane = lax.broadcasted_iota(jnp.int32, (HEADS, STRETCH), 1)
    rate = jnp.exp(a_log[:, 0:1])
    if first:
        state = jnp.zeros((STATE, LANES), f32)
        total = jnp.zeros((HEADS, 1), f32)
    else:
        state = state_in[...]
        total = total_in[:, 0:1]
        xbuf[0:HALO, :] = tail_in[...]
    for i in range(rows // BLOCK):
        span = pl.ds(i * BLOCK, BLOCK)
        above = pl.ds(offset + i * BLOCK, BLOCK)
        pieces = [r[above, :] for r in (own, left, right, opposite)]
        widen = [x.astype(f32) for x in pieces]
        square = sum(jnp.sum(x * x, axis=1, keepdims=True) for x in widen)
        scale = lax.rsqrt(square * (1.0 / 2048) + epsilon)
        for p in range(4):
            nbuf[HALO : HALO + BLOCK, p * 512 : (p + 1) * 512] = (
                widen[p] * scale * gain[order[p]]
            ).astype(bf16)
        if first and i == 0:
            widen = [r[0:HALO, :].astype(f32) for r in (own, left, right, opposite)]
            square = sum(jnp.sum(x * x, axis=1, keepdims=True) for x in widen)
            scale = lax.rsqrt(square * (1.0 / 2048) + epsilon)
            for p in range(4):
                nbuf[0:HALO, p * 512 : (p + 1) * 512] = (
                    widen[p] * scale * gain[order[p]]
                ).astype(bf16)
        low = 0 if first and i == 0 else HALO
        if low and i > 0:
            xbuf[0:HALO, :] = xbuf[BLOCK : BLOCK + HALO, :]
        normed = nbuf[low : HALO + BLOCK, :]
        xbuf[low : HALO + BLOCK, 0:LANES] = dot(normed, wv[:, 0:LANES]).astype(bf16).astype(f32)
        z_out[span, :] = dot(nbuf[HALO:, :], wv[:, LANES:]).astype(bf16)
        xbuf[low : HALO + BLOCK, LANES:] = dot(normed, wbcv[...]).astype(bf16).astype(f32)
        dt = sum(
            dot(wdt[order[p]], nbuf[HALO:, p * 512 : (p + 1) * 512], NT) for p in range(4)
        )
        mixed = jnp.zeros((BLOCK, LANES + 2 * STATE), f32)
        for k in range(4):
            mixed = mixed + taps[k : k + 1, :] * xbuf[pl.ds(HALO - 3 + k, BLOCK), :]
        mixed = silu(mixed)
        xc = mixed[:, 0:LANES]
        b = mixed[:, LANES : LANES + STATE].astype(bf16)
        xc_out[span, :] = xc.astype(bf16)
        b_out[span, :] = b
        c_out[span, :] = mixed[:, LANES + STATE :].astype(bf16)
        step = softplus(dt + dt_bias[:, 0:1])
        decay = -step * rate
        step_out[:, i * BLOCK : (i + 1) * BLOCK] = step
        cums, marks = [], jnp.zeros((HEADS, STRETCH), f32)
        for j in range(2):
            part = decay[:, j * STRETCH : (j + 1) * STRETCH]
            cum = lax.dot_general(
                part,
                upto,
                (((1,), (0,)), ((), ())),
                preferred_element_type=f32,
                precision=lax.Precision.HIGHEST,
            )
            cum_out[:, i * BLOCK + j * STRETCH : i * BLOCK + (j + 1) * STRETCH] = cum
            end = cum[:, STRETCH - 1 : STRETCH]
            marks = jnp.where(lane == j, end, jnp.where(lane == 2 + j, total, marks))
            total = total + end
            cums.append((cum, end))
        marks = jnp.where(lane == 4, total, marks)
        marks = spread_heads(jnp.exp(marks), fan)
        for j in range(2):
            cum, end = cums[j]
            here = slice(j * STRETCH, (j + 1) * STRETCH)
            weight = spread_heads(step[:, here] * jnp.exp(end - cum), fan)
            fresh = dot(b[here, :], (xc[here, :] * weight).astype(bf16), TN)
            ent_out[2 * i + j] = state
            pri_out[2 * i + j] = marks[2 + j : 3 + j, :]
            state = state * marks[j : j + 1, :] + fresh
    if last:
        decayed = marks[4:5, :]
        near = packed(state[:, 0:HALF], decayed[:, 0:HALF], columns[...])
        far = packed(state[:, HALF:], decayed[:, HALF:], columns[...])
        even = order[4] == 0
        keep_out[...] = jnp.where(even, near, far).astype(bf16)
        send_out[...] = jnp.where(even, far, near).astype(bf16)
    else:
        tail_out[...] = xbuf[BLOCK : BLOCK + HALO, :]
        state_out[...] = state
        total_out[...] = jnp.broadcast_to(total, (HEADS, STRETCH))


def stage_kernel(which, order, w, wbc, w_out, wbc_out, sems):
    copies = []
    for p in range(4):
        source = pl.ds(pl.multiple_of(order[p] * 512, 512), 512)
        target = pl.ds(p * 512, 512)
        copies.append(
            pltpu.make_async_copy(w.at[which, source, :], w_out.at[target, :], sems.at[0, p])
        )
        copies.append(
            pltpu.make_async_copy(wbc.at[which, source, :], wbc_out.at[target, :], sems.at[1, p])
        )
    for c in copies:
        c.start()
    for c in copies:
        c.wait()


def staged(which, order, w, wbc):
    return pl.pallas_call(
        functools.partial(stage_kernel, which),
        out_shape=[pltpu.VMEM((2048, 2 * LANES), bf16), pltpu.VMEM((2048, 2 * STATE), bf16)],
        in_specs=[smem(), in_hbm(), in_hbm()],
        out_specs=[vmem()] * 2,
        scratch_shapes=[pltpu.SemaphoreType.DMA((2, 4))],
        compiler_params=pltpu.CompilerParams(vmem_limit_bytes=2 * MIB),
        name="stage",
    )(order, kept_in_hbm(w), kept_in_hbm(wbc))


def stage_out_kernel(which, order, w, out, sems):
    copies = []
    for p in range(4):
        source = pl.ds(pl.multiple_of(order[(0, 2, 1, 3)[p]] * 512, 512), 512)
        copies.append(pltpu.make_async_copy(w.at[which, :, source], out.at[p], sems.at[p]))
    for c in copies:
        c.start()
    for c in copies:
        c.wait()


def staged_out(which, order, w):
    return pl.pallas_call(
        functools.partial(stage_out_kernel, which),
        out_shape=pltpu.VMEM((4, LANES, LANES), bf16),
        in_specs=[smem(), in_hbm()],
        out_specs=vmem(),
        scratch_shapes=[pltpu.SemaphoreType.DMA((4,))],
        compiler_params=pltpu.CompilerParams(vmem_limit_bytes=2 * MIB),
        name="stage_out",
    )(order, kept_in_hbm(w))


def vmem():
    return pl.BlockSpec(memory_space=pltpu.VMEM)


def smem():
    return pl.BlockSpec(memory_space=pltpu.SMEM)


def in_hbm():
    return pl.BlockSpec(memory_space=pltpu.HBM)


def kept_in_hbm(x):
    return pltpu.with_memory_space_constraint(x, pltpu.HBM)


def entry(order, pieces, offset, columns, carry, gain, w, wbc, wdt, taps, dt_bias, a_log, last):
    first = carry is None
    rows = BLOCK
    shape = jax.ShapeDtypeStruct
    outs = [
        pltpu.VMEM((rows, LANES), bf16),
        pltpu.VMEM((rows, LANES), bf16),
        pltpu.VMEM((rows, STATE), bf16),
        pltpu.VMEM((rows, STATE), bf16),
        pltpu.VMEM((HEADS, rows), f32),
        pltpu.VMEM((HEADS, rows), f32),
        pltpu.VMEM((rows // STRETCH, STATE, LANES), f32),
        pltpu.VMEM((rows // STRETCH, 1, LANES), f32),
    ]
    if last:
        outs += [shape((MSG, HALF), bf16)] * 2
    else:
        outs += [
            pltpu.VMEM((HALO, LANES + 2 * STATE), f32),
            pltpu.VMEM((STATE, LANES), f32),
            pltpu.VMEM((HEADS, STRETCH), f32),
        ]
    extra = [] if first else list(carry)
    operands = [order, *pieces, *([columns] if last else []), *extra, gain, w, wbc, wdt, taps, dt_bias, a_log]
    specs = [smem()] + [vmem()] * (len(operands) - 1)
    return pl.pallas_call(
        functools.partial(entry_kernel, first, last, offset, rows),
        out_shape=outs,
        in_specs=specs,
        out_specs=[vmem()] * len(outs),
        scratch_shapes=[
            pltpu.VMEM((HALO + BLOCK, 2048), bf16),
            pltpu.VMEM((HALO + BLOCK, LANES + 2 * STATE), f32),
        ],
        compiler_params=pltpu.CompilerParams(vmem_limit_bytes=8 * MIB),
        name="entry",
    )(*operands)


def inside_kernel(rows, xc, b, c, cum, step, skip, y_out):
    q_pos = lax.broadcasted_iota(jnp.int32, (STRETCH, STRETCH), 0)
    k_pos = lax.broadcasted_iota(jnp.int32, (STRETCH, STRETCH), 1)
    causal = k_pos <= q_pos
    low_half = k_pos < HEAD_DIM
    skips = spread_heads(skip[...], head_fan())[0:1, :]
    for j in range(rows // STRETCH):
        here = slice(j * STRETCH, (j + 1) * STRETCH)
        match = jnp.where(causal, dot(c[here, :], b[here, :], NT), 0.0)
        cum_rows = cum[:, here]
        step_rows = step[:, here]
        cum_cols = jnp.transpose(cum_rows)
        for pair in range(HEADS // 2):
            weights = []
            for h in (2 * pair, 2 * pair + 1):
                gap = jnp.minimum(cum_cols[:, h : h + 1] - cum_rows[h : h + 1, :], 0.0)
                weights.append((match * (jnp.exp(gap) * step_rows[h : h + 1, :])).astype(bf16))
            lanes = slice(pair * STRETCH, (pair + 1) * STRETCH)
            x = xc[here, lanes].astype(f32)
            stacked = jnp.concatenate(
                [jnp.where(low_half, x, 0.0), jnp.where(low_half, 0.0, x)], axis=0
            ).astype(bf16)
            y_out[here, lanes] = (
                dot(jnp.concatenate(weights, axis=1), stacked) + skips[:, lanes] * x
            )


def inside(xc, b, c, cum, step, skip):
    rows = xc.shape[0]
    return pl.pallas_call(
        functools.partial(inside_kernel, rows),
        out_shape=pltpu.VMEM((rows, LANES), f32),
        in_specs=[vmem()] * 6,
        out_specs=vmem(),
        compiler_params=pltpu.CompilerParams(vmem_limit_bytes=4 * MIB),
        name="inside",
    )(xc, b, c, cum, step, skip)


def exit_kernel(chunks, order, mine, other, gain, wv, *refs):
    parts = [refs[6 * i : 6 * i + 6] for i in range(chunks)]
    own, up, down, plus_a, minus_b = refs[6 * chunks :]
    split = chunks * BLOCK // 2
    outs = (((plus_a, 0), (up, split)), ((down, split), (minus_b, 0)), ((up, 0), (down, 0)))
    fan = head_fan()
    row = lax.broadcasted_iota(jnp.int32, (BLOCK, BLOCK), 0) // HEAD_DIM
    lane = lax.broadcasted_iota(jnp.int32, (BLOCK, BLOCK), 1) // HEAD_DIM
    same_head = (row == lane).astype(bf16)
    here, there = mine[...].astype(f32), other[...].astype(f32)
    even = order[4] == 0
    came = jnp.concatenate([jnp.where(even, here, there), jnp.where(even, there, here)], axis=1)
    for i in range(chunks):
        y, z, c, cum, ent, pri = parts[i]
        mixed = []
        for j in range(2):
            here = slice(j * STRETCH, (j + 1) * STRETCH)
            entering = (ent[j] + pri[j] * came).astype(bf16)
            carried = dot(c[here, :], entering) * spread_heads(jnp.exp(cum[:, here]), fan)
            gated = (y[here, :] + carried) * silu(z[here, :].astype(f32))
            square = (gated * gated).astype(bf16)
            sums = jnp.concatenate(
                [dot(square[:, 0:BLOCK], same_head), dot(square[:, BLOCK:], same_head)], axis=1
            )
            scale = lax.rsqrt(sums * (1.0 / HEAD_DIM) + epsilon)
            mixed.append((gated * scale * gain[...]).astype(bf16))
        mixed = jnp.concatenate(mixed, axis=0)
        own[i * BLOCK : (i + 1) * BLOCK, :] = dot(mixed, wv[0]).astype(bf16)
        for p in range(3):
            product = dot(mixed, wv[p + 1]).astype(bf16)
            for j in range(2):
                at = i * BLOCK + j * STRETCH
                out, base = outs[p][at // split]
                at = base + at % split
                out[at : at + STRETCH, :] = product[j * STRETCH : (j + 1) * STRETCH, :]


def leave(order, mine, other, gain, w, parts):
    rows = len(parts) * BLOCK
    shape = jax.ShapeDtypeStruct
    outs = [shape((rows, LANES), bf16)] * 3 + [shape((rows // 2, LANES), bf16)] * 2
    operands = [order, mine, other, gain, w, *(a for part in parts for a in part)]
    return pl.pallas_call(
        functools.partial(exit_kernel, len(parts)),
        out_shape=outs,
        in_specs=[smem()] + [vmem()] * (len(operands) - 1),
        out_specs=[vmem()] * len(outs),
        compiler_params=pltpu.CompilerParams(vmem_limit_bytes=6 * MIB),
        name="leave",
    )(*operands)


def small_call(kernel, name, outs, place, *operands):
    return pl.pallas_call(
        kernel,
        out_shape=outs,
        in_specs=[smem()] + [vmem()] * len(operands),
        out_specs=[vmem()] * len(outs),
        compiler_params=pltpu.CompilerParams(vmem_limit_bytes=2 * MIB),
        name=name,
    )(place, *operands)


def chip_kernel(place, keep, got, out):
    even = place[4] == 0
    mine, other = opened(keep), opened(got)
    both = after(chosen(even, mine, other), chosen(even, other, mine))
    out[...] = packed(*both, columns_in(keep) + columns_in(got)).astype(bf16)


def row_kernel(place, chip, one, two, three, row_out, before_out):
    y = place[5]
    ring = [opened(r) for r in (chip, one, two, three)]
    row, before = nothing(), nothing()
    for at in range(4):
        here = ring[0]
        for k in range(1, 4):
            here = chosen((y + 4 - at) % 4 == k, ring[k], here)
        before = chosen(at < y, after(before, here), before)
        row = after(row, here)
    columns = sum(columns_in(r) for r in (chip, one, two, three))
    row_out[...] = packed(*row, columns).astype(bf16)
    before_out[...] = packed(*before, columns)


def arrive_kernel(place, one, two, three, before, keep, got, mine_out, other_out, columns_out):
    even = place[4] == 0
    z = place[6]
    came = nothing()
    for k, r in ((3, three), (2, two), (1, one)):
        came = chosen(z >= k, after(came, opened(r)), came)
    first = after(came, opened(before))
    second = after(first, chosen(even, opened(keep), opened(got)))
    mine_out[...] = jnp.where(even, first[0], second[0]).astype(bf16)
    other_out[...] = jnp.where(even, second[0], first[0]).astype(bf16)
    columns_out[...] = sum(columns_in(r) for r in (before, one, two, three))


def give_kernel(columns, x, out):
    cell = lax.broadcasted_iota(jnp.int32, (512, HALF), 0)
    for part in range(2):
        wanted = 2.0 * columns[2 * part : 2 * part + 1, :] + columns[2 * part + 1 : 2 * part + 2, :]
        pick = (cell == wanted.astype(jnp.int32)).astype(bf16)
        for r in range(2):
            rows = dot(pick, x[r * 512 : (r + 1) * 512, :], TN).astype(bf16)
            out[part * 16 : (part + 1) * 16, r * 16 : (r + 1) * 16, :] = rows.reshape(16, 16, 512)


def given(columns, x):
    return pl.pallas_call(
        give_kernel,
        out_shape=jax.ShapeDtypeStruct((32, 32, 512), bf16),
        in_specs=[vmem()] * 2,
        out_specs=vmem(),
        compiler_params=pltpu.CompilerParams(vmem_limit_bytes=6 * MIB),
        name="give",
    )(columns, x)


def turned(by):
    return [(i, (i + by) % TP) for i in range(TP)]


def around(x, by):
    return lax.ppermute(x, "tp", turned(by))


def swapped(x):
    return lax.ppermute(x, "seq_2", [(0, 1), (1, 0)])


def arriving_state(place, keep, send, weights, beside, wrapped):
    shape = jax.ShapeDtypeStruct
    got = swapped(send)
    msg = shape((MSG, HALF), bf16)
    (chip,) = small_call(chip_kernel, "chip", [msg], place, keep, got)
    ring = [lax.ppermute(chip, "seq_1", turned(k)) for k in (1, 2, 3)]
    row, before = small_call(
        row_kernel,
        "row",
        [msg, shape((MSG, HALF), f32)],
        behind(place, weights),
        chip,
        *ring,
    )
    earlier = [
        lax.ppermute(row, "seq_0", turned(k)[: 4 if wrapped else 4 - k]) for k in (1, 2, 3)
    ]
    mine, other, columns = small_call(
        arrive_kernel,
        "arrive",
        [shape((STATE, HALF), bf16)] * 2 + [shape((8, HALF), f32)],
        behind(place, *beside),
        *earlier,
        before,
        keep,
        got,
    )
    return mine, swapped(other), columns


def behind(x, *done):
    return lax.optimization_barrier((x, *done))[0]


def with_halo(shard, count):
    pairs = [(i, i + 1) for i in range(lax.axis_size(SEQ) - 1)]
    return jnp.concatenate([lax.ppermute(shard[-HALO:], SEQ, pairs), shard[:count]], axis=0)


def layer(which, shard, first, place, params, large, columns, early=()):
    gain, wdt, taps, dt_bias, a_log, skip, out_gain = params
    w, wbc, w_out = large
    rows = [shard[i * BLOCK : (i + 1) * BLOCK] for i in range(shard.shape[0] // BLOCK)]
    wv, wbcv = staged(which, behind(place, first), w, wbc)
    carry, kept, gate = None, [], place

    def enter(i, pieces, offset=0):
        nonlocal carry, gate
        out = entry(
            gate, pieces, offset, columns, carry, gain, wv, wbcv, wdt, taps, dt_bias, a_log, i == 3
        )
        z, xc, b, c, cum, step, ent, pri = out[:8]
        carry = out[8:]
        y = inside(xc, b, c, cum, step, skip)
        kept.append((y, z, c, cum, ent, pri))
        if i < 2:
            gate = behind(place, y)

    if which == 0:
        own = [first, behind(rows[2], first), behind(rows[3], first)]
        left, right = [around(first, 1)], [around(first, -1)]
        right.append(around(own[1], -1))
        opposite = [around(behind(left[0], *early), 1)]
        right.append(around(own[2], -1))
        left.append(around(behind(rows[2], right[1]), 1))
        opposite.append(around(right[1], -1))
        pieces = (own[0], left[0], right[0], opposite[0])
        enter(0, pieces, HALO)
        left.append(around(behind(rows[3], carry[0]), 1))
        opposite.append(around(behind(right[2], carry[0]), -1))
        enter(1, pieces, HALO + BLOCK)
        for i in (1, 2):
            enter(i + 1, (own[i], left[i], right[i], opposite[i]))
    else:
        own = [first, behind(rows[1], first), behind(rows[2], first)]
        left, right = [around(x, 1) for x in own], [around(x, -1) for x in own]
        opposite = [around(behind(left[0], wbcv), 1)]
        enter(0, (own[0], left[0], right[0], opposite[0]), HALO)
        own.append(behind(rows[3], first, carry[0]))
        left.append(around(own[3], 1))
        right.append(around(own[3], -1))
        opposite.append(around(right[1], -1))
        enter(1, (own[1], left[1], right[1], opposite[1]))
        opposite.append(around(left[2], 1))
        opposite.append(around(behind(right[3], carry[0]), -1))
        for i in (2, 3):
            enter(i, (own[i], left[i], right[i], opposite[i]))
    wov = staged_out(which, behind(place, carry[0]), w_out)
    mine, other, columns = arriving_state(
        place, *carry, wov, [k[0] for k in kept], which == 0
    )
    results = []
    for low in (0, 2):
        own_part, up, down, plus_a, minus_b = leave(
            place, mine, other, out_gain, wov, kept[low : low + 2]
        )
        up, down = around(up, 1), around(down, -1)
        plus_a = around((plus_a.astype(f32) + up[:BLOCK].astype(f32)).astype(bf16), 1)
        minus_b = around((minus_b.astype(f32) + down[:BLOCK].astype(f32)).astype(bf16), -1)
        here = shard[low * BLOCK : (low + 2) * BLOCK].astype(f32) + own_part.astype(f32)
        results.append(here[:BLOCK] + plus_a.astype(f32) + down[BLOCK:].astype(f32))
        results.append(here[BLOCK:] + up[BLOCK:].astype(f32) + minus_b.astype(f32))
    return jnp.concatenate(results, axis=0).astype(bf16), columns


def permuted(x, source):
    pick = (source[:, None] == jnp.arange(x.shape[0])[None, :]).astype(bf16)
    return jnp.dot(pick, x, preferred_element_type=f32).astype(bf16)


def body(
    tokens,
    col_order,
    in_gain,
    w_in,
    w_bc,
    w_dt,
    conv_x,
    conv_bc,
    dt_bias,
    a_log,
    d_skip,
    out_gain,
    w_out,
):
    first = with_halo(tokens, 2 * BLOCK)
    arguments = (in_gain, w_in, w_dt, conv_x, conv_bc, dt_bias, a_log, d_skip, out_gain, col_order)
    in_gain, w_in, w_dt, conv_x, conv_bc, dt_bias, a_log, d_skip, out_gain, col_order = behind(
        arguments, first
    )
    x = lax.axis_index("tp")
    core, y, z = (lax.axis_index(a) for a in ("seq_2", "seq_1", "seq_0"))
    place = jnp.stack([x, (x + 3) & 3, (x + 1) & 3, (x + 2) & 3, core, y, z]).astype(jnp.int32)
    w = w_in.reshape(2, 2048, 2 * LANES)

    def on_lanes(heads):
        return jnp.broadcast_to(heads[:, None], (HEADS, STRETCH))

    def params(which):
        return (
            in_gain[which].reshape(TP, 1, 512),
            w_dt[which].T.reshape(HEADS, TP, 512).transpose(1, 0, 2),
            jnp.concatenate([conv_x[which], conv_bc[which]], axis=1),
            on_lanes(dt_bias[which]),
            on_lanes(a_log[which]),
            on_lanes(d_skip[which]),
            out_gain[which].reshape(1, LANES),
        )

    starts = col_order.reshape(16, 64)[:, 0]
    slot = jnp.arange(512)
    columns = jnp.where(
        slot // 16 == lax.axis_index(SEQ), jnp.tile(starts % 512, 32), 0
    ).reshape(2, 256)
    columns = jnp.stack([columns[0] // 2, columns[0] % 2, columns[1] // 2, columns[1] % 2])
    columns = jnp.pad(columns.astype(f32), ((0, 4), (0, 0)))
    visit = jnp.arange(16)[:, None]
    along = jnp.arange(64)[None, :]
    row = jnp.where((starts >= 512)[:, None], 63 - along, along)
    take = ((row // 2) * 32 + (row % 2) * 16 + visit).reshape(1024)
    place, small, w, columns, take = lax.optimization_barrier(
        (place, [params(0), params(1)], w, columns, take)
    )
    large = (w, w_bc, w_out)

    row_result, columns = layer(0, tokens, first, place, small[0], large, columns, (w,))
    payload = given(columns, row_result)
    arrived = lax.all_to_all(payload, SEQ, 0, 0, tiled=True).reshape(1024, 512)
    own_rows = permuted(arrived, take)
    return layer(1, own_rows, with_halo(own_rows, BLOCK), place, small[1], large, columns)[0]


def solution(mesh):
    torus = Mesh(mesh.devices.reshape(4, 4, 2, mesh.shape["tp"]), ("seq_0", "seq_1", "seq_2", "tp"))
    return jax.shard_map(
        body,
        mesh=torus,
        in_specs=(
            P(SEQ, "tp"),
            P(SEQ),
            P(),
            P(None, None, None, "tp"),
            P(),
            P(None, None, "tp"),
            P(None, None, "tp"),
            P(),
            P(None, "tp"),
            P(None, "tp"),
            P(None, "tp"),
            P(None, "tp"),
            P(None, "tp", None),
        ),
        out_specs=P(SEQ, "tp"),
        check_vma=False,
    )
```

```python
import functools

import jax
import jax.numpy as jnp
from jax import lax
from jax.experimental import pallas as pl
from jax.experimental.pallas import tpu as pltpu
from jax.sharding import Mesh
from jax.sharding import PartitionSpec as P

HEAD_DIM = 64
STATE = 128
STRETCH = 128
HEADS = 8
LANES = 512
HALF = 256
HALO = 16
BLOCK = 256
MSG = 144
SEQ = ("seq_0", "seq_1", "seq_2")
TP = 4
epsilon = 1e-05
f32 = jnp.float32
bf16 = jnp.bfloat16
NT = (((1,), (1,)), ((), ()))
TN = (((0,), (0,)), ((), ()))
MIB = 2**20


def dot(a, b, dims=None):
    dims = dims or (((1,), (0,)), ((), ()))
    return lax.dot_general(a, b, dims, preferred_element_type=f32)


def silu(x):
    return x / (1.0 + jnp.exp(-x))


def softplus(x):
    return jnp.maximum(x, 0.0) + jnp.log1p(jnp.exp(-jnp.abs(x)))


def spread_heads(values, fan):
    high = values.astype(bf16)
    low = (values - high.astype(f32)).astype(bf16)
    return dot(jnp.concatenate([high, low], axis=0), fan, TN)


def packed(state, decay, columns):
    high = decay.astype(bf16).astype(f32)
    row = lax.broadcasted_iota(jnp.int32, (8, decay.shape[1]), 0)
    rest = jnp.where(row == 0, high, jnp.where(row == 1, decay - high, 0.0))
    return jnp.concatenate([state, columns, rest], axis=0)


def opened(msg):
    msg = msg[...].astype(f32)
    at = STATE + 8
    return msg[:STATE], msg[at : at + 1] + msg[at + 1 : at + 2]


def columns_in(msg):
    return msg[...].astype(f32)[STATE : STATE + 8]


def after(a, b):
    return b[0] + b[1] * a[0], a[1] * b[1]


def chosen(pred, a, b):
    return jnp.where(pred, a[0], b[0]), jnp.where(pred, a[1], b[1])


def nothing():
    return jnp.zeros((STATE, HALF), f32), jnp.ones((1, HALF), f32)


def head_fan():
    row = lax.broadcasted_iota(jnp.int32, (2 * HEADS, LANES), 0)
    lane = lax.broadcasted_iota(jnp.int32, (2 * HEADS, LANES), 1)
    return (row % HEADS == lane // HEAD_DIM).astype(bf16)


def entry_kernel(first, last, offset, rows, apart, *refs):
    (order, own, left, right, opposite) = refs[:5]
    halos, refs = refs[5 : 5 + apart], refs[5 + apart :]
    columns = ()
    if last:
        columns, refs = refs[:1], refs[1:]
    if not first:
        tail_in, state_in, total_in, refs = *refs[:3], refs[3:]
    (gain, wv, wbcv, wdt, taps, dt_bias, a_log), refs = refs[:7], refs[7:]
    (z_out, xc_out, b_out, c_out, cum_out, step_out, ent_out, pri_out), refs = refs[:8], refs[8:]
    if last:
        (keep_out, send_out), refs = refs[:2], refs[2:]
        columns = columns[0]
    else:
        (tail_out, state_out, total_out), refs = refs[:3], refs[3:]
    nbuf, xbuf = refs

    fan = head_fan()
    k_pos = lax.broadcasted_iota(jnp.int32, (STRETCH, STRETCH), 0)
    q_pos = lax.broadcasted_iota(jnp.int32, (STRETCH, STRETCH), 1)
    upto = (k_pos <= q_pos).astype(f32)
    lane = lax.broadcasted_iota(jnp.int32, (HEADS, STRETCH), 1)
    rate = jnp.exp(a_log[:, 0:1])
    if first:
        state = jnp.zeros((STATE, LANES), f32)
        total = jnp.zeros((HEADS, 1), f32)
    else:
        state = state_in[...]
        total = total_in[:, 0:1]
        xbuf[0:HALO, :] = tail_in[...]
    for i in range(rows // BLOCK):
        span = pl.ds(i * BLOCK, BLOCK)
        above = pl.ds(offset + i * BLOCK, BLOCK)
        pieces = [r[above, :] for r in (own, left, right, opposite)]
        widen = [x.astype(f32) for x in pieces]
        square = sum(jnp.sum(x * x, axis=1, keepdims=True) for x in widen)
        scale = lax.rsqrt(square * (1.0 / 2048) + epsilon)
        for p in range(4):
            nbuf[HALO : HALO + BLOCK, p * 512 : (p + 1) * 512] = (
                widen[p] * scale * gain[order[p]]
            ).astype(bf16)
        if first and i == 0:
            sources = halos or (own, left, right, opposite)
            widen = [r[0:HALO, :].astype(f32) for r in sources]
            square = sum(jnp.sum(x * x, axis=1, keepdims=True) for x in widen)
            scale = lax.rsqrt(square * (1.0 / 2048) + epsilon)
            for p in range(4):
                nbuf[0:HALO, p * 512 : (p + 1) * 512] = (
                    widen[p] * scale * gain[order[p]]
                ).astype(bf16)
        low = 0 if first and i == 0 else HALO
        if low and i > 0:
            xbuf[0:HALO, :] = xbuf[BLOCK : BLOCK + HALO, :]
        normed = nbuf[low : HALO + BLOCK, :]
        xbuf[low : HALO + BLOCK, 0:LANES] = dot(normed, wv[:, 0:LANES]).astype(bf16).astype(f32)
        z_out[span, :] = dot(nbuf[HALO:, :], wv[:, LANES:]).astype(bf16)
        xbuf[low : HALO + BLOCK, LANES:] = dot(normed, wbcv[...]).astype(bf16).astype(f32)
        dt = sum(
            dot(wdt[order[p]], nbuf[HALO:, p * 512 : (p + 1) * 512], NT) for p in range(4)
        )
        mixed = jnp.zeros((BLOCK, LANES + 2 * STATE), f32)
        for k in range(4):
            mixed = mixed + taps[k : k + 1, :] * xbuf[pl.ds(HALO - 3 + k, BLOCK), :]
        mixed = silu(mixed)
        xc = mixed[:, 0:LANES]
        b = mixed[:, LANES : LANES + STATE].astype(bf16)
        xc_out[span, :] = xc.astype(bf16)
        b_out[span, :] = b
        c_out[span, :] = mixed[:, LANES + STATE :].astype(bf16)
        step = softplus(dt + dt_bias[:, 0:1])
        decay = -step * rate
        step_out[:, i * BLOCK : (i + 1) * BLOCK] = step
        cums, marks = [], jnp.zeros((HEADS, STRETCH), f32)
        for j in range(2):
            part = decay[:, j * STRETCH : (j + 1) * STRETCH]
            cum = lax.dot_general(
                part,
                upto,
                (((1,), (0,)), ((), ())),
                preferred_element_type=f32,
                precision=lax.Precision.HIGHEST,
            )
            cum_out[:, i * BLOCK + j * STRETCH : i * BLOCK + (j + 1) * STRETCH] = cum
            end = cum[:, STRETCH - 1 : STRETCH]
            marks = jnp.where(lane == j, end, jnp.where(lane == 2 + j, total, marks))
            total = total + end
            cums.append((cum, end))
        marks = jnp.where(lane == 4, total, marks)
        marks = spread_heads(jnp.exp(marks), fan)
        for j in range(2):
            cum, end = cums[j]
            here = slice(j * STRETCH, (j + 1) * STRETCH)
            weight = spread_heads(step[:, here] * jnp.exp(end - cum), fan)
            fresh = dot(b[here, :], (xc[here, :] * weight).astype(bf16), TN)
            ent_out[2 * i + j] = state
            pri_out[2 * i + j] = marks[2 + j : 3 + j, :]
            state = state * marks[j : j + 1, :] + fresh
    if last:
        decayed = marks[4:5, :]
        near = packed(state[:, 0:HALF], decayed[:, 0:HALF], columns[...])
        far = packed(state[:, HALF:], decayed[:, HALF:], columns[...])
        even = order[4] == 0
        keep_out[...] = jnp.where(even, near, far).astype(bf16)
        send_out[...] = jnp.where(even, far, near).astype(bf16)
    else:
        tail_out[...] = xbuf[BLOCK : BLOCK + HALO, :]
        state_out[...] = state
        total_out[...] = jnp.broadcast_to(total, (HEADS, STRETCH))


def stage_kernel(which, order, w, wbc, w_out, wbc_out, sems):
    copies = []
    for p in range(4):
        source = pl.ds(pl.multiple_of(order[p] * 512, 512), 512)
        target = pl.ds(p * 512, 512)
        copies.append(
            pltpu.make_async_copy(w.at[which, source, :], w_out.at[target, :], sems.at[0, p])
        )
        copies.append(
            pltpu.make_async_copy(wbc.at[which, source, :], wbc_out.at[target, :], sems.at[1, p])
        )
    for c in copies:
        c.start()
    for c in copies:
        c.wait()


def staged(which, order, w, wbc):
    return pl.pallas_call(
        functools.partial(stage_kernel, which),
        out_shape=[pltpu.VMEM((2048, 2 * LANES), bf16), pltpu.VMEM((2048, 2 * STATE), bf16)],
        in_specs=[smem(), in_hbm(), in_hbm()],
        out_specs=[vmem()] * 2,
        scratch_shapes=[pltpu.SemaphoreType.DMA((2, 4))],
        compiler_params=pltpu.CompilerParams(vmem_limit_bytes=2 * MIB),
        name="stage",
    )(order, kept_in_hbm(w), kept_in_hbm(wbc))


def stage_out_kernel(which, order, w, out, sems):
    copies = []
    for p in range(4):
        source = pl.ds(pl.multiple_of(order[(0, 2, 1, 3)[p]] * 512, 512), 512)
        copies.append(pltpu.make_async_copy(w.at[which, :, source], out.at[p], sems.at[p]))
    for c in copies:
        c.start()
    for c in copies:
        c.wait()


def staged_out(which, order, w):
    return pl.pallas_call(
        functools.partial(stage_out_kernel, which),
        out_shape=pltpu.VMEM((4, LANES, LANES), bf16),
        in_specs=[smem(), in_hbm()],
        out_specs=vmem(),
        scratch_shapes=[pltpu.SemaphoreType.DMA((4,))],
        compiler_params=pltpu.CompilerParams(vmem_limit_bytes=2 * MIB),
        name="stage_out",
    )(order, kept_in_hbm(w))


def vmem():
    return pl.BlockSpec(memory_space=pltpu.VMEM)


def smem():
    return pl.BlockSpec(memory_space=pltpu.SMEM)


def in_hbm():
    return pl.BlockSpec(memory_space=pltpu.HBM)


def kept_in_hbm(x):
    return pltpu.with_memory_space_constraint(x, pltpu.HBM)


def entry(order, pieces, halos, offset, columns, carry, gain, w, wbc, wdt, taps, dt_bias, a_log, last):
    first = carry is None
    rows = BLOCK
    shape = jax.ShapeDtypeStruct
    outs = [
        pltpu.VMEM((rows, LANES), bf16),
        pltpu.VMEM((rows, LANES), bf16),
        pltpu.VMEM((rows, STATE), bf16),
        pltpu.VMEM((rows, STATE), bf16),
        pltpu.VMEM((HEADS, rows), f32),
        pltpu.VMEM((HEADS, rows), f32),
        pltpu.VMEM((rows // STRETCH, STATE, LANES), f32),
        pltpu.VMEM((rows // STRETCH, 1, LANES), f32),
    ]
    if last:
        outs += [shape((MSG, HALF), bf16)] * 2
    else:
        outs += [
            pltpu.VMEM((HALO, LANES + 2 * STATE), f32),
            pltpu.VMEM((STATE, LANES), f32),
            pltpu.VMEM((HEADS, STRETCH), f32),
        ]
    extra = [] if first else list(carry)
    operands = [order, *pieces, *halos, *([columns] if last else []), *extra, gain, w, wbc, wdt, taps, dt_bias, a_log]
    specs = [smem()] + [vmem()] * (len(operands) - 1)
    return pl.pallas_call(
        functools.partial(entry_kernel, first, last, offset, rows, len(halos)),
        out_shape=outs,
        in_specs=specs,
        out_specs=[vmem()] * len(outs),
        scratch_shapes=[
            pltpu.VMEM((HALO + BLOCK, 2048), bf16),
            pltpu.VMEM((HALO + BLOCK, LANES + 2 * STATE), f32),
        ],
        compiler_params=pltpu.CompilerParams(vmem_limit_bytes=8 * MIB),
        name="entry",
    )(*operands)


def inside_kernel(rows, xc, b, c, cum, step, skip, y_out):
    q_pos = lax.broadcasted_iota(jnp.int32, (STRETCH, STRETCH), 0)
    k_pos = lax.broadcasted_iota(jnp.int32, (STRETCH, STRETCH), 1)
    causal = k_pos <= q_pos
    low_half = k_pos < HEAD_DIM
    skips = spread_heads(skip[...], head_fan())[0:1, :]
    for j in range(rows // STRETCH):
        here = slice(j * STRETCH, (j + 1) * STRETCH)
        match = jnp.where(causal, dot(c[here, :], b[here, :], NT), 0.0)
        cum_rows = cum[:, here]
        step_rows = step[:, here]
        cum_cols = jnp.transpose(cum_rows)
        for pair in range(HEADS // 2):
            weights = []
            for h in (2 * pair, 2 * pair + 1):
                gap = jnp.minimum(cum_cols[:, h : h + 1] - cum_rows[h : h + 1, :], 0.0)
                weights.append((match * (jnp.exp(gap) * step_rows[h : h + 1, :])).astype(bf16))
            lanes = slice(pair * STRETCH, (pair + 1) * STRETCH)
            x = xc[here, lanes].astype(f32)
            stacked = jnp.concatenate(
                [jnp.where(low_half, x, 0.0), jnp.where(low_half, 0.0, x)], axis=0
            ).astype(bf16)
            y_out[here, lanes] = (
                dot(jnp.concatenate(weights, axis=1), stacked) + skips[:, lanes] * x
            )


def inside(xc, b, c, cum, step, skip):
    rows = xc.shape[0]
    return pl.pallas_call(
        functools.partial(inside_kernel, rows),
        out_shape=pltpu.VMEM((rows, LANES), f32),
        in_specs=[vmem()] * 6,
        out_specs=vmem(),
        compiler_params=pltpu.CompilerParams(vmem_limit_bytes=4 * MIB),
        name="inside",
    )(xc, b, c, cum, step, skip)


def exit_kernel(chunks, order, mine, other, gain, wv, *refs):
    parts = [refs[6 * i : 6 * i + 6] for i in range(chunks)]
    own, up, down, plus_a, minus_b = refs[6 * chunks :]
    split = chunks * BLOCK // 2
    outs = (((plus_a, 0), (up, split)), ((down, split), (minus_b, 0)), ((up, 0), (down, 0)))
    fan = head_fan()
    row = lax.broadcasted_iota(jnp.int32, (BLOCK, BLOCK), 0) // HEAD_DIM
    lane = lax.broadcasted_iota(jnp.int32, (BLOCK, BLOCK), 1) // HEAD_DIM
    same_head = (row == lane).astype(bf16)
    here, there = mine[...].astype(f32), other[...].astype(f32)
    even = order[4] == 0
    came = jnp.concatenate([jnp.where(even, here, there), jnp.where(even, there, here)], axis=1)
    for i in range(chunks):
        y, z, c, cum, ent, pri = parts[i]
        mixed = []
        for j in range(2):
            here = slice(j * STRETCH, (j + 1) * STRETCH)
            entering = (ent[j] + pri[j] * came).astype(bf16)
            carried = dot(c[here, :], entering) * spread_heads(jnp.exp(cum[:, here]), fan)
            gated = (y[here, :] + carried) * silu(z[here, :].astype(f32))
            square = (gated * gated).astype(bf16)
            sums = jnp.concatenate(
                [dot(square[:, 0:BLOCK], same_head), dot(square[:, BLOCK:], same_head)], axis=1
            )
            scale = lax.rsqrt(sums * (1.0 / HEAD_DIM) + epsilon)
            mixed.append((gated * scale * gain[...]).astype(bf16))
        mixed = jnp.concatenate(mixed, axis=0)
        own[i * BLOCK : (i + 1) * BLOCK, :] = dot(mixed, wv[0]).astype(bf16)
        for p in range(3):
            product = dot(mixed, wv[p + 1]).astype(bf16)
            for j in range(2):
                at = i * BLOCK + j * STRETCH
                out, base = outs[p][at // split]
                at = base + at % split
                out[at : at + STRETCH, :] = product[j * STRETCH : (j + 1) * STRETCH, :]


def leave(order, mine, other, gain, w, parts):
    rows = len(parts) * BLOCK
    shape = jax.ShapeDtypeStruct
    outs = [shape((rows, LANES), bf16)] * 3 + [shape((rows // 2, LANES), bf16)] * 2
    operands = [order, mine, other, gain, w, *(a for part in parts for a in part)]
    return pl.pallas_call(
        functools.partial(exit_kernel, len(parts)),
        out_shape=outs,
        in_specs=[smem()] + [vmem()] * (len(operands) - 1),
        out_specs=[vmem()] * len(outs),
        compiler_params=pltpu.CompilerParams(vmem_limit_bytes=6 * MIB),
        name="leave",
    )(*operands)


def small_call(kernel, name, outs, place, *operands):
    return pl.pallas_call(
        kernel,
        out_shape=outs,
        in_specs=[smem()] + [vmem()] * len(operands),
        out_specs=[vmem()] * len(outs),
        compiler_params=pltpu.CompilerParams(vmem_limit_bytes=2 * MIB),
        name=name,
    )(place, *operands)


def chip_kernel(place, keep, got, out):
    even = place[4] == 0
    mine, other = opened(keep), opened(got)
    both = after(chosen(even, mine, other), chosen(even, other, mine))
    out[...] = packed(*both, columns_in(keep) + columns_in(got)).astype(bf16)


def row_kernel(place, chip, one, two, three, row_out, before_out):
    y = place[5]
    ring = [opened(r) for r in (chip, one, two, three)]
    row, before = nothing(), nothing()
    for at in range(4):
        here = ring[0]
        for k in range(1, 4):
            here = chosen((y + 4 - at) % 4 == k, ring[k], here)
        before = chosen(at < y, after(before, here), before)
        row = after(row, here)
    columns = sum(columns_in(r) for r in (chip, one, two, three))
    row_out[...] = packed(*row, columns).astype(bf16)
    before_out[...] = packed(*before, columns)


def arrive_kernel(place, one, two, three, before, keep, got, mine_out, other_out, columns_out):
    even = place[4] == 0
    z = place[6]
    came = nothing()
    for k, r in ((3, three), (2, two), (1, one)):
        came = chosen(z >= k, after(came, opened(r)), came)
    first = after(came, opened(before))
    second = after(first, chosen(even, opened(keep), opened(got)))
    mine_out[...] = jnp.where(even, first[0], second[0]).astype(bf16)
    other_out[...] = jnp.where(even, second[0], first[0]).astype(bf16)
    columns_out[...] = sum(columns_in(r) for r in (before, one, two, three))


def give_kernel(columns, x, out):
    cell = lax.broadcasted_iota(jnp.int32, (512, HALF), 0)
    for part in range(2):
        wanted = 2.0 * columns[2 * part : 2 * part + 1, :] + columns[2 * part + 1 : 2 * part + 2, :]
        pick = (cell == wanted.astype(jnp.int32)).astype(bf16)
        for r in range(2):
            rows = dot(pick, x[r * 512 : (r + 1) * 512, :], TN).astype(bf16)
            out[part * 16 : (part + 1) * 16, r * 16 : (r + 1) * 16, :] = rows.reshape(16, 16, 512)


def given(columns, x):
    return pl.pallas_call(
        give_kernel,
        out_shape=jax.ShapeDtypeStruct((32, 32, 512), bf16),
        in_specs=[vmem()] * 2,
        out_specs=vmem(),
        compiler_params=pltpu.CompilerParams(vmem_limit_bytes=6 * MIB),
        name="give",
    )(columns, x)


def turned(by):
    return [(i, (i + by) % TP) for i in range(TP)]


def around(x, by):
    return lax.ppermute(x, "tp", turned(by))


def swapped(x):
    return lax.ppermute(x, "seq_2", [(0, 1), (1, 0)])


def arriving_state(place, keep, send, weights, beside, wrapped):
    shape = jax.ShapeDtypeStruct
    got = swapped(send)
    msg = shape((MSG, HALF), bf16)
    (chip,) = small_call(chip_kernel, "chip", [msg], place, keep, got)
    ring = [lax.ppermute(chip, "seq_1", turned(k)) for k in (1, 2, 3)]
    row, before = small_call(
        row_kernel,
        "row",
        [msg, shape((MSG, HALF), f32)],
        behind(place, weights),
        chip,
        *ring,
    )
    earlier = [
        lax.ppermute(row, "seq_0", turned(k)[: 4 if wrapped else 4 - k]) for k in (1, 2, 3)
    ]
    mine, other, columns = small_call(
        arrive_kernel,
        "arrive",
        [shape((STATE, HALF), bf16)] * 2 + [shape((8, HALF), f32)],
        behind(place, *beside),
        *earlier,
        before,
        keep,
        got,
    )
    return mine, swapped(other), columns


def behind(x, *done):
    return lax.optimization_barrier((x, *done))[0]


def halo_from(rows, by):
    pairs = [
        (s * TP + t, (s + 1) * TP + (t + by) % TP)
        for s in range(lax.axis_size(SEQ) - 1)
        for t in range(TP)
    ]
    return lax.ppermute(rows, SEQ + ("tp",), pairs)


def with_halo(shard, count):
    pairs = [(i, i + 1) for i in range(lax.axis_size(SEQ) - 1)]
    return jnp.concatenate([lax.ppermute(shard[-HALO:], SEQ, pairs), shard[:count]], axis=0)


def layer(which, shard, first, place, params, large, columns, early=()):
    gain, wdt, taps, dt_bias, a_log, skip, out_gain = params
    w, wbc, w_out = large
    rows = [shard[i * BLOCK : (i + 1) * BLOCK] for i in range(shard.shape[0] // BLOCK)]
    wv, wbcv = staged(which, behind(place, first), w, wbc)
    carry, kept, gate = None, [], place

    def enter(i, pieces, offset=0, halos=()):
        nonlocal carry, gate
        out = entry(
            gate, pieces, halos, offset, columns, carry, gain, wv, wbcv, wdt, taps, dt_bias, a_log, i == 3
        )
        z, xc, b, c, cum, step, ent, pri = out[:8]
        carry = out[8:]
        y = inside(xc, b, c, cum, step, skip)
        kept.append((y, z, c, cum, ent, pri))
        if i < 2:
            gate = behind(place, y)

    if which == 0:
        own = [first, behind(rows[2], first), behind(rows[3], first)]
        left, right = [around(first, 1)], [around(first, -1)]
        right.append(around(own[1], -1))
        opposite = [around(behind(left[0], *early), 1)]
        right.append(around(own[2], -1))
        left.append(around(behind(rows[2], right[1]), 1))
        opposite.append(around(right[1], -1))
        pieces = (own[0], left[0], right[0], opposite[0])
        enter(0, pieces, HALO)
        left.append(around(behind(rows[3], carry[0]), 1))
        opposite.append(around(behind(right[2], carry[0]), -1))
        enter(1, pieces, HALO + BLOCK)
        for i in (1, 2):
            enter(i + 1, (own[i], left[i], right[i], opposite[i]))
    else:
        own = [first, behind(rows[1], first), behind(rows[2], first)]
        left, right = [around(x, 1) for x in own], [around(x, -1) for x in own]
        opposite = [around(behind(left[0], wbcv), 1)]
        tail = behind(shard[-HALO:], wbcv)
        halos = [halo_from(tail, by) for by in (0, 1, -1, 2)]
        enter(0, (own[0], left[0], right[0], opposite[0]), 0, halos)
        own.append(behind(rows[3], first, carry[0]))
        left.append(around(own[3], 1))
        right.append(around(own[3], -1))
        opposite.append(around(right[1], -1))
        enter(1, (own[1], left[1], right[1], opposite[1]))
        opposite.append(around(left[2], 1))
        opposite.append(around(behind(right[3], carry[0]), -1))
        for i in (2, 3):
            enter(i, (own[i], left[i], right[i], opposite[i]))
    wov = staged_out(which, behind(place, carry[0]), w_out)
    mine, other, columns = arriving_state(
        place, *carry, wov, [k[0] for k in kept], which == 0
    )
    results = []
    for low in (0, 2):
        own_part, up, down, plus_a, minus_b = leave(
            place, mine, other, out_gain, wov, kept[low : low + 2]
        )
        up, down = around(up, 1), around(down, -1)
        plus_a = around((plus_a.astype(f32) + up[:BLOCK].astype(f32)).astype(bf16), 1)
        minus_b = around((minus_b.astype(f32) + down[:BLOCK].astype(f32)).astype(bf16), -1)
        here = shard[low * BLOCK : (low + 2) * BLOCK].astype(f32) + own_part.astype(f32)
        results.append(here[:BLOCK] + plus_a.astype(f32) + down[BLOCK:].astype(f32))
        results.append(here[BLOCK:] + up[BLOCK:].astype(f32) + minus_b.astype(f32))
    return jnp.concatenate(results, axis=0).astype(bf16), columns


def permuted(x, source):
    pick = (source[:, None] == jnp.arange(x.shape[0])[None, :]).astype(bf16)
    return jnp.dot(pick, x, preferred_element_type=f32).astype(bf16)


def body(
    tokens,
    col_order,
    in_gain,
    w_in,
    w_bc,
    w_dt,
    conv_x,
    conv_bc,
    dt_bias,
    a_log,
    d_skip,
    out_gain,
    w_out,
):
    first = with_halo(tokens, 2 * BLOCK)
    arguments = (in_gain, w_in, w_dt, conv_x, conv_bc, dt_bias, a_log, d_skip, out_gain, col_order)
    in_gain, w_in, w_dt, conv_x, conv_bc, dt_bias, a_log, d_skip, out_gain, col_order = behind(
        arguments, first
    )
    x = lax.axis_index("tp")
    core, y, z = (lax.axis_index(a) for a in ("seq_2", "seq_1", "seq_0"))
    place = jnp.stack([x, (x + 3) & 3, (x + 1) & 3, (x + 2) & 3, core, y, z]).astype(jnp.int32)
    w = w_in.reshape(2, 2048, 2 * LANES)

    def on_lanes(heads):
        return jnp.broadcast_to(heads[:, None], (HEADS, STRETCH))

    def params(which):
        return (
            in_gain[which].reshape(TP, 1, 512),
            w_dt[which].T.reshape(HEADS, TP, 512).transpose(1, 0, 2),
            jnp.concatenate([conv_x[which], conv_bc[which]], axis=1),
            on_lanes(dt_bias[which]),
            on_lanes(a_log[which]),
            on_lanes(d_skip[which]),
            out_gain[which].reshape(1, LANES),
        )

    starts = col_order.reshape(16, 64)[:, 0]
    slot = jnp.arange(512)
    columns = jnp.where(
        slot // 16 == lax.axis_index(SEQ), jnp.tile(starts % 512, 32), 0
    ).reshape(2, 256)
    columns = jnp.stack([columns[0] // 2, columns[0] % 2, columns[1] // 2, columns[1] % 2])
    columns = jnp.pad(columns.astype(f32), ((0, 4), (0, 0)))
    visit = jnp.arange(16)[:, None]
    along = jnp.arange(64)[None, :]
    row = jnp.where((starts >= 512)[:, None], 63 - along, along)
    take = ((row // 2) * 32 + (row % 2) * 16 + visit).reshape(1024)
    place, small, w, columns, take = lax.optimization_barrier(
        (place, [params(0), params(1)], w, columns, take)
    )
    large = (w, w_bc, w_out)

    row_result, columns = layer(0, tokens, first, place, small[0], large, columns, (w,))
    payload = given(columns, row_result)
    arrived = lax.all_to_all(payload, SEQ, 0, 0, tiled=True).reshape(1024, 512)
    own_rows = permuted(arrived, take)
    return layer(1, own_rows, own_rows[:BLOCK], place, small[1], large, columns)[0]


def solution(mesh):
    torus = Mesh(mesh.devices.reshape(4, 4, 2, mesh.shape["tp"]), ("seq_0", "seq_1", "seq_2", "tp"))
    return jax.shard_map(
        body,
        mesh=torus,
        in_specs=(
            P(SEQ, "tp"),
            P(SEQ),
            P(),
            P(None, None, None, "tp"),
            P(),
            P(None, None, "tp"),
            P(None, None, "tp"),
            P(),
            P(None, "tp"),
            P(None, "tp"),
            P(None, "tp"),
            P(None, "tp"),
            P(None, "tp", None),
        ),
        out_specs=P(SEQ, "tp"),
        check_vma=False,
    )
```

```python
import functools

import jax
import jax.numpy as jnp
from jax import lax
from jax.experimental import pallas as pl
from jax.experimental.pallas import tpu as pltpu
from jax.sharding import Mesh
from jax.sharding import PartitionSpec as P

HEAD_DIM = 64
STATE = 128
STRETCH = 128
HEADS = 8
LANES = 512
HALF = 256
HALO = 16
BLOCK = 256
MSG = 144
SEQ = ("seq_0", "seq_1", "seq_2")
TP = 4
epsilon = 1e-05
f32 = jnp.float32
bf16 = jnp.bfloat16
NT = (((1,), (1,)), ((), ()))
TN = (((0,), (0,)), ((), ()))
MIB = 2**20


def dot(a, b, dims=None):
    dims = dims or (((1,), (0,)), ((), ()))
    return lax.dot_general(a, b, dims, preferred_element_type=f32)


def silu(x):
    return x / (1.0 + jnp.exp(-x))


def softplus(x):
    return jnp.maximum(x, 0.0) + jnp.log1p(jnp.exp(-jnp.abs(x)))


def spread_heads(values, fan):
    high = values.astype(bf16)
    low = (values - high.astype(f32)).astype(bf16)
    return dot(jnp.concatenate([high, low], axis=0), fan, TN)


def packed(state, decay, columns):
    high = decay.astype(bf16).astype(f32)
    row = lax.broadcasted_iota(jnp.int32, (8, decay.shape[1]), 0)
    rest = jnp.where(row == 0, high, jnp.where(row == 1, decay - high, 0.0))
    return jnp.concatenate([state, columns, rest], axis=0)


def opened(msg):
    msg = msg[...].astype(f32)
    at = STATE + 8
    return msg[:STATE], msg[at : at + 1] + msg[at + 1 : at + 2]


def columns_in(msg):
    return msg[...].astype(f32)[STATE : STATE + 8]


def after(a, b):
    return b[0] + b[1] * a[0], a[1] * b[1]


def chosen(pred, a, b):
    return jnp.where(pred, a[0], b[0]), jnp.where(pred, a[1], b[1])


def nothing():
    return jnp.zeros((STATE, HALF), f32), jnp.ones((1, HALF), f32)


def head_fan():
    row = lax.broadcasted_iota(jnp.int32, (2 * HEADS, LANES), 0)
    lane = lax.broadcasted_iota(jnp.int32, (2 * HEADS, LANES), 1)
    return (row % HEADS == lane // HEAD_DIM).astype(bf16)


def entry_kernel(first, last, offset, rows, *refs):
    (order, own, left, right, opposite) = refs[:5]
    refs = refs[5:]
    columns = ()
    if last:
        columns, refs = refs[:1], refs[1:]
    if not first:
        tail_in, state_in, total_in, refs = *refs[:3], refs[3:]
    (gain, wv, wbcv, wdt, taps, dt_bias, a_log), refs = refs[:7], refs[7:]
    (z_out, xc_out, b_out, c_out, cum_out, step_out, ent_out, pri_out), refs = refs[:8], refs[8:]
    if last:
        (keep_out, send_out), refs = refs[:2], refs[2:]
        columns = columns[0]
    else:
        (tail_out, state_out, total_out), refs = refs[:3], refs[3:]
    nbuf, xbuf = refs

    fan = head_fan()
    k_pos = lax.broadcasted_iota(jnp.int32, (STRETCH, STRETCH), 0)
    q_pos = lax.broadcasted_iota(jnp.int32, (STRETCH, STRETCH), 1)
    upto = (k_pos <= q_pos).astype(f32)
    lane = lax.broadcasted_iota(jnp.int32, (HEADS, STRETCH), 1)
    rate = jnp.exp(a_log[:, 0:1])
    if first:
        state = jnp.zeros((STATE, LANES), f32)
        total = jnp.zeros((HEADS, 1), f32)
    else:
        state = state_in[...]
        total = total_in[:, 0:1]
        xbuf[0:HALO, :] = tail_in[...]
    for i in range(rows // BLOCK):
        span = pl.ds(i * BLOCK, BLOCK)
        above = pl.ds(offset + i * BLOCK, BLOCK)
        pieces = [r[above, :] for r in (own, left, right, opposite)]
        widen = [x.astype(f32) for x in pieces]
        square = sum(jnp.sum(x * x, axis=1, keepdims=True) for x in widen)
        scale = lax.rsqrt(square * (1.0 / 2048) + epsilon)
        for p in range(4):
            nbuf[HALO : HALO + BLOCK, p * 512 : (p + 1) * 512] = (
                widen[p] * scale * gain[order[p]]
            ).astype(bf16)
        if first and i == 0:
            widen = [r[0:HALO, :].astype(f32) for r in (own, left, right, opposite)]
            square = sum(jnp.sum(x * x, axis=1, keepdims=True) for x in widen)
            scale = lax.rsqrt(square * (1.0 / 2048) + epsilon)
            for p in range(4):
                nbuf[0:HALO, p * 512 : (p + 1) * 512] = (
                    widen[p] * scale * gain[order[p]]
                ).astype(bf16)
        low = 0 if first and i == 0 else HALO
        if low and i > 0:
            xbuf[0:HALO, :] = xbuf[BLOCK : BLOCK + HALO, :]
        normed = nbuf[low : HALO + BLOCK, :]
        xbuf[low : HALO + BLOCK, 0:LANES] = dot(normed, wv[:, 0:LANES]).astype(bf16).astype(f32)
        z_out[span, :] = dot(nbuf[HALO:, :], wv[:, LANES:]).astype(bf16)
        xbuf[low : HALO + BLOCK, LANES:] = dot(normed, wbcv[...]).astype(bf16).astype(f32)
        dt = sum(
            dot(wdt[order[p]], nbuf[HALO:, p * 512 : (p + 1) * 512], NT) for p in range(4)
        )
        mixed = jnp.zeros((BLOCK, LANES + 2 * STATE), f32)
        for k in range(4):
            mixed = mixed + taps[k : k + 1, :] * xbuf[pl.ds(HALO - 3 + k, BLOCK), :]
        mixed = silu(mixed)
        xc = mixed[:, 0:LANES]
        b = mixed[:, LANES : LANES + STATE].astype(bf16)
        xc_out[span, :] = xc.astype(bf16)
        b_out[span, :] = b
        c_out[span, :] = mixed[:, LANES + STATE :].astype(bf16)
        step = softplus(dt + dt_bias[:, 0:1])
        decay = -step * rate
        step_out[:, i * BLOCK : (i + 1) * BLOCK] = step
        cums, marks = [], jnp.zeros((HEADS, STRETCH), f32)
        for j in range(2):
            part = decay[:, j * STRETCH : (j + 1) * STRETCH]
            cum = lax.dot_general(
                part,
                upto,
                (((1,), (0,)), ((), ())),
                preferred_element_type=f32,
                precision=lax.Precision.HIGHEST,
            )
            cum_out[:, i * BLOCK + j * STRETCH : i * BLOCK + (j + 1) * STRETCH] = cum
            end = cum[:, STRETCH - 1 : STRETCH]
            marks = jnp.where(lane == j, end, jnp.where(lane == 2 + j, total, marks))
            total = total + end
            cums.append((cum, end))
        marks = jnp.where(lane == 4, total, marks)
        marks = spread_heads(jnp.exp(marks), fan)
        for j in range(2):
            cum, end = cums[j]
            here = slice(j * STRETCH, (j + 1) * STRETCH)
            weight = spread_heads(step[:, here] * jnp.exp(end - cum), fan)
            fresh = dot(b[here, :], (xc[here, :] * weight).astype(bf16), TN)
            ent_out[2 * i + j] = state
            pri_out[2 * i + j] = marks[2 + j : 3 + j, :]
            state = state * marks[j : j + 1, :] + fresh
    if last:
        decayed = marks[4:5, :]
        near = packed(state[:, 0:HALF], decayed[:, 0:HALF], columns[...])
        far = packed(state[:, HALF:], decayed[:, HALF:], columns[...])
        even = order[4] == 0
        keep_out[...] = jnp.where(even, near, far).astype(bf16)
        send_out[...] = jnp.where(even, far, near).astype(bf16)
    else:
        tail_out[...] = xbuf[BLOCK : BLOCK + HALO, :]
        state_out[...] = state
        total_out[...] = jnp.broadcast_to(total, (HEADS, STRETCH))


def stage_kernel(which, order, w, wbc, w_out, wbc_out, sems):
    copies = []
    for p in range(4):
        source = pl.ds(pl.multiple_of(order[p] * 512, 512), 512)
        target = pl.ds(p * 512, 512)
        copies.append(
            pltpu.make_async_copy(w.at[which, source, :], w_out.at[target, :], sems.at[0, p])
        )
        copies.append(
            pltpu.make_async_copy(wbc.at[which, source, :], wbc_out.at[target, :], sems.at[1, p])
        )
    for c in copies:
        c.start()
    for c in copies:
        c.wait()


def staged(which, order, w, wbc):
    return pl.pallas_call(
        functools.partial(stage_kernel, which),
        out_shape=[pltpu.VMEM((2048, 2 * LANES), bf16), pltpu.VMEM((2048, 2 * STATE), bf16)],
        in_specs=[smem(), in_hbm(), in_hbm()],
        out_specs=[vmem()] * 2,
        scratch_shapes=[pltpu.SemaphoreType.DMA((2, 4))],
        compiler_params=pltpu.CompilerParams(vmem_limit_bytes=2 * MIB),
        name="stage",
    )(order, kept_in_hbm(w), kept_in_hbm(wbc))


def stage_out_kernel(which, order, w, out, sems):
    copies = []
    for p in range(4):
        source = pl.ds(pl.multiple_of(order[(0, 2, 1, 3)[p]] * 512, 512), 512)
        copies.append(pltpu.make_async_copy(w.at[which, :, source], out.at[p], sems.at[p]))
    for c in copies:
        c.start()
    for c in copies:
        c.wait()


def staged_out(which, order, w):
    return pl.pallas_call(
        functools.partial(stage_out_kernel, which),
        out_shape=pltpu.VMEM((4, LANES, LANES), bf16),
        in_specs=[smem(), in_hbm()],
        out_specs=vmem(),
        scratch_shapes=[pltpu.SemaphoreType.DMA((4,))],
        compiler_params=pltpu.CompilerParams(vmem_limit_bytes=2 * MIB),
        name="stage_out",
    )(order, kept_in_hbm(w))


def vmem():
    return pl.BlockSpec(memory_space=pltpu.VMEM)


def smem():
    return pl.BlockSpec(memory_space=pltpu.SMEM)


def in_hbm():
    return pl.BlockSpec(memory_space=pltpu.HBM)


def kept_in_hbm(x):
    return pltpu.with_memory_space_constraint(x, pltpu.HBM)


def entry(order, pieces, offset, columns, carry, gain, w, wbc, wdt, taps, dt_bias, a_log, last):
    first = carry is None
    rows = BLOCK
    shape = jax.ShapeDtypeStruct
    outs = [
        pltpu.VMEM((rows, LANES), bf16),
        pltpu.VMEM((rows, LANES), bf16),
        pltpu.VMEM((rows, STATE), bf16),
        pltpu.VMEM((rows, STATE), bf16),
        pltpu.VMEM((HEADS, rows), f32),
        pltpu.VMEM((HEADS, rows), f32),
        pltpu.VMEM((rows // STRETCH, STATE, LANES), f32),
        pltpu.VMEM((rows // STRETCH, 1, LANES), f32),
    ]
    if last:
        outs += [shape((MSG, HALF), bf16)] * 2
    else:
        outs += [
            pltpu.VMEM((HALO, LANES + 2 * STATE), f32),
            pltpu.VMEM((STATE, LANES), f32),
            pltpu.VMEM((HEADS, STRETCH), f32),
        ]
    extra = [] if first else list(carry)
    operands = [order, *pieces, *([columns] if last else []), *extra, gain, w, wbc, wdt, taps, dt_bias, a_log]
    specs = [smem()] + [vmem()] * (len(operands) - 1)
    return pl.pallas_call(
        functools.partial(entry_kernel, first, last, offset, rows),
        out_shape=outs,
        in_specs=specs,
        out_specs=[vmem()] * len(outs),
        scratch_shapes=[
            pltpu.VMEM((HALO + BLOCK, 2048), bf16),
            pltpu.VMEM((HALO + BLOCK, LANES + 2 * STATE), f32),
        ],
        compiler_params=pltpu.CompilerParams(vmem_limit_bytes=8 * MIB),
        name="entry",
    )(*operands)


def inside_kernel(rows, xc, b, c, cum, step, skip, y_out):
    q_pos = lax.broadcasted_iota(jnp.int32, (STRETCH, STRETCH), 0)
    k_pos = lax.broadcasted_iota(jnp.int32, (STRETCH, STRETCH), 1)
    causal = k_pos <= q_pos
    low_half = k_pos < HEAD_DIM
    skips = spread_heads(skip[...], head_fan())[0:1, :]
    for j in range(rows // STRETCH):
        here = slice(j * STRETCH, (j + 1) * STRETCH)
        match = jnp.where(causal, dot(c[here, :], b[here, :], NT), 0.0)
        cum_rows = cum[:, here]
        step_rows = step[:, here]
        cum_cols = jnp.transpose(cum_rows)
        for pair in range(HEADS // 2):
            weights = []
            for h in (2 * pair, 2 * pair + 1):
                gap = jnp.minimum(cum_cols[:, h : h + 1] - cum_rows[h : h + 1, :], 0.0)
                weights.append((match * (jnp.exp(gap) * step_rows[h : h + 1, :])).astype(bf16))
            lanes = slice(pair * STRETCH, (pair + 1) * STRETCH)
            x = xc[here, lanes].astype(f32)
            stacked = jnp.concatenate(
                [jnp.where(low_half, x, 0.0), jnp.where(low_half, 0.0, x)], axis=0
            ).astype(bf16)
            y_out[here, lanes] = (
                dot(jnp.concatenate(weights, axis=1), stacked) + skips[:, lanes] * x
            )


def inside(xc, b, c, cum, step, skip):
    rows = xc.shape[0]
    return pl.pallas_call(
        functools.partial(inside_kernel, rows),
        out_shape=pltpu.VMEM((rows, LANES), f32),
        in_specs=[vmem()] * 6,
        out_specs=vmem(),
        compiler_params=pltpu.CompilerParams(vmem_limit_bytes=4 * MIB),
        name="inside",
    )(xc, b, c, cum, step, skip)


def exit_kernel(chunks, order, mine, other, gain, wv, *refs):
    parts = [refs[6 * i : 6 * i + 6] for i in range(chunks)]
    own, up, down, plus_a, minus_b = refs[6 * chunks :]
    split = chunks * BLOCK // 2
    outs = (((plus_a, 0), (up, split)), ((down, split), (minus_b, 0)), ((up, 0), (down, 0)))
    fan = head_fan()
    row = lax.broadcasted_iota(jnp.int32, (BLOCK, BLOCK), 0) // HEAD_DIM
    lane = lax.broadcasted_iota(jnp.int32, (BLOCK, BLOCK), 1) // HEAD_DIM
    same_head = (row == lane).astype(bf16)
    here, there = mine[...].astype(f32), other[...].astype(f32)
    even = order[4] == 0
    came = jnp.concatenate([jnp.where(even, here, there), jnp.where(even, there, here)], axis=1)
    for i in range(chunks):
        y, z, c, cum, ent, pri = parts[i]
        mixed = []
        for j in range(2):
            here = slice(j * STRETCH, (j + 1) * STRETCH)
            entering = (ent[j] + pri[j] * came).astype(bf16)
            carried = dot(c[here, :], entering) * spread_heads(jnp.exp(cum[:, here]), fan)
            gated = (y[here, :] + carried) * silu(z[here, :].astype(f32))
            square = (gated * gated).astype(bf16)
            sums = jnp.concatenate(
                [dot(square[:, 0:BLOCK], same_head), dot(square[:, BLOCK:], same_head)], axis=1
            )
            scale = lax.rsqrt(sums * (1.0 / HEAD_DIM) + epsilon)
            mixed.append((gated * scale * gain[...]).astype(bf16))
        mixed = jnp.concatenate(mixed, axis=0)
        own[i * BLOCK : (i + 1) * BLOCK, :] = dot(mixed, wv[0]).astype(bf16)
        for p in range(3):
            product = dot(mixed, wv[p + 1]).astype(bf16)
            for j in range(2):
                at = i * BLOCK + j * STRETCH
                out, base = outs[p][at // split]
                at = base + at % split
                out[at : at + STRETCH, :] = product[j * STRETCH : (j + 1) * STRETCH, :]


def leave(order, mine, other, gain, w, parts):
    rows = len(parts) * BLOCK
    shape = jax.ShapeDtypeStruct
    outs = [shape((rows, LANES), bf16)] * 3 + [shape((rows // 2, LANES), bf16)] * 2
    operands = [order, mine, other, gain, w, *(a for part in parts for a in part)]
    return pl.pallas_call(
        functools.partial(exit_kernel, len(parts)),
        out_shape=outs,
        in_specs=[smem()] + [vmem()] * (len(operands) - 1),
        out_specs=[vmem()] * len(outs),
        compiler_params=pltpu.CompilerParams(vmem_limit_bytes=6 * MIB),
        name="leave",
    )(*operands)


def small_call(kernel, name, outs, place, *operands):
    return pl.pallas_call(
        kernel,
        out_shape=outs,
        in_specs=[smem()] + [vmem()] * len(operands),
        out_specs=[vmem()] * len(outs),
        compiler_params=pltpu.CompilerParams(vmem_limit_bytes=2 * MIB),
        name=name,
    )(place, *operands)


def chip_kernel(place, keep, got, out):
    even = place[4] == 0
    mine, other = opened(keep), opened(got)
    both = after(chosen(even, mine, other), chosen(even, other, mine))
    out[...] = packed(*both, columns_in(keep) + columns_in(got)).astype(bf16)


def row_kernel(place, chip, one, two, three, row_out, before_out):
    y = place[5]
    ring = [opened(r) for r in (chip, one, two, three)]
    row, before = nothing(), nothing()
    for at in range(4):
        here = ring[0]
        for k in range(1, 4):
            here = chosen((y + 4 - at) % 4 == k, ring[k], here)
        before = chosen(at < y, after(before, here), before)
        row = after(row, here)
    columns = sum(columns_in(r) for r in (chip, one, two, three))
    row_out[...] = packed(*row, columns).astype(bf16)
    before_out[...] = packed(*before, columns)


def arrive_kernel(place, one, two, three, before, keep, got, mine_out, other_out, columns_out):
    even = place[4] == 0
    z = place[6]
    came = nothing()
    for k, r in ((3, three), (2, two), (1, one)):
        came = chosen(z >= k, after(came, opened(r)), came)
    first = after(came, opened(before))
    second = after(first, chosen(even, opened(keep), opened(got)))
    mine_out[...] = jnp.where(even, first[0], second[0]).astype(bf16)
    other_out[...] = jnp.where(even, second[0], first[0]).astype(bf16)
    columns_out[...] = sum(columns_in(r) for r in (before, one, two, three))


def give_kernel(columns, x, out):
    cell = lax.broadcasted_iota(jnp.int32, (512, HALF), 0)
    for part in range(2):
        wanted = 2.0 * columns[2 * part : 2 * part + 1, :] + columns[2 * part + 1 : 2 * part + 2, :]
        pick = (cell == wanted.astype(jnp.int32)).astype(bf16)
        for r in range(2):
            rows = dot(pick, x[r * 512 : (r + 1) * 512, :], TN).astype(bf16)
            out[part * 16 : (part + 1) * 16, r * 16 : (r + 1) * 16, :] = rows.reshape(16, 16, 512)


def given(columns, x):
    return pl.pallas_call(
        give_kernel,
        out_shape=jax.ShapeDtypeStruct((32, 32, 512), bf16),
        in_specs=[vmem()] * 2,
        out_specs=vmem(),
        compiler_params=pltpu.CompilerParams(vmem_limit_bytes=6 * MIB),
        name="give",
    )(columns, x)


def turned(by):
    return [(i, (i + by) % TP) for i in range(TP)]


def around(x, by):
    return lax.ppermute(x, "tp", turned(by))


def swapped(x):
    return lax.ppermute(x, "seq_2", [(0, 1), (1, 0)])


def arriving_state(place, keep, send, weights, beside, wrapped):
    shape = jax.ShapeDtypeStruct
    got = swapped(send)
    msg = shape((MSG, HALF), bf16)
    (chip,) = small_call(chip_kernel, "chip", [msg], place, keep, got)
    ring = [lax.ppermute(chip, "seq_1", turned(k)) for k in (1, 2, 3)]
    row, before = small_call(
        row_kernel,
        "row",
        [msg, shape((MSG, HALF), f32)],
        behind(place, weights, beside[2]),
        chip,
        *ring,
    )
    earlier = [
        lax.ppermute(row, "seq_0", turned(k)[: 4 if wrapped else 4 - k]) for k in (1, 2, 3)
    ]
    mine, other, columns = small_call(
        arrive_kernel,
        "arrive",
        [shape((STATE, HALF), bf16)] * 2 + [shape((8, HALF), f32)],
        behind(place, *beside),
        *earlier,
        before,
        keep,
        got,
    )
    return mine, swapped(other), columns


def behind(x, *done):
    return lax.optimization_barrier((x, *done))[0]


def with_halo(shard, count):
    pairs = [(i, i + 1) for i in range(lax.axis_size(SEQ) - 1)]
    return jnp.concatenate([lax.ppermute(shard[-HALO:], SEQ, pairs), shard[:count]], axis=0)


def layer(which, shard, first, place, params, large, columns, early=()):
    gain, wdt, taps, dt_bias, a_log, skip, out_gain = params
    w, wbc, w_out = large
    rows = [shard[i * BLOCK : (i + 1) * BLOCK] for i in range(shard.shape[0] // BLOCK)]
    wv, wbcv = staged(which, behind(place, first), w, wbc)
    carry, kept, gate = None, [], place

    def enter(i, pieces, offset=0):
        nonlocal carry, gate
        out = entry(
            gate, pieces, offset, columns, carry, gain, wv, wbcv, wdt, taps, dt_bias, a_log, i == 3
        )
        z, xc, b, c, cum, step, ent, pri = out[:8]
        carry = out[8:]
        y = inside(xc, b, c, cum, step, skip)
        kept.append((y, z, c, cum, ent, pri))
        if i < 2:
            gate = behind(place, y)

    if which == 0:
        own = [first, behind(rows[2], first), behind(rows[3], first)]
        left, right = [around(first, 1)], [around(first, -1)]
        right.append(around(own[1], -1))
        opposite = [around(behind(left[0], *early), 1)]
        right.append(around(own[2], -1))
        left.append(around(behind(rows[2], right[1]), 1))
        opposite.append(around(right[1], -1))
        pieces = (own[0], left[0], right[0], opposite[0])
        enter(0, pieces, HALO)
        left.append(around(behind(rows[3], carry[0]), 1))
        opposite.append(around(behind(right[2], carry[0]), -1))
        enter(1, pieces, HALO + BLOCK)
        for i in (1, 2):
            enter(i + 1, (own[i], left[i], right[i], opposite[i]))
    else:
        own = [first, behind(rows[1], first), behind(rows[2], first)]
        left, right = [around(x, 1) for x in own], [around(x, -1) for x in own]
        opposite = [around(behind(left[0], wbcv), 1)]
        enter(0, (own[0], left[0], right[0], opposite[0]), HALO)
        own.append(behind(rows[3], first, carry[0]))
        left.append(around(own[3], 1))
        right.append(around(own[3], -1))
        opposite.append(around(right[1], -1))
        enter(1, (own[1], left[1], right[1], opposite[1]))
        opposite.append(around(left[2], 1))
        opposite.append(around(behind(right[3], carry[0]), -1))
        for i in (2, 3):
            enter(i, (own[i], left[i], right[i], opposite[i]))
    wov = staged_out(which, behind(place, carry[0]), w_out)
    mine, other, columns = arriving_state(
        place, *carry, wov, [k[0] for k in kept], which == 0
    )
    results = []
    for low in (0, 2):
        own_part, up, down, plus_a, minus_b = leave(
            place, mine, other, out_gain, wov, kept[low : low + 2]
        )
        up, down = around(up, 1), around(down, -1)
        plus_a = around((plus_a.astype(f32) + up[:BLOCK].astype(f32)).astype(bf16), 1)
        minus_b = around((minus_b.astype(f32) + down[:BLOCK].astype(f32)).astype(bf16), -1)
        here = shard[low * BLOCK : (low + 2) * BLOCK].astype(f32) + own_part.astype(f32)
        results.append(here[:BLOCK] + plus_a.astype(f32) + down[BLOCK:].astype(f32))
        results.append(here[BLOCK:] + up[BLOCK:].astype(f32) + minus_b.astype(f32))
    return jnp.concatenate(results, axis=0).astype(bf16), columns


def permuted(x, source):
    pick = (source[:, None] == jnp.arange(x.shape[0])[None, :]).astype(bf16)
    return jnp.dot(pick, x, preferred_element_type=f32).astype(bf16)


def body(
    tokens,
    col_order,
    in_gain,
    w_in,
    w_bc,
    w_dt,
    conv_x,
    conv_bc,
    dt_bias,
    a_log,
    d_skip,
    out_gain,
    w_out,
):
    first = with_halo(tokens, 2 * BLOCK)
    arguments = (in_gain, w_in, w_dt, conv_x, conv_bc, dt_bias, a_log, d_skip, out_gain, col_order)
    in_gain, w_in, w_dt, conv_x, conv_bc, dt_bias, a_log, d_skip, out_gain, col_order = behind(
        arguments, first
    )
    x = lax.axis_index("tp")
    core, y, z = (lax.axis_index(a) for a in ("seq_2", "seq_1", "seq_0"))
    place = jnp.stack([x, (x + 3) & 3, (x + 1) & 3, (x + 2) & 3, core, y, z]).astype(jnp.int32)
    w = w_in.reshape(2, 2048, 2 * LANES)

    def on_lanes(heads):
        return jnp.broadcast_to(heads[:, None], (HEADS, STRETCH))

    def params(which):
        return (
            in_gain[which].reshape(TP, 1, 512),
            w_dt[which].T.reshape(HEADS, TP, 512).transpose(1, 0, 2),
            jnp.concatenate([conv_x[which], conv_bc[which]], axis=1),
            on_lanes(dt_bias[which]),
            on_lanes(a_log[which]),
            on_lanes(d_skip[which]),
            out_gain[which].reshape(1, LANES),
        )

    starts = col_order.reshape(16, 64)[:, 0]
    slot = jnp.arange(512)
    columns = jnp.where(
        slot // 16 == lax.axis_index(SEQ), jnp.tile(starts % 512, 32), 0
    ).reshape(2, 256)
    columns = jnp.stack([columns[0] // 2, columns[0] % 2, columns[1] // 2, columns[1] % 2])
    columns = jnp.pad(columns.astype(f32), ((0, 4), (0, 0)))
    visit = jnp.arange(16)[:, None]
    along = jnp.arange(64)[None, :]
    row = jnp.where((starts >= 512)[:, None], 63 - along, along)
    take = ((row // 2) * 32 + (row % 2) * 16 + visit).reshape(1024)
    place, small, w, columns, take = lax.optimization_barrier(
        (place, [params(0), params(1)], w, columns, take)
    )
    large = (w, w_bc, w_out)

    row_result, columns = layer(0, tokens, first, place, small[0], large, columns, (w,))
    payload = given(columns, row_result)
    arrived = lax.all_to_all(payload, SEQ, 0, 0, tiled=True).reshape(1024, 512)
    own_rows = permuted(arrived, take)
    return layer(1, own_rows, with_halo(own_rows, BLOCK), place, small[1], large, columns)[0]


def solution(mesh):
    torus = Mesh(mesh.devices.reshape(4, 4, 2, mesh.shape["tp"]), ("seq_0", "seq_1", "seq_2", "tp"))
    return jax.shard_map(
        body,
        mesh=torus,
        in_specs=(
            P(SEQ, "tp"),
            P(SEQ),
            P(),
            P(None, None, None, "tp"),
            P(),
            P(None, None, "tp"),
            P(None, None, "tp"),
            P(),
            P(None, "tp"),
            P(None, "tp"),
            P(None, "tp"),
            P(None, "tp"),
            P(None, "tp", None),
        ),
        out_specs=P(SEQ, "tp"),
        check_vma=False,
    )
```
